256 devices in a mesh: row: 16 (over x, y_hi, core), col: 16 (over z, y_lo).
Axes of the slice: x: 4, y: 4 (y_hi: 2, y_lo: 2; y = y_hi * 2 + y_lo), z: 8, core: 2. Of those that a mesh axis runs over, the one named last changes fastest.
Arguments:
- object_field: float32 [2, 6144, 6144], P(None, 'row', 'col'), may hold values from -6 to 6
- probe: float32 [2, 128, 128], replicated, may hold values from -6 to 6
- amplitudes: float32 [16, 16, 12, 128, 128], P('row', 'col'), may hold values from 0.2 to 4
- offsets: int32 [16, 16, 12, 2], P('row', 'col'), may hold values from -64 to 319
- counts: int32 [16, 16], P('row', 'col'), may hold values from 1 to 12, as said below
Outputs:
- updated_object: float32 [2, 6144, 6144], P(None, 'row', 'col')
The draws below stay inside these ranges and needn't reach their ends.
Inputs may be any that keep to these rules, and one draw needn't show every extreme that they name: `counts`: some tile has exactly 12 live positions in every draw.
All inputs are finite; a program needn't handle non-finite values.
Results may differ from the reference program's by a relative error of at most 0.0001.
Values sent between devices are 32-bit elements; how exact they have to be, the bound alone decides.
A program may use at most 64 MiB of HBM per device.

```python
import math
import jax
import jax.numpy as jnp
from jax import lax

PROBE = 128
TILE = 384
MAXPOS = 12
ITERS = 2
BLOCK_ROWS = 16
BLOCK_COLS = 16
NY = 6144
NX = 6144


def draw_counts(key, part):
    first, second, third = jax.random.split(jax.random.fold_in(key, 11), 3)
    shape = (BLOCK_ROWS, BLOCK_COLS)
    small = jax.random.randint(first, shape, 1, MAXPOS // 4 + 1)
    full = jax.random.randint(second, shape, 0, 4) == 0
    values = jnp.where(full, MAXPOS, small).reshape(-1)
    chosen = jax.random.randint(third, (), 0, BLOCK_ROWS * BLOCK_COLS)
    values = values.at[chosen].set(MAXPOS)
    return values.reshape(shape).astype(jnp.int32)


def with_ends(array, key, smallest, top_value):
    spot = [jax.random.randint(jax.random.fold_in(key, axis), (), 0, length) for axis, length in enumerate(array.shape)]
    longest = array.shape.index(max(array.shape))
    next_to = spot[:longest] + [(spot[longest] + 1) % array.shape[longest]] + spot[longest + 1:]
    return array.at[tuple(spot)].set(smallest).at[tuple(next_to)].set(top_value)


def level_of(own_key, extent, cuts, low, largest):
    def one(position, blocks):
        steps = jax.random.uniform(jax.random.fold_in(jax.random.fold_in(own_key, 6), position), (blocks,), jnp.float32, low / len(cuts), largest / len(cuts))
        return jnp.repeat(jnp.exp(steps), extent[position] // blocks).reshape((-1,) + (1,) * (len(extent) - position - 1))

    gain = one(*cuts[0])
    for cut in cuts[1:]:
        gain = gain * one(*cut)
    return gain


def centred(stream_key, extent, spread, limit, shards=(), kind=jnp.bfloat16):
    result = jax.random.normal(stream_key, extent, jnp.float32) * spread
    if len(shards) > 0:
        result = level_of(stream_key, extent, shards, -0.22, 0.18) * result
    return jnp.clip(result, min=-limit, max=limit).astype(kind)


def setup_inputs(seed: int = 0) -> dict:
    key_list = jax.random.split(jax.random.key(seed), 6)
    object_field = centred(key_list[0], (2, NY, NX), 1.0, 6.0, ((1, 16), (2, 16)), jnp.float32)
    probe = centred(key_list[1], (2, PROBE, PROBE), 1.0, 6.0, (), jnp.float32)
    amplitudes = jnp.clip(jnp.exp(math.log(4.0) - 2.9957323 * jax.random.uniform(key_list[2], (BLOCK_ROWS, BLOCK_COLS, MAXPOS, PROBE, PROBE), jnp.float32) ** level_of(key_list[2], (BLOCK_ROWS, BLOCK_COLS, MAXPOS, PROBE, PROBE), ((0, 16), (1, 16)), -0.2, 0.2)), 0.2, 4.0)
    offsets = with_ends(jax.random.randint(key_list[3], (BLOCK_ROWS, BLOCK_COLS, MAXPOS, 2), -(PROBE // 2), TILE - PROBE // 2), jax.random.fold_in(key_list[3], 1), -(PROBE // 2), (TILE - PROBE // 2) - 1).astype(jnp.int32)
    counts = draw_counts(jax.random.fold_in(key_list[5], 71), 0)
    return {"object_field": object_field, "probe": probe, "amplitudes": amplitudes, "offsets": offsets, "counts": counts}


def reference(object_field, probe, amplitudes, offsets, counts):
    half = PROBE // 2
    blocks = BLOCK_ROWS * BLOCK_COLS
    row_base = (jnp.arange(BLOCK_ROWS, dtype=jnp.int32) * TILE)[:, None, None]
    col_base = (jnp.arange(BLOCK_COLS, dtype=jnp.int32) * TILE)[None, :, None]
    start_rows = (row_base + offsets[..., 0] + half).reshape(blocks, MAXPOS).astype(jnp.int32)
    start_cols = (col_base + offsets[..., 1] + half).reshape(blocks, MAXPOS).astype(jnp.int32)
    live = (jnp.arange(MAXPOS, dtype=jnp.int32)[None, None, :] < counts[..., None]).astype(jnp.float32)
    live = live.reshape(blocks, MAXPOS)
    measured = amplitudes.reshape(blocks, MAXPOS, PROBE, PROBE)
    probe_c = lax.complex(probe[0], probe[1])
    power = probe[0] * probe[0] + probe[1] * probe[1]
    zero_i = jnp.int32(0)

    def add_light(index, total):
        block = index // MAXPOS
        slot = index % MAXPOS
        srow = start_rows[block, slot]
        scol = start_cols[block, slot]
        old = lax.dynamic_slice(total, (srow, scol), (PROBE, PROBE))
        return lax.dynamic_update_slice(total, old + power * live[block, slot], (srow, scol))
    light = lax.fori_loop(0, blocks * MAXPOS, add_light, jnp.zeros((NY + PROBE, NX + PROBE), jnp.float32))
    light = light[half:half + NY, half:half + NX]
    field = object_field
    for step in range(ITERS):
        padded = jnp.pad(field, ((0, 0), (half, half), (half, half)))

        def per_block(block, total):

            def window(srow, scol):
                return lax.dynamic_slice(padded, (zero_i, srow, scol), (2, PROBE, PROBE))
            wins = jax.vmap(window)(start_rows[block], start_cols[block])
            exit_wave = probe_c[None] * lax.complex(wins[:, 0], wins[:, 1])
            far = jnp.fft.fft2(exit_wave, norm='ortho')
            mag2 = jnp.real(far) ** 2 + jnp.imag(far) ** 2
            ratio = measured[block] / jnp.sqrt(mag2 + 0.25) - 1.0
            back = jnp.fft.ifft2(far * ratio, norm='ortho')
            grad = jnp.conj(probe_c)[None] * back * live[block][:, None, None]
            grads = jnp.stack([jnp.real(grad), jnp.imag(grad)], axis=1)

            def place(slot, acc):
                srow = start_rows[block, slot]
                scol = start_cols[block, slot]
                old = lax.dynamic_slice(acc, (zero_i, srow, scol), (2, PROBE, PROBE))
                return lax.dynamic_update_slice(acc, old + grads[slot], (zero_i, srow, scol))
            return lax.fori_loop(0, MAXPOS, place, total)
        update = lax.fori_loop(0, blocks, per_block, jnp.zeros((2, NY + PROBE, NX + PROBE), jnp.float32))
        update = update[:, half:half + NY, half:half + NX]
        field = field + update / (light[None] + 1.0)
    return field
```

```python
import math

import jax
import jax.numpy as jnp
import numpy as np
from jax import lax
from jax.experimental import pallas as pl
from jax.experimental.pallas import tpu as pltpu
from jax.sharding import PartitionSpec as P

ITERS = 2
NEIGHBOURS = ((-1, 0), (1, 0), (0, -1), (0, 1), (-1, -1), (-1, 1), (1, -1), (1, 1))
OPPOSITE = (1, 0, 3, 2, 7, 6, 5, 4)
MESH = pl.DeviceIdType.MESH
VMEM = pl.BlockSpec(memory_space=pltpu.VMEM)
SMEM = pl.BlockSpec(memory_space=pltpu.SMEM)
LIMIT = 24 << 20


def dft_tables(length):
    index = np.arange(length)
    angle = (np.outer(index, index) % length) * (2.0 * math.pi / length)
    cosine, sine = np.cos(angle) / math.sqrt(length), np.sin(angle) / math.sqrt(length)
    table = np.block([[cosine, -sine], [sine, cosine]])
    high = table.astype(jnp.bfloat16)
    low = (table - high.astype(np.float64)).astype(jnp.bfloat16)
    return np.stack([high, low, high.T, low.T])


def there(d, grid):
    row, col = lax.axis_index("row"), lax.axis_index("col")
    ok = None
    if d[0]:
        ok = row > 0 if d[0] < 0 else row < grid[0] - 1
    if d[1]:
        side = col > 0 if d[1] < 0 else col < grid[1] - 1
        ok = side if ok is None else jnp.logical_and(ok, side)
    return ok


def target(d):
    return {"row": lax.axis_index("row") + d[0], "col": lax.axis_index("col") + d[1]}


def enter(grid):
    barrier = pltpu.get_barrier_semaphore()
    for d in NEIGHBOURS:

        @pl.when(there(d, grid))
        def _():
            pl.semaphore_signal(barrier, inc=1, device_id=target(d), device_id_type=MESH)

    up_down, left_right = 1, 1
    for d in NEIGHBOURS[:2]:
        up_down += jnp.where(there(d, grid), 1, 0)
    for d in NEIGHBOURS[2:4]:
        left_right += jnp.where(there(d, grid), 1, 0)
    pl.semaphore_wait(barrier, up_down * left_right - 1)


def start_all(copies, grid):
    for d, copy in zip(NEIGHBOURS, copies):

        @pl.when(there(d, grid))
        def _():
            copy.start()


def wait_all(copies, grid):
    for i, copy in enumerate(copies):

        @pl.when(there(NEIGHBOURS[i], grid))
        def _():
            copy.wait_send()

        @pl.when(there(NEIGHBOURS[OPPOSITE[i]], grid))
        def _():
            copy.wait_recv()


def swap(x):
    return pltpu.roll(x, 64, x.ndim - 1)


def lower(rows):
    return lax.broadcasted_iota(jnp.int32, (rows, 128), 1) < 64


def pack(x, keep_low):
    rows = x.shape[0] // 2
    keep = lower(rows) if keep_low else ~lower(rows)
    return jnp.where(keep, x[:rows], swap(x[rows:]))


def unpack(x):
    return jnp.concatenate([x, swap(x)], axis=0)


def remote(src, dst, sems, i):
    return pltpu.make_async_remote_copy(
        src, dst, sems.at[0, i], sems.at[1, i], device_id=target(NEIGHBOURS[i]), device_id_type=MESH
    )


def halo_copies(tile, ext, side, corner, side_in, corner_in, sems):
    half, edge = 64, tile.shape[1]
    first = edge - 384
    ends = [
        remote(
            tile.at[:, first // 2 : first // 2 + half, 0:384],
            ext.at[:, 448:512, 0:384],
            sems,
            0,
        ),
        remote(
            tile.at[:, first // 2 + 320 : first // 2 + 384, 0:384],
            ext.at[:, 0:half, 0:384],
            sems,
            1,
        ),
    ]
    ends += [remote(side.at[k], side_in.at[k], sems, 2 + k) for k in range(2)]
    ends += [remote(corner.at[k], corner_in.at[k], sems, 4 + k) for k in range(4)]
    return ends


def halo_pack(tile, base, side, corner):
    for p in range(2):
        for k, lane in enumerate((0, 256)):
            side[k, p] = pack(tile[p, base : base + 384, lane : lane + 128], k == 0)
        for k, (row, lane) in enumerate(((0, 0), (0, 256), (320, 0), (320, 256))):
            corner[k, p] = pack(tile[p, base + row : base + row + 64, lane : lane + 128], lane == 0)


def halo_unpack(ext, side_in, corner_in):
    for p in range(2):
        ext[p, 64:448, 384:512] = jnp.concatenate(
            [
                jnp.where(lower(192), side_in[0, p], side_in[1, p]),
                jnp.where(lower(192), swap(side_in[0, p]), swap(side_in[1, p])),
            ],
            axis=0,
        )
        for row, k in ((448, 0), (0, 2)):
            a, b = corner_in[k, p], corner_in[k + 1, p]
            ext[p, row : row + 64, 384:512] = jnp.concatenate(
                [jnp.where(lower(32), a, b), jnp.where(lower(32), swap(a), swap(b))], axis=0
            )


def halo_clear(ext, side_in, corner_in, grid):
    for i, d in enumerate(NEIGHBOURS):

        @pl.when(jnp.logical_not(there(d, grid)))
        def _():
            if i == 0:
                ext[:, 0:64, 0:384] = jnp.zeros((2, 64, 384), jnp.float32)
            elif i == 1:
                ext[:, 448:512, 0:384] = jnp.zeros((2, 64, 384), jnp.float32)
            elif i < 4:
                side_in[OPPOSITE[i] - 2] = jnp.zeros((2, 192, 128), jnp.float32)
            else:
                corner_in[OPPOSITE[i] - 4] = jnp.zeros((2, 32, 128), jnp.float32)


def fold_pack(update, side, corner):
    for p in range(2):
        for k in range(2):
            side[k, p] = pack(update[p, 64:448, 384:512], k == 1)
        for k, row in enumerate((0, 0, 448, 448)):
            corner[k, p] = pack(update[p, row : row + 64, 384:512], k % 2 == 1)


def fold_copies(update, ends_in, side, corner, side_in, corner_in, sems):
    ends = [
        remote(update.at[:, 0:64, 0:384], ends_in.at[0], sems, 0),
        remote(update.at[:, 448:512, 0:384], ends_in.at[1], sems, 1),
    ]
    ends += [remote(side.at[k], side_in.at[k], sems, 2 + k) for k in range(2)]
    ends += [remote(corner.at[k], corner_in.at[k], sems, 4 + k) for k in range(4)]
    return ends


def fold_add(dest, base, inverse, ends_in, side_in, corner_in, grid):
    def add(p, row, lane, value):
        rows, lanes = pl.ds(base + row, value.shape[0]), pl.ds(lane, value.shape[1])
        dest[p, rows, lanes] += value * inverse[pl.ds(row, value.shape[0]), lanes]

    for i, d in enumerate(NEIGHBOURS):

        @pl.when(there(NEIGHBOURS[OPPOSITE[i]], grid))
        def _():
            for p in range(2):
                if i < 2:
                    add(p, 320 if i == 0 else 0, 0, ends_in[i, p])
                elif i < 4:
                    x = unpack(side_in[i - 2, p])
                    keep = lower(384) if i == 3 else ~lower(384)
                    add(p, 0, 0 if i == 3 else 256, jnp.where(keep, x, 0.0))
                else:
                    x = unpack(corner_in[i - 4, p])
                    keep = lower(64) if d[1] == 1 else ~lower(64)
                    row, lane = (320 if d[0] == -1 else 0), (0 if d[1] == 1 else 256)
                    add(p, row, lane, jnp.where(keep, x, 0.0))


def spread_kernel(grid):
    def kernel(field, offsets, counts, ext, around, mine, side, corner, side_in, corner_in, sems, small):
        mine[...] = jnp.zeros_like(mine)
        mine[0:12, 0:2] = offsets[...]
        mine[12:13, 0:1] = counts[...]
        for i, d in enumerate(NEIGHBOURS):

            @pl.when(jnp.logical_not(there(d, grid)))
            def _():
                around[OPPOSITE[i]] = jnp.zeros((16, 128), jnp.int32)

        halo_clear(ext, side_in, corner_in, grid)
        halo_pack(field, 0, side, corner)
        enter(grid)
        copies = halo_copies(field, ext, side, corner, side_in, corner_in, sems)
        notes = [remote(mine, around.at[i], small, i) for i in range(8)]
        start_all(notes, grid)
        start_all(copies, grid)
        ext[:, 64:448, 0:384] = field[...]
        wait_all(copies, grid)
        wait_all(notes, grid)
        halo_unpack(ext, side_in, corner_in)

    return kernel


def split(x):
    high = x.astype(jnp.bfloat16)
    return high, (x - high.astype(jnp.float32)).astype(jnp.bfloat16)


def dot(a, b):
    return jnp.dot(a, b, preferred_element_type=jnp.float32)


def right_mul(x, high, low):
    xh, xl = split(x)
    return dot(xh, high) + dot(xl, high) + dot(xh, low)


def left_mul(high, low, x):
    xh, xl = split(x)
    return dot(high, xh) + dot(high, xl) + dot(low, xh)


def cross(x):
    return jnp.concatenate(
        [
            jnp.concatenate([x[:128, :128], x[128:, :128]], axis=1),
            jnp.concatenate([x[:128, 128:], x[128:, 128:]], axis=1),
        ],
        axis=0,
    )


def gradient_kernel(with_light):
    def kernel(*refs):
        if with_light:
            offsets, counts, around, ext, probe, measured, tables, update, inverse, tall, light, power = refs
        else:
            offsets, counts, ext, probe, measured, tables, update, tall = refs
        count = counts[0, 0]
        update[...] = jnp.zeros_like(update)
        for p in range(2):
            tall[p, 0:8] = probe[p, 120:128]
            tall[p, 8:136] = probe[p]
        if with_light:
            light[...] = jnp.zeros_like(light)
            power[...] = tall[0] * tall[0] + tall[1] * tall[1]
        lane = lax.broadcasted_iota(jnp.int32, (128, 128), 1)
        sub = lax.broadcasted_iota(jnp.int32, (8, 128), 0)

        def turned(source, shift_rows, shift_lanes):
            return pltpu.roll(source[pl.ds(8 - shift_rows, 128), :], shift_lanes, 1)

        def scatter(dest, first, lanes, shift_rows, shift_lanes, value):
            head = jnp.where(sub >= shift_rows, value[:8], 0.0)
            main = jnp.concatenate([head, value[8:]], axis=0)
            tail = jnp.where(sub < shift_rows, value[:8], 0.0)
            for which, at in enumerate(lanes):
                keep = lane >= shift_lanes if which == 0 else lane < shift_lanes
                dest[pl.ds(first, 128), at] += jnp.where(keep, main, 0.0)
                dest[pl.ds(first + 128, 8), at] += jnp.where(keep[:8], tail, 0.0)

        def tiles_of(col, base, wrap):
            tile = lax.shift_right_arithmetic(col, 7) + base
            first = lax.rem(tile + wrap, wrap)
            second = lax.rem(tile + wrap + 1, wrap)
            return [pl.ds(pl.multiple_of(t * 128, 128), 128) for t in (first, second)]

        def brighten(row, col):
            low_row, low_col = jnp.bitwise_and(row, 7), jnp.bitwise_and(col, 127)
            first = pl.multiple_of(row - low_row + 128, 8)
            scatter(light, first, tiles_of(col, 1, 5), low_row, low_col, turned(power, low_row, low_col))

        def pair(step, carry):
            places, waves, beams = [], [], []
            for which in range(2):
                slot = step * 2 + which
                row, col = offsets[slot, 0], offsets[slot, 1]
                low_row, low_col = jnp.bitwise_and(row, 7), jnp.bitwise_and(col, 127)
                first = pl.multiple_of(row - low_row + 64, 8)
                lanes = tiles_of(col, 0, 4)
                beam = [turned(tall.at[p], low_row, low_col) for p in range(2)]
                window = []
                for p in range(2):
                    main = jnp.where(
                        lane >= low_col, ext[p, pl.ds(first, 128), lanes[0]], ext[p, pl.ds(first, 128), lanes[1]]
                    )
                    tail = jnp.where(
                        lane[:8] >= low_col,
                        ext[p, pl.ds(first + 128, 8), lanes[0]],
                        ext[p, pl.ds(first + 128, 8), lanes[1]],
                    )
                    window.append(
                        jnp.concatenate([jnp.where(sub >= low_row, main[:8], tail), main[8:]], axis=0)
                    )
                real = beam[0] * window[0] - beam[1] * window[1]
                imag = beam[0] * window[1] + beam[1] * window[0]
                waves.append(jnp.concatenate([real, imag], axis=1))
                beams.append(beam)
                places.append((first, lanes, low_row, low_col, (slot < count).astype(jnp.float32), row, col))
            half = cross(right_mul(jnp.concatenate(waves, axis=0), tables[0], tables[1]))
            far = left_mul(tables[2], tables[3], half)
            real, imag = far[:128], far[128:]
            known = jnp.concatenate([measured[step * 2], measured[step * 2 + 1]], axis=1)
            ratio = known * lax.rsqrt(real * real + imag * imag + 0.25) - 1.0
            change = jnp.concatenate([real * ratio, imag * ratio], axis=0)
            half = cross(left_mul(tables[0], tables[1], change))
            back = right_mul(half, tables[2], tables[3])
            for which in range(2):
                first, lanes, low_row, low_col, live, row, col = places[which]
                beam = [b * live for b in beams[which]]
                real, imag = back[which * 128 : which * 128 + 128, :128], back[which * 128 : which * 128 + 128, 128:]
                scatter(update.at[0], first, lanes, low_row, low_col, beam[0] * real + beam[1] * imag)
                scatter(update.at[1], first, lanes, low_row, low_col, beam[0] * imag - beam[1] * real)
            return carry

        lax.fori_loop(0, lax.shift_right_logical(count + 1, 1), pair, 0)
        if with_light:

            def own(slot, carry):
                brighten(offsets[slot, 0], offsets[slot, 1])
                return carry

            lax.fori_loop(0, count, own, 0)
            for i, d in enumerate(NEIGHBOURS):

                def other(slot, carry):
                    row = around[i, slot, 0] - d[0] * 384
                    col = around[i, slot, 1] - d[1] * 384
                    touches = (row > -128) & (row < 384) & (col > -128) & (col < 384)

                    @pl.when(touches)
                    def _():
                        brighten(row, col)

                    return carry

                lax.fori_loop(0, around[i, 12, 0], other, 0)
            inverse[...] = 1.0 / (light[128:512, 128:512] + 1.0)

    return kernel


def between_kernel(grid):
    def kernel(update, inverse, field, ext, side, corner, side_in, corner_in, ends_in, sems, out_side, out_corner, halo_side, halo_corner, more):
        halo_clear(ext, halo_side, halo_corner, grid)
        fold_pack(update, side, corner)
        enter(grid)
        copies = fold_copies(update, ends_in, side, corner, side_in, corner_in, sems)
        start_all(copies, grid)
        for p in range(2):
            ext[p, 64:448, 0:384] = field[p] + update[p, 64:448, 0:384] * inverse[...]
        wait_all(copies, grid)
        fold_add(ext, 64, inverse, ends_in, side_in, corner_in, grid)
        halo_pack(ext, 64, out_side, out_corner)
        copies = halo_copies(ext, ext, out_side, out_corner, halo_side, halo_corner, more)
        start_all(copies, grid)
        wait_all(copies, grid)
        halo_unpack(ext, halo_side, halo_corner)

    return kernel


def last_kernel(grid):
    def kernel(update, inverse, ext, out, side, corner, side_in, corner_in, ends_in, sems):
        fold_pack(update, side, corner)
        enter(grid)
        copies = fold_copies(update, ends_in, side, corner, side_in, corner_in, sems)
        start_all(copies, grid)
        for p in range(2):
            out[p] = ext[p, 64:448, 0:384] + update[p, 64:448, 0:384] * inverse[...]
        wait_all(copies, grid)
        fold_add(out, 0, inverse, ends_in, side_in, corner_in, grid)

    return kernel


def params(collective_id=None):
    if collective_id is None:
        return pltpu.CompilerParams(vmem_limit_bytes=LIMIT)
    return pltpu.CompilerParams(collective_id=collective_id, has_side_effects=True, vmem_limit_bytes=LIMIT)


def shards(grid, tables, object_field, probe, amplitudes, offsets, counts):
    f32 = jnp.float32
    offsets, measured = offsets[0, 0], amplitudes[0, 0]
    ext_shape = jax.ShapeDtypeStruct((2, 512, 512), f32)
    packs = [pltpu.VMEM((2, 2, 192, 128), f32), pltpu.VMEM((4, 2, 32, 128), f32)]
    ends = pltpu.VMEM((2, 2, 64, 384), f32)
    sems = pltpu.SemaphoreType.DMA((2, 8))
    ext, around = pl.pallas_call(
        spread_kernel(grid),
        name="spread",
        out_shape=(ext_shape, jax.ShapeDtypeStruct((8, 16, 128), jnp.int32)),
        in_specs=[VMEM] * 3,
        out_specs=(VMEM, VMEM),
        scratch_shapes=[pltpu.VMEM((16, 128), jnp.int32)] + packs + packs + [sems, sems],
        compiler_params=params(0),
    )(object_field, offsets, counts)
    tall = pltpu.VMEM((2, 136, 128), f32)
    update, inverse = pl.pallas_call(
        gradient_kernel(True),
        name="gradient_light",
        out_shape=(ext_shape, jax.ShapeDtypeStruct((384, 384), f32)),
        in_specs=[SMEM] * 3 + [VMEM] * 4,
        out_specs=(VMEM, VMEM),
        scratch_shapes=[tall, pltpu.VMEM((648, 640), f32), pltpu.VMEM((136, 128), f32)],
        compiler_params=params(),
    )(offsets, counts, around, ext, probe, measured, tables)
    ext = pl.pallas_call(
        between_kernel(grid),
        name="between",
        out_shape=ext_shape,
        in_specs=[VMEM] * 3,
        out_specs=VMEM,
        scratch_shapes=packs + packs + [ends, sems] + packs + packs + [sems],
        compiler_params=params(1),
    )(update, inverse, object_field)
    update = pl.pallas_call(
        gradient_kernel(False),
        name="gradient",
        out_shape=ext_shape,
        in_specs=[SMEM] * 2 + [VMEM] * 4,
        out_specs=VMEM,
        scratch_shapes=[tall],
        compiler_params=params(),
    )(offsets, counts, ext, probe, measured, tables)
    return pl.pallas_call(
        last_kernel(grid),
        name="last",
        out_shape=jax.ShapeDtypeStruct((2, 384, 384), f32),
        in_specs=[VMEM] * 3,
        out_specs=VMEM,
        scratch_shapes=packs + packs + [ends, sems],
        compiler_params=params(2),
    )(update, inverse, ext)


def solution(mesh):
    grid = (mesh.shape["row"], mesh.shape["col"])
    tables = dft_tables(128)
    placed = (
        P(None, "row", "col"),
        P(),
        P("row", "col", None, None, None),
        P("row", "col", None, None),
        P("row", "col"),
    )

    def body(*args):
        return shards(grid, jnp.asarray(tables), *args)

    return jax.shard_map(body, mesh=mesh, in_specs=placed, out_specs=P(None, "row", "col"), check_vma=False)
```

```python
import math

import jax
import jax.numpy as jnp
import numpy as np
from jax import lax
from jax.experimental import pallas as pl
from jax.experimental.pallas import tpu as pltpu
from jax.sharding import PartitionSpec as P

AROUND = ((-1, 0), (1, 0), (0, -1), (0, 1), (-1, -1), (-1, 1), (1, -1), (1, 1))
MESH = pl.DeviceIdType.MESH
VMEM = pl.BlockSpec(memory_space=pltpu.VMEM)
SMEM = pl.BlockSpec(memory_space=pltpu.SMEM)
HBM = pl.BlockSpec(memory_space=pltpu.MemorySpace.HBM)
LIMIT = 24 << 20
NEAR, FAR, LEFT, RIGHT, FAR_LEFT, FAR_RIGHT, LEFT_NEXT, RIGHT_NEXT, RELAY = range(9)


def dft_tables(length):
    index = np.arange(length)
    angle = (np.outer(index, index) % length) * (2.0 * math.pi / length)
    cosine, sine = np.cos(angle) / math.sqrt(length), np.sin(angle) / math.sqrt(length)
    table = np.block([[cosine, -sine], [sine, cosine]])
    high = table.astype(jnp.bfloat16)
    low = (table - high.astype(np.float64)).astype(jnp.bfloat16)
    return np.stack([high, low, high.T, low.T])


def swap(x):
    return pltpu.roll(x, 64, x.ndim - 1)


def lower(rows):
    return lax.broadcasted_iota(jnp.int32, (rows, 128), 1) < 64


def pack(x, keep_low):
    rows = x.shape[0] // 2
    keep = lower(rows) if keep_low else ~lower(rows)
    return jnp.where(keep, x[:rows], swap(x[rows:]))


def unpack(x):
    return jnp.concatenate([x, swap(x)], axis=0)


def merge(a, b):
    keep = lower(a.shape[0])
    return jnp.concatenate([jnp.where(keep, a, b), jnp.where(keep, swap(a), swap(b))], axis=0)


class Place:
    def __init__(self, grid):
        self.row, self.col = lax.axis_index("row"), lax.axis_index("col")
        self.odd = lax.rem(self.row, 2)
        self.near_row = self.row + 1 - 2 * self.odd
        self.far_row = self.row - 1 + 2 * self.odd
        self.grid = grid
        far = (self.far_row >= 0) & (self.far_row < grid[0])
        left, right = self.col > 0, self.col < grid[1] - 1
        self.far, self.left, self.right = far, left, right
        both = (None, far, left, right, far & left, far & right, left, right, None)
        self.sends = both
        self.gets = tuple(both[i] for i in (NEAR, FAR, RIGHT, LEFT, FAR_RIGHT, FAR_LEFT, RIGHT_NEXT, LEFT_NEXT, RELAY))
        self.near_border = self.pick(320, 0)
        self.far_border = self.pick(0, 320)
        self.near_halo = self.pick(448, 0)
        self.far_halo = self.pick(0, 448)
        self.first = self.pick(256, 0)
        self.rest = self.pick(0, 128)

    def pick(self, even, odd):
        return pl.multiple_of(even + self.odd * (odd - even), 64)

    def target(self, which):
        row = {NEAR: self.near_row, RELAY: self.near_row, FAR: self.far_row, FAR_LEFT: self.far_row, FAR_RIGHT: self.far_row}
        side = {LEFT: -1, FAR_LEFT: -1, LEFT_NEXT: -1, RIGHT: 1, FAR_RIGHT: 1, RIGHT_NEXT: 1}
        return {"row": row.get(which, self.row), "col": self.col + side.get(which, 0)}


def when(condition, body):
    if condition is None:
        body()
    else:
        pl.when(condition)(body)


def greet(place):
    barrier = pltpu.get_barrier_semaphore()
    for which in (NEAR, FAR, LEFT, RIGHT, FAR_LEFT, FAR_RIGHT):
        when(
            place.sends[which],
            lambda: pl.semaphore_signal(
                barrier, inc=1, device_id=place.target(which), device_id_type=MESH
            ),
        )


def greeted(place):
    far, left, right = (jnp.where(x, 1, 0) for x in (place.far, place.left, place.right))
    pl.semaphore_wait(pltpu.get_barrier_semaphore(), 1 + far + (left + right) * (1 + far))


def greet_all(place):
    barrier = pltpu.get_barrier_semaphore()
    count = 0
    for d in AROUND:
        count += jnp.where(beside(place, d), 1, 0)

        @pl.when(beside(place, d))
        def _():
            pl.semaphore_signal(
                barrier, inc=1, device_id={"row": place.row + d[0], "col": place.col + d[1]}, device_id_type=MESH
            )

    return count


def beside(place, d):
    row, col = place.row + d[0], place.col + d[1]
    return (row >= 0) & (row < place.grid[0]) & (col >= 0) & (col < place.grid[1])


def remote(place, which, src, dst, sems, p):
    return pltpu.make_async_remote_copy(
        src, dst, sems.at[0, p, which], sems.at[1, p, which], device_id=place.target(which), device_id_type=MESH
    )


def start(place, copies, *which):
    for i in which:
        when(place.sends[i], copies[i].start)


def wait_recv(place, copies, *which):
    for i in which:
        when(place.gets[i], copies[i].wait_recv)


def wait_send(place, copies):
    for i, copy in enumerate(copies):
        when(place.sends[i], copy.wait_send)


def strips(side, side_in, corner, corner_in, p):
    return {
        FAR_LEFT: (corner.at[0, p], corner_in.at[0, p]),
        FAR_RIGHT: (corner.at[1, p], corner_in.at[1, p]),
        LEFT: (side.at[0, p, 0:64], side_in.at[0, p, 0:64]),
        RIGHT: (side.at[1, p, 0:64], side_in.at[1, p, 0:64]),
        LEFT_NEXT: (side.at[0, p, 64:192], side_in.at[0, p, 64:192]),
        RIGHT_NEXT: (side.at[1, p, 64:192], side_in.at[1, p, 64:192]),
    }


class Halo:
    def __init__(self, place, ext, side, corner, side_in, corner_in, sems):
        self.place, self.ext = place, ext
        self.side, self.corner, self.side_in, self.corner_in = side, corner, side_in, corner_in
        self.copies = []
        for p in range(2):
            ends = strips(side, side_in, corner, corner_in, p)
            rows = lambda first: pl.ds(first, 64)
            inner = lambda first: pl.ds(pl.multiple_of(first + 64, 64), 64)
            ends[NEAR] = (ext.at[p, inner(place.near_border), 0:384], ext.at[p, rows(place.far_halo), 0:384])
            ends[FAR] = (ext.at[p, inner(place.far_border), 0:384], ext.at[p, rows(place.near_halo), 0:384])
            ends[RELAY] = (ext.at[p, inner(place.near_border), 384:512], ext.at[p, rows(place.far_halo), 384:512])
            self.copies.append([remote(place, i, *ends[i], sems, p) for i in range(9)])

    def clear(self):
        place, ext = self.place, self.ext

        @pl.when(jnp.logical_not(place.far))
        def _():
            for p in range(2):
                ext[p, pl.ds(place.far_halo, 64), 0:384] = jnp.zeros((64, 384), jnp.float32)

        for k, side in enumerate((place.right, place.left)):

            @pl.when(jnp.logical_not(side))
            def _():
                self.side_in[k] = jnp.zeros((2, 192, 128), jnp.float32)

            @pl.when(jnp.logical_not(side & place.far))
            def _():
                self.corner_in[k] = jnp.zeros((2, 32, 128), jnp.float32)

    def pack(self, p):
        place, ext = self.place, self.ext
        for k, lane in enumerate((0, 256)):
            take = lambda first, rows: ext[p, pl.ds(pl.multiple_of(first + 64, 64), rows), lane : lane + 128]
            self.side[k, p, 0:64] = pack(take(place.first, 128), k == 0)
            self.side[k, p, 64:192] = pack(take(place.rest, 256), k == 0)
            self.corner[k, p] = pack(take(place.far_border, 64), k == 0)

    def start(self, p):
        start(self.place, self.copies[p], LEFT, RIGHT, FAR, NEAR, FAR_LEFT, FAR_RIGHT, LEFT_NEXT, RIGHT_NEXT)

    def finish(self):
        place, ext = self.place, self.ext
        for p in range(2):
            wait_recv(place, self.copies[p], LEFT, RIGHT)
            rows = pl.ds(pl.multiple_of(place.first + 64, 64), 128)
            ext[p, rows, 384:512] = merge(self.side_in[0, p, 0:64], self.side_in[1, p, 0:64])
            start(place, self.copies[p], RELAY)
            wait_recv(place, self.copies[p], FAR_LEFT, FAR_RIGHT, LEFT_NEXT, RIGHT_NEXT)
            ext[p, pl.ds(place.far_halo, 64), 384:512] = merge(self.corner_in[0, p], self.corner_in[1, p])
            rows = pl.ds(pl.multiple_of(place.rest + 64, 64), 256)
            ext[p, rows, 384:512] = merge(self.side_in[0, p, 64:192], self.side_in[1, p, 64:192])
        for p in range(2):
            wait_recv(place, self.copies[p], FAR, NEAR, RELAY)
            wait_send(place, self.copies[p])


class Fold:
    def __init__(self, place, update, ends_in, near_in, side, corner, side_in, corner_in, sems):
        self.place, self.update, self.ends_in, self.near_in = place, update, ends_in, near_in
        self.side, self.corner, self.side_in, self.corner_in = side, corner, side_in, corner_in
        self.copies = []
        for p in range(2):
            ends = strips(side, side_in, corner, corner_in, p)
            ends[NEAR] = (update.at[p, pl.ds(place.near_halo, 64), 0:384], ends_in.at[0, p])
            ends[FAR] = (update.at[p, pl.ds(place.far_halo, 64), 0:384], ends_in.at[1, p])
            ends[RELAY] = (update.at[p, pl.ds(place.near_halo, 64), 384:512], near_in.at[p])
            self.copies.append([remote(place, i, *ends[i], sems, p) for i in range(9)])

    def take(self, p, first, rows):
        return self.update[p, pl.ds(pl.multiple_of(first + 64, 64), rows), 384:512]

    def pack(self):
        place = self.place
        for p in range(2):
            for k in range(2):
                self.side[k, p, 64:192] = pack(self.take(p, place.rest, 256), k == 1)
                self.corner[k, p] = pack(self.update[p, pl.ds(place.far_halo, 64), 384:512], k == 1)

    def start(self):
        place = self.place
        odd = place.odd.astype(jnp.float32)
        for p in range(2):
            start(place, self.copies[p], RELAY)
        for p in range(2):
            start(place, self.copies[p], FAR, NEAR, FAR_LEFT, FAR_RIGHT, LEFT_NEXT, RIGHT_NEXT)
            wait_recv(place, self.copies[p], RELAY)
            part = self.take(p, place.first, 128)
            near = self.near_in[p]
            part = jnp.concatenate([part[:64] + near * odd, part[64:] + near * (1.0 - odd)], axis=0)
            for k in range(2):
                self.side[k, p, 0:64] = pack(part, k == 1)
            start(place, self.copies[p], LEFT, RIGHT)

    def finish(self, p, dest, base, inverse):
        place = self.place

        def add(first, lane, value):
            lanes, rows = pl.ds(lane, value.shape[1]), value.shape[0]
            at = pl.ds(pl.multiple_of(first + base, 64), rows)
            dest[p, at, lanes] += value * inverse[pl.ds(pl.multiple_of(first, 64), rows), lanes]

        def side(k, value):
            keep = ~lower(value.shape[0]) if k == 0 else lower(value.shape[0])
            return 256 if k == 0 else 0, jnp.where(keep, value, 0.0)

        for i in (FAR, NEAR, FAR_LEFT, FAR_RIGHT, LEFT_NEXT, RIGHT_NEXT, LEFT, RIGHT):

            def body():
                self.copies[p][i].wait_recv()
                k = i % 2
                if i == NEAR:
                    add(place.near_border, 0, self.ends_in[0, p])
                elif i == FAR:
                    add(place.far_border, 0, self.ends_in[1, p])
                elif i in (FAR_LEFT, FAR_RIGHT):
                    add(place.far_border, *side(k, unpack(self.corner_in[k, p])))
                elif i in (LEFT, RIGHT):
                    add(place.first, *side(k, unpack(self.side_in[k, p, 0:64])))
                else:
                    add(place.rest, *side(k, unpack(self.side_in[k, p, 64:192])))

            when(place.gets[i], body)

    def close(self):
        for p in range(2):
            wait_send(self.place, self.copies[p])


def spread_kernel(grid):
    def kernel(
        field, offsets, counts, measured, tables, probe,
        ext, around, measured_here, tables_here, probe_here, update, light,
        mine, offsets_here, side, corner, side_in, corner_in, sems, notes, local,
    ):
        place = Place(grid)
        peers = greet_all(place)
        pulls = [pltpu.make_async_copy(offsets, offsets_here, local.at[0])]
        pulls += [pltpu.make_async_copy(field.at[p], ext.at[p, 64:448, 0:384], local.at[1 + p]) for p in range(2)]
        later = [
            pltpu.make_async_copy(measured, measured_here, local.at[3]),
            pltpu.make_async_copy(tables, tables_here, local.at[4]),
            pltpu.make_async_copy(probe, probe_here, local.at[5]),
        ]
        for pull in pulls:
            pull.start()
        halo = Halo(place, ext, side, corner, side_in, corner_in, sems)
        halo.clear()
        for i, d in enumerate(AROUND):

            @pl.when(jnp.logical_not(beside(place, d)))
            def _():
                around[i] = jnp.zeros((8, 128), jnp.int32)

        pulls[0].wait()
        mine[0:2, 0:12] = offsets_here[0, 0]
        mine[2:3, 0:1] = jnp.full((1, 1), counts[0, 0], jnp.int32)
        around[8] = mine[...]
        pulls[1].wait()
        halo.pack(0)
        pl.semaphore_wait(pltpu.get_barrier_semaphore(), peers)
        halo.start(0)
        pulls[2].wait()
        halo.pack(1)
        halo.start(1)
        letters = []
        for i, d in enumerate(AROUND):
            letter = pltpu.make_async_remote_copy(
                mine,
                around.at[AROUND.index((-d[0], -d[1]))],
                notes.at[0, i],
                notes.at[1, i],
                device_id={"row": place.row + d[0], "col": place.col + d[1]},
                device_id_type=MESH,
            )
            letters.append(letter)
            pl.when(beside(place, d))(letter.start)
        for pull in later:
            pull.start()
        update[...] = jnp.zeros_like(update)
        light[...] = jnp.zeros_like(light)
        halo.finish()
        for i, d in enumerate(AROUND):
            pl.when(beside(place, d))(letters[i].wait_send)
            pl.when(beside(place, (-d[0], -d[1])))(letters[i].wait_recv)
        for pull in later:
            pull.wait()

    return kernel


def split(x):
    high = x.astype(jnp.bfloat16)
    return high, (x - high.astype(jnp.float32)).astype(jnp.bfloat16)


def dot(a, b):
    return jnp.dot(a, b, preferred_element_type=jnp.float32)


def right_mul(x, high, low):
    xh, xl = split(x)
    return dot(xh, high) + dot(xl, high) + dot(xh, low)


def left_mul(high, low, x):
    xh, xl = split(x)
    return dot(high, xh) + dot(high, xl) + dot(low, xh)


def cross(x):
    return jnp.concatenate(
        [
            jnp.concatenate([x[:128, :128], x[128:, :128]], axis=1),
            jnp.concatenate([x[:128, 128:], x[128:, 128:]], axis=1),
        ],
        axis=0,
    )


def gradient_kernel(with_light):
    def kernel(*refs):
        if with_light:
            around, ext, probe, measured, tables, _, _, update, inverse, light, tall, power = refs
        else:
            around, ext, probe, measured, tables, _, update, tall = refs
        count = around[8, 2, 0]
        for p in range(2):
            tall[p, 0:8] = probe[p, 120:128]
            tall[p, 8:136] = probe[p]
        lane = lax.broadcasted_iota(jnp.int32, (128, 128), 1)
        sub = lax.broadcasted_iota(jnp.int32, (8, 128), 0)

        def turned(source, shift_rows, shift_lanes):
            return pltpu.roll(source[pl.ds(8 - shift_rows, 128), :], shift_lanes, 1)

        def scatter(dest, first, lanes, shift_rows, shift_lanes, value):
            head = jnp.where(sub >= shift_rows, value[:8], 0.0)
            main = jnp.concatenate([head, value[8:]], axis=0)
            tail = jnp.where(sub < shift_rows, value[:8], 0.0)
            for which, at in enumerate(lanes):
                keep = lane >= shift_lanes if which == 0 else lane < shift_lanes
                dest[pl.ds(first, 128), at] += jnp.where(keep, main, 0.0)
                dest[pl.ds(first + 128, 8), at] += jnp.where(keep[:8], tail, 0.0)

        def tiles_of(col, base, wrap):
            tile = lax.shift_right_arithmetic(col, 7) + base
            first = lax.rem(tile + wrap, wrap)
            second = lax.rem(tile + wrap + 1, wrap)
            return [pl.ds(pl.multiple_of(t * 128, 128), 128) for t in (first, second)]

        def brighten(row, col, value):
            low_row, low_col = jnp.bitwise_and(row, 7), jnp.bitwise_and(col, 127)
            first = pl.multiple_of(row - low_row + 128, 8)
            scatter(light, first, tiles_of(col, 1, 5), low_row, low_col, value)

        def gather(slot):
            row, col = around[8, 0, slot], around[8, 1, slot]
            low_row, low_col = jnp.bitwise_and(row, 7), jnp.bitwise_and(col, 127)
            first = pl.multiple_of(row - low_row + 64, 8)
            lanes = tiles_of(col, 0, 4)
            beam = [turned(tall.at[p], low_row, low_col) for p in range(2)]
            window = []
            for p in range(2):
                main = jnp.where(
                    lane >= low_col, ext[p, pl.ds(first, 128), lanes[0]], ext[p, pl.ds(first, 128), lanes[1]]
                )
                tail = jnp.where(
                    lane[:8] >= low_col,
                    ext[p, pl.ds(first + 128, 8), lanes[0]],
                    ext[p, pl.ds(first + 128, 8), lanes[1]],
                )
                window.append(jnp.concatenate([jnp.where(sub >= low_row, main[:8], tail), main[8:]], axis=0))
            real = beam[0] * window[0] - beam[1] * window[1]
            imag = beam[0] * window[1] + beam[1] * window[0]
            live = (slot < count).astype(jnp.float32)
            return jnp.concatenate([real, imag], axis=1), (first, lanes, low_row, low_col, live, row, col)

        def put(back, at):
            first, lanes, low_row, low_col, live, row, col = at
            beam = [turned(tall.at[p], low_row, low_col) * live for p in range(2)]
            real, imag = back[:, :128], back[:, 128:]
            scatter(update.at[0], first, lanes, low_row, low_col, beam[0] * real + beam[1] * imag)
            scatter(update.at[1], first, lanes, low_row, low_col, beam[0] * imag - beam[1] * real)
            if with_light:
                brighten(row, col, beam[0] * beam[0] + beam[1] * beam[1])

        def quad(step, carry):
            slots = [step * 4 + k for k in range(4)]
            pairs = ((0, 1), (2, 3))
            gathered = [gather(slot) for slot in slots]
            waves = [jnp.concatenate([gathered[a][0], gathered[b][0]], axis=0) for a, b in pairs]
            half = [cross(right_mul(wave, tables[0], tables[1])) for wave in waves]
            far = [left_mul(tables[2], tables[3], x) for x in half]
            change = []
            for x, (a, b) in zip(far, pairs):
                real, imag = x[:128], x[128:]
                known = jnp.concatenate([measured[0, 0, slots[a]], measured[0, 0, slots[b]]], axis=1)
                ratio = known * lax.rsqrt(real * real + imag * imag + 0.25) - 1.0
                change.append(jnp.concatenate([real * ratio, imag * ratio], axis=0))
            half = [cross(left_mul(tables[0], tables[1], x)) for x in change]
            back = [right_mul(x, tables[2], tables[3]) for x in half]
            for x, (a, b) in zip(back, pairs):
                put(x[:128], gathered[a][1])
                put(x[128:], gathered[b][1])
            return carry

        lax.fori_loop(0, lax.shift_right_logical(count + 3, 2), quad, 0)
        if with_light:
            power[...] = tall[0] * tall[0] + tall[1] * tall[1]
            for i, d in enumerate(AROUND):

                def other(slot, carry):
                    row = around[i, 0, slot] + d[0] * 384
                    col = around[i, 1, slot] + d[1] * 384
                    touches = (row > -128) & (row < 384) & (col > -128) & (col < 384)

                    @pl.when(touches)
                    def _():
                        low_row, low_col = jnp.bitwise_and(row, 7), jnp.bitwise_and(col, 127)
                        brighten(row, col, turned(power, low_row, low_col))

                    return carry

                lax.fori_loop(0, around[i, 2, 0], other, 0)
            inverse[...] = 1.0 / (light[128:512, 128:512] + 1.0)

    return kernel


def between_kernel(grid):
    def kernel(
        update, inverse, field,
        ext, cleared,
        ends_in, near_in, side, corner, side_in, corner_in, sems,
        halo_side, halo_corner, halo_side_in, halo_corner_in, more,
    ):
        place = Place(grid)
        greet(place)
        fold = Fold(place, update, ends_in, near_in, side, corner, side_in, corner_in, sems)
        halo = Halo(place, ext, halo_side, halo_corner, halo_side_in, halo_corner_in, more)
        fold.pack()
        greeted(place)
        fold.start()
        halo.clear()
        for p in range(2):
            ext[p, 64:448, 0:384] = field[p, 64:448, 0:384] + update[p, 64:448, 0:384] * inverse[...]
        cleared[...] = jnp.zeros_like(cleared)
        for p in range(2):
            fold.finish(p, ext, 64, inverse)
            halo.pack(p)
            halo.start(p)
        halo.finish()
        fold.close()

    return kernel


def last_kernel(grid):
    def kernel(update, inverse, ext, out, ends_in, near_in, side, corner, side_in, corner_in, sems):
        place = Place(grid)
        greet(place)
        fold = Fold(place, update, ends_in, near_in, side, corner, side_in, corner_in, sems)
        fold.pack()
        greeted(place)
        fold.start()
        for p in range(2):
            out[p] = ext[p, 64:448, 0:384] + update[p, 64:448, 0:384] * inverse[...]
        for p in range(2):
            fold.finish(p, out, 0, inverse)
        fold.close()

    return kernel


def hold(x):
    return pltpu.with_memory_space_constraint(x, pltpu.MemorySpace.HBM)


def params(collective_id=None):
    if collective_id is None:
        return pltpu.CompilerParams(vmem_limit_bytes=LIMIT)
    return pltpu.CompilerParams(collective_id=collective_id, has_side_effects=True, vmem_limit_bytes=LIMIT)


def shards(grid, tables, object_field, probe, amplitudes, offsets, counts):
    f32, i32 = jnp.float32, jnp.int32
    shape = jax.ShapeDtypeStruct
    ext_shape = shape((2, 512, 512), f32)
    packs = [pltpu.VMEM((2, 2, 192, 128), f32), pltpu.VMEM((2, 2, 32, 128), f32)]
    folds = [pltpu.VMEM((2, 2, 64, 384), f32), pltpu.VMEM((2, 64, 128), f32)] + packs + packs
    sems = pltpu.SemaphoreType.DMA((2, 2, 9))
    ext, around, measured, tables, probe, update, light = pl.pallas_call(
        spread_kernel(grid),
        name="spread",
        out_shape=(
            ext_shape,
            shape((9, 8, 128), i32),
            shape(amplitudes.shape, f32),
            shape(tables.shape, tables.dtype),
            shape(probe.shape, f32),
            ext_shape,
            shape((648, 640), f32),
        ),
        in_specs=[HBM, HBM, SMEM, HBM, HBM, HBM],
        out_specs=(VMEM,) * 7,
        scratch_shapes=[pltpu.VMEM((8, 128), i32), pltpu.VMEM((1, 1, 2, 12), i32)]
        + packs
        + packs
        + [sems, pltpu.SemaphoreType.DMA((2, 8)), pltpu.SemaphoreType.DMA((6,))],
        compiler_params=params(0),
    )(*(hold(x) for x in (object_field, jnp.swapaxes(offsets, 2, 3))), counts, *(hold(x) for x in (amplitudes, tables, probe)))
    tall = pltpu.VMEM((2, 136, 128), f32)
    update, inverse, _ = pl.pallas_call(
        gradient_kernel(True),
        name="gradient_light",
        out_shape=(ext_shape, shape((384, 384), f32), shape((648, 640), f32)),
        in_specs=[SMEM] + [VMEM] * 6,
        out_specs=(VMEM,) * 3,
        scratch_shapes=[tall, pltpu.VMEM((136, 128), f32)],
        input_output_aliases={5: 0, 6: 2},
        compiler_params=params(),
    )(around, ext, probe, measured, tables, update, light)
    ext, cleared = pl.pallas_call(
        between_kernel(grid),
        name="between",
        out_shape=(ext_shape, ext_shape),
        in_specs=[VMEM] * 3,
        out_specs=(VMEM, VMEM),
        scratch_shapes=folds + [sems] + packs + packs + [sems],
        compiler_params=params(1),
    )(update, inverse, ext)
    update = pl.pallas_call(
        gradient_kernel(False),
        name="gradient",
        out_shape=ext_shape,
        in_specs=[SMEM] + [VMEM] * 5,
        out_specs=VMEM,
        scratch_shapes=[tall],
        input_output_aliases={5: 0},
        compiler_params=params(),
    )(around, ext, probe, measured, tables, cleared)
    return pl.pallas_call(
        last_kernel(grid),
        name="last",
        out_shape=shape((2, 384, 384), f32),
        in_specs=[VMEM] * 3,
        out_specs=VMEM,
        scratch_shapes=folds + [sems],
        compiler_params=params(2),
    )(update, inverse, ext)


def solution(mesh):
    grid = (mesh.shape["row"], mesh.shape["col"])
    tables = dft_tables(128)
    placed = (
        P(None, "row", "col"),
        P(),
        P("row", "col", None, None, None),
        P("row", "col", None, None),
        P("row", "col"),
    )

    def body(*args):
        return shards(grid, jnp.asarray(tables), *args)

    return jax.shard_map(body, mesh=mesh, in_specs=placed, out_specs=P(None, "row", "col"), check_vma=False)
```

```python
import math

import jax
import jax.numpy as jnp
import numpy as np
from jax import lax
from jax.experimental import pallas as pl
from jax.experimental.pallas import tpu as pltpu
from jax.sharding import PartitionSpec as P

AROUND = ((-1, 0), (1, 0), (0, -1), (0, 1), (-1, -1), (-1, 1), (1, -1), (1, 1))
MESH = pl.DeviceIdType.MESH
VMEM = pl.BlockSpec(memory_space=pltpu.VMEM)
SMEM = pl.BlockSpec(memory_space=pltpu.SMEM)
HBM = pl.BlockSpec(memory_space=pltpu.MemorySpace.HBM)
LIMIT = 24 << 20
GROUP = 6
NEAR, FAR, LEFT, RIGHT, FAR_LEFT, FAR_RIGHT, LEFT_NEXT, RIGHT_NEXT, RELAY = range(9)


def dft_tables(length):
    index = np.arange(length)
    angle = (np.outer(index, index) % length) * (2.0 * math.pi / length)
    cosine, sine = np.cos(angle) / math.sqrt(length), np.sin(angle) / math.sqrt(length)
    table = np.block([[cosine, -sine], [sine, cosine]])
    high = table.astype(jnp.bfloat16)
    low = (table - high.astype(np.float64)).astype(jnp.bfloat16)
    return np.stack([high, low, high.T, low.T])


def swap(x):
    return pltpu.roll(x, 64, x.ndim - 1)


def lower(rows):
    return lax.broadcasted_iota(jnp.int32, (rows, 128), 1) < 64


def pack(x, keep_low):
    rows = x.shape[0] // 2
    keep = lower(rows) if keep_low else ~lower(rows)
    return jnp.where(keep, x[:rows], swap(x[rows:]))


def unpack(x):
    return jnp.concatenate([x, swap(x)], axis=0)


def merge(a, b):
    keep = lower(a.shape[0])
    return jnp.concatenate([jnp.where(keep, a, b), jnp.where(keep, swap(a), swap(b))], axis=0)


class Place:
    def __init__(self, grid):
        self.row, self.col = lax.axis_index("row"), lax.axis_index("col")
        self.odd = lax.rem(self.row, 2)
        self.near_row = self.row + 1 - 2 * self.odd
        self.far_row = self.row - 1 + 2 * self.odd
        self.grid = grid
        far = (self.far_row >= 0) & (self.far_row < grid[0])
        left, right = self.col > 0, self.col < grid[1] - 1
        self.far, self.left, self.right = far, left, right
        both = (None, far, left, right, far & left, far & right, left, right, None)
        self.sends = both
        self.gets = tuple(both[i] for i in (NEAR, FAR, RIGHT, LEFT, FAR_RIGHT, FAR_LEFT, RIGHT_NEXT, LEFT_NEXT, RELAY))
        self.near_border = self.pick(320, 0)
        self.far_border = self.pick(0, 320)
        self.near_halo = self.pick(448, 0)
        self.far_halo = self.pick(0, 448)
        self.first = self.pick(256, 0)
        self.rest = self.pick(0, 128)

    def pick(self, even, odd):
        return pl.multiple_of(even + self.odd * (odd - even), 64)

    def target(self, which):
        row = {NEAR: self.near_row, RELAY: self.near_row, FAR: self.far_row, FAR_LEFT: self.far_row, FAR_RIGHT: self.far_row}
        side = {LEFT: -1, FAR_LEFT: -1, LEFT_NEXT: -1, RIGHT: 1, FAR_RIGHT: 1, RIGHT_NEXT: 1}
        return {"row": row.get(which, self.row), "col": self.col + side.get(which, 0)}


def when(condition, body):
    if condition is None:
        body()
    else:
        pl.when(condition)(body)


def greet(place):
    barrier = pltpu.get_barrier_semaphore()
    for which in (NEAR, FAR, LEFT, RIGHT, FAR_LEFT, FAR_RIGHT):
        when(
            place.sends[which],
            lambda: pl.semaphore_signal(
                barrier, inc=1, device_id=place.target(which), device_id_type=MESH
            ),
        )


def greeted(place):
    far, left, right = (jnp.where(x, 1, 0) for x in (place.far, place.left, place.right))
    pl.semaphore_wait(pltpu.get_barrier_semaphore(), 1 + far + (left + right) * (1 + far))


def greet_all(place):
    barrier = pltpu.get_barrier_semaphore()
    count = 0
    for d in AROUND:
        count += jnp.where(beside(place, d), 1, 0)

        @pl.when(beside(place, d))
        def _():
            pl.semaphore_signal(
                barrier, inc=1, device_id={"row": place.row + d[0], "col": place.col + d[1]}, device_id_type=MESH
            )

    return count


def beside(place, d):
    row, col = place.row + d[0], place.col + d[1]
    return (row >= 0) & (row < place.grid[0]) & (col >= 0) & (col < place.grid[1])


def remote(place, which, src, dst, sems, p):
    return pltpu.make_async_remote_copy(
        src, dst, sems.at[0, p, which], sems.at[1, p, which], device_id=place.target(which), device_id_type=MESH
    )


def start(place, copies, *which):
    for i in which:
        when(place.sends[i], copies[i].start)


def wait_recv(place, copies, *which):
    for i in which:
        when(place.gets[i], copies[i].wait_recv)


def wait_send(place, copies):
    for i, copy in enumerate(copies):
        when(place.sends[i], copy.wait_send)


def strips(side, side_in, corner, corner_in, p):
    return {
        FAR_LEFT: (corner.at[0, p], corner_in.at[0, p]),
        FAR_RIGHT: (corner.at[1, p], corner_in.at[1, p]),
        LEFT: (side.at[0, p, 0:64], side_in.at[0, p, 0:64]),
        RIGHT: (side.at[1, p, 0:64], side_in.at[1, p, 0:64]),
        LEFT_NEXT: (side.at[0, p, 64:192], side_in.at[0, p, 64:192]),
        RIGHT_NEXT: (side.at[1, p, 64:192], side_in.at[1, p, 64:192]),
    }


class Halo:
    def __init__(self, place, ext, side, corner, side_in, corner_in, sems):
        self.place, self.ext = place, ext
        self.side, self.corner, self.side_in, self.corner_in = side, corner, side_in, corner_in
        self.copies = []
        for p in range(2):
            ends = strips(side, side_in, corner, corner_in, p)
            rows = lambda first: pl.ds(first, 64)
            inner = lambda first: pl.ds(pl.multiple_of(first + 64, 64), 64)
            ends[NEAR] = (ext.at[p, inner(place.near_border), 0:384], ext.at[p, rows(place.far_halo), 0:384])
            ends[FAR] = (ext.at[p, inner(place.far_border), 0:384], ext.at[p, rows(place.near_halo), 0:384])
            ends[RELAY] = (ext.at[p, inner(place.near_border), 384:512], ext.at[p, rows(place.far_halo), 384:512])
            self.copies.append([remote(place, i, *ends[i], sems, p) for i in range(9)])

    def clear(self):
        place, ext = self.place, self.ext

        @pl.when(jnp.logical_not(place.far))
        def _():
            for p in range(2):
                ext[p, pl.ds(place.far_halo, 64), 0:384] = jnp.zeros((64, 384), jnp.float32)

        for k, side in enumerate((place.right, place.left)):

            @pl.when(jnp.logical_not(side))
            def _():
                self.side_in[k] = jnp.zeros((2, 192, 128), jnp.float32)

            @pl.when(jnp.logical_not(side & place.far))
            def _():
                self.corner_in[k] = jnp.zeros((2, 32, 128), jnp.float32)

    def pack(self, p):
        place, ext = self.place, self.ext
        for k, lane in enumerate((0, 256)):
            take = lambda first, rows: ext[p, pl.ds(pl.multiple_of(first + 64, 64), rows), lane : lane + 128]
            self.side[k, p, 0:64] = pack(take(place.first, 128), k == 0)
            self.side[k, p, 64:192] = pack(take(place.rest, 256), k == 0)
            self.corner[k, p] = pack(take(place.far_border, 64), k == 0)

    def start(self, p):
        start(self.place, self.copies[p], LEFT, RIGHT, FAR, NEAR, FAR_LEFT, FAR_RIGHT, LEFT_NEXT, RIGHT_NEXT)

    def finish(self):
        place, ext = self.place, self.ext
        for p in range(2):
            wait_recv(place, self.copies[p], LEFT, RIGHT)
            rows = pl.ds(pl.multiple_of(place.first + 64, 64), 128)
            ext[p, rows, 384:512] = merge(self.side_in[0, p, 0:64], self.side_in[1, p, 0:64])
            start(place, self.copies[p], RELAY)
            wait_recv(place, self.copies[p], FAR_LEFT, FAR_RIGHT, LEFT_NEXT, RIGHT_NEXT)
            ext[p, pl.ds(place.far_halo, 64), 384:512] = merge(self.corner_in[0, p], self.corner_in[1, p])
            rows = pl.ds(pl.multiple_of(place.rest + 64, 64), 256)
            ext[p, rows, 384:512] = merge(self.side_in[0, p, 64:192], self.side_in[1, p, 64:192])
        for p in range(2):
            wait_recv(place, self.copies[p], FAR, NEAR, RELAY)
            wait_send(place, self.copies[p])


class Fold:
    def __init__(self, place, update, ends_in, near_in, side, corner, side_in, corner_in, sems):
        self.place, self.update, self.ends_in, self.near_in = place, update, ends_in, near_in
        self.side, self.corner, self.side_in, self.corner_in = side, corner, side_in, corner_in
        self.copies = []
        for p in range(2):
            ends = strips(side, side_in, corner, corner_in, p)
            ends[NEAR] = (update.at[p, pl.ds(place.near_halo, 64), 0:384], ends_in.at[0, p])
            ends[FAR] = (update.at[p, pl.ds(place.far_halo, 64), 0:384], ends_in.at[1, p])
            ends[RELAY] = (update.at[p, pl.ds(place.near_halo, 64), 384:512], near_in.at[p])
            self.copies.append([remote(place, i, *ends[i], sems, p) for i in range(9)])

    def take(self, p, first, rows):
        return self.update[p, pl.ds(pl.multiple_of(first + 64, 64), rows), 384:512]

    def pack(self):
        place = self.place
        for p in range(2):
            for k in range(2):
                self.side[k, p, 64:192] = pack(self.take(p, place.rest, 256), k == 1)
                self.corner[k, p] = pack(self.update[p, pl.ds(place.far_halo, 64), 384:512], k == 1)

    def start(self):
        place = self.place
        odd = place.odd.astype(jnp.float32)
        for p in range(2):
            start(place, self.copies[p], RELAY)
        for p in range(2):
            start(place, self.copies[p], FAR, NEAR, FAR_LEFT, FAR_RIGHT, LEFT_NEXT, RIGHT_NEXT)
            wait_recv(place, self.copies[p], RELAY)
            part = self.take(p, place.first, 128)
            near = self.near_in[p]
            part = jnp.concatenate([part[:64] + near * odd, part[64:] + near * (1.0 - odd)], axis=0)
            for k in range(2):
                self.side[k, p, 0:64] = pack(part, k == 1)
            start(place, self.copies[p], LEFT, RIGHT)

    def finish(self, p, dest, base, inverse):
        place = self.place

        def add(first, lane, value):
            lanes, rows = pl.ds(lane, value.shape[1]), value.shape[0]
            at = pl.ds(pl.multiple_of(first + base, 64), rows)
            dest[p, at, lanes] += value * inverse[pl.ds(pl.multiple_of(first, 64), rows), lanes]

        def side(k, value):
            keep = ~lower(value.shape[0]) if k == 0 else lower(value.shape[0])
            return 256 if k == 0 else 0, jnp.where(keep, value, 0.0)

        for i in (FAR, NEAR, FAR_LEFT, FAR_RIGHT, LEFT_NEXT, RIGHT_NEXT, LEFT, RIGHT):

            def body():
                self.copies[p][i].wait_recv()
                k = i % 2
                if i == NEAR:
                    add(place.near_border, 0, self.ends_in[0, p])
                elif i == FAR:
                    add(place.far_border, 0, self.ends_in[1, p])
                elif i in (FAR_LEFT, FAR_RIGHT):
                    add(place.far_border, *side(k, unpack(self.corner_in[k, p])))
                elif i in (LEFT, RIGHT):
                    add(place.first, *side(k, unpack(self.side_in[k, p, 0:64])))
                else:
                    add(place.rest, *side(k, unpack(self.side_in[k, p, 64:192])))

            when(place.gets[i], body)

    def close(self):
        for p in range(2):
            wait_send(self.place, self.copies[p])


def spread_kernel(grid):
    def kernel(
        field, offsets, counts, places, measured, tables, probe,
        ext, around, measured_here, tables_here, beams, power, update, light,
        mine, offsets_here, tall, side, corner, side_in, corner_in, sems, notes, local,
    ):
        place = Place(grid)
        peers = greet_all(place)
        pulls = [pltpu.make_async_copy(offsets, offsets_here, local.at[0])]
        pulls += [pltpu.make_async_copy(field.at[p], ext.at[p, 64:448, 0:384], local.at[1 + p]) for p in range(2)]
        later = [
            pltpu.make_async_copy(measured, measured_here, local.at[3]),
            pltpu.make_async_copy(tables, tables_here, local.at[4]),
        ]
        pulls.append(pltpu.make_async_copy(probe, tall.at[:, 8:136], local.at[5]))
        for pull in pulls:
            pull.start()
        halo = Halo(place, ext, side, corner, side_in, corner_in, sems)
        halo.clear()
        for i, d in enumerate(AROUND):

            @pl.when(jnp.logical_not(beside(place, d)))
            def _():
                around[i] = jnp.zeros((8, 128), jnp.int32)

        pulls[0].wait()
        mine[0:2, 0:12] = offsets_here[0, 0]
        mine[2:3, 0:1] = jnp.full((1, 1), counts[0, 0], jnp.int32)
        around[8] = mine[...]
        letters = []
        for i, d in enumerate(AROUND):
            letter = pltpu.make_async_remote_copy(
                mine,
                around.at[AROUND.index((-d[0], -d[1]))],
                notes.at[0, i],
                notes.at[1, i],
                device_id={"row": place.row + d[0], "col": place.col + d[1]},
                device_id_type=MESH,
            )
            letters.append(letter)
        pulls[1].wait()
        halo.pack(0)
        pl.semaphore_wait(pltpu.get_barrier_semaphore(), peers)
        for i, d in enumerate(AROUND):
            pl.when(beside(place, d))(letters[i].start)
        halo.start(0)
        pulls[2].wait()
        halo.pack(1)
        halo.start(1)
        for pull in later:
            pull.start()
        update[...] = jnp.zeros_like(update)
        light[...] = jnp.zeros_like(light)
        pulls[3].wait()
        for p in range(2):
            tall[p, 0:8] = tall[p, 128:136]
        power[...] = tall[0] * tall[0] + tall[1] * tall[1]

        def turn(slot, carry):
            live = (slot < counts[0, 0]).astype(jnp.float32)
            low_row, low_col = places[0, 0, 0, slot] & 7, places[0, 0, 1, slot] & 127
            for p in range(2):
                beams[slot, p] = pltpu.roll(tall[p, pl.ds(8 - low_row, 128), :], low_col, 1) * live
            return carry

        lax.fori_loop(0, 12, turn, 0)
        halo.finish()
        for i, d in enumerate(AROUND):
            pl.when(beside(place, d))(letters[i].wait_send)
            pl.when(beside(place, (-d[0], -d[1])))(letters[i].wait_recv)
        for pull in later:
            pull.wait()

    return kernel


def split(x):
    high = x.astype(jnp.bfloat16)
    return high, (x - high.astype(jnp.float32)).astype(jnp.bfloat16)


def dot(a, b):
    return jnp.dot(a, b, preferred_element_type=jnp.float32)


def right_mul(x, high, low):
    xh, xl = split(x)
    return dot(xh, high) + dot(xl, high) + dot(xh, low)


def left_mul(high, low, x):
    xh, xl = split(x)
    return dot(high, xh) + dot(high, xl) + dot(low, xh)


def cross(x):
    return jnp.concatenate(
        [
            jnp.concatenate([x[:128, :128], x[128:, :128]], axis=1),
            jnp.concatenate([x[:128, 128:], x[128:, 128:]], axis=1),
        ],
        axis=0,
    )


def gradient_kernel(with_light):
    def kernel(*refs):
        if with_light:
            around, ext, beams, measured, tables, _, power, _, update, light = refs
        else:
            around, ext, beams, measured, tables, _, update = refs
        count = around[8, 2, 0]
        lane = lax.broadcasted_iota(jnp.int32, (128, 128), 1)
        sub = lax.broadcasted_iota(jnp.int32, (8, 128), 0)

        def turned(source, shift_rows, shift_lanes):
            return pltpu.roll(source[pl.ds(8 - shift_rows, 128), :], shift_lanes, 1)

        def scatter(dest, first, lanes, shift_rows, shift_lanes, value):
            head = jnp.where(sub >= shift_rows, value[:8], 0.0)
            main = jnp.concatenate([head, value[8:]], axis=0)
            tail = jnp.where(sub < shift_rows, value[:8], 0.0)
            for which, at in enumerate(lanes):
                keep = lane >= shift_lanes if which == 0 else lane < shift_lanes
                dest[pl.ds(first, 128), at] += jnp.where(keep, main, 0.0)
                dest[pl.ds(first + 128, 8), at] += jnp.where(keep[:8], tail, 0.0)

        def tiles_of(col, base, wrap):
            tile = lax.shift_right_arithmetic(col, 7) + base
            first = lax.rem(tile + wrap, wrap)
            second = lax.rem(tile + wrap + 1, wrap)
            return [pl.ds(pl.multiple_of(t * 128, 128), 128) for t in (first, second)]

        def brighten(row, col, value):
            low_row, low_col = jnp.bitwise_and(row, 7), jnp.bitwise_and(col, 127)
            first = pl.multiple_of(row - low_row + 128, 8)
            scatter(light, first, tiles_of(col, 1, 5), low_row, low_col, value)

        def gather(slot):
            row, col = around[8, 0, slot], around[8, 1, slot]
            low_row, low_col = jnp.bitwise_and(row, 7), jnp.bitwise_and(col, 127)
            first = pl.multiple_of(row - low_row + 64, 8)
            lanes = tiles_of(col, 0, 4)
            beam = [beams[slot, p] for p in range(2)]
            window = []
            for p in range(2):
                main = jnp.where(
                    lane >= low_col, ext[p, pl.ds(first, 128), lanes[0]], ext[p, pl.ds(first, 128), lanes[1]]
                )
                tail = jnp.where(
                    lane[:8] >= low_col,
                    ext[p, pl.ds(first + 128, 8), lanes[0]],
                    ext[p, pl.ds(first + 128, 8), lanes[1]],
                )
                window.append(jnp.concatenate([jnp.where(sub >= low_row, main[:8], tail), main[8:]], axis=0))
            real = beam[0] * window[0] - beam[1] * window[1]
            imag = beam[0] * window[1] + beam[1] * window[0]
            return jnp.concatenate([real, imag], axis=1), (slot, first, lanes, low_row, low_col, row, col)

        def put(back, at):
            slot, first, lanes, low_row, low_col, row, col = at
            beam = [beams[slot, p] for p in range(2)]
            real, imag = back[:, :128], back[:, 128:]
            scatter(update.at[0], first, lanes, low_row, low_col, beam[0] * real + beam[1] * imag)
            scatter(update.at[1], first, lanes, low_row, low_col, beam[0] * imag - beam[1] * real)
            if with_light:
                brighten(row, col, beam[0] * beam[0] + beam[1] * beam[1])

        def some(step, carry):
            slots = [step * GROUP + k for k in range(GROUP)]
            pairs = [(k, k + 1) for k in range(0, GROUP, 2)]
            gathered = [gather(slot) for slot in slots]
            waves = [jnp.concatenate([gathered[a][0], gathered[b][0]], axis=0) for a, b in pairs]
            half = [cross(right_mul(wave, tables[0], tables[1])) for wave in waves]
            far = [left_mul(tables[2], tables[3], x) for x in half]
            change = []
            for x, (a, b) in zip(far, pairs):
                real, imag = x[:128], x[128:]
                known = jnp.concatenate([measured[0, 0, slots[a]], measured[0, 0, slots[b]]], axis=1)
                ratio = known * lax.rsqrt(real * real + imag * imag + 0.25) - 1.0
                change.append(jnp.concatenate([real * ratio, imag * ratio], axis=0))
            half = [cross(left_mul(tables[0], tables[1], x)) for x in change]
            back = [right_mul(x, tables[2], tables[3]) for x in half]
            for x, (a, b) in zip(back, pairs):
                put(x[:128], gathered[a][1])
                put(x[128:], gathered[b][1])
            return carry

        lax.fori_loop(0, (count + GROUP - 1) // GROUP, some, 0)
        if with_light:
            for i, d in enumerate(AROUND):

                def other(slot, carry):
                    row = around[i, 0, slot] + d[0] * 384
                    col = around[i, 1, slot] + d[1] * 384
                    touches = (row > -128) & (row < 384) & (col > -128) & (col < 384)

                    @pl.when(touches)
                    def _():
                        low_row, low_col = jnp.bitwise_and(row, 7), jnp.bitwise_and(col, 127)
                        brighten(row, col, turned(power, low_row, low_col))

                    return carry

                lax.fori_loop(0, around[i, 2, 0], other, 0)

    return kernel


def between_kernel(grid):
    def kernel(
        update, light, field,
        ext, cleared, inverse,
        ends_in, near_in, side, corner, side_in, corner_in, sems,
        halo_side, halo_corner, halo_side_in, halo_corner_in, more,
    ):
        place = Place(grid)
        greet(place)
        fold = Fold(place, update, ends_in, near_in, side, corner, side_in, corner_in, sems)
        halo = Halo(place, ext, halo_side, halo_corner, halo_side_in, halo_corner_in, more)
        fold.pack()
        greeted(place)
        fold.start()
        halo.clear()
        inverse[...] = 1.0 / (light[128:512, 128:512] + 1.0)
        for p in range(2):
            ext[p, 64:448, 0:384] = field[p, 64:448, 0:384] + update[p, 64:448, 0:384] * inverse[...]
        cleared[...] = jnp.zeros_like(cleared)
        for p in range(2):
            fold.finish(p, ext, 64, inverse)
            halo.pack(p)
            halo.start(p)
        halo.finish()
        fold.close()

    return kernel


def last_kernel(grid):
    def kernel(update, inverse, ext, out, ends_in, near_in, side, corner, side_in, corner_in, sems):
        place = Place(grid)
        greet(place)
        fold = Fold(place, update, ends_in, near_in, side, corner, side_in, corner_in, sems)
        fold.pack()
        greeted(place)
        fold.start()
        for p in range(2):
            out[p] = ext[p, 64:448, 0:384] + update[p, 64:448, 0:384] * inverse[...]
        for p in range(2):
            fold.finish(p, out, 0, inverse)
        fold.close()

    return kernel


def hold(x):
    return pltpu.with_memory_space_constraint(x, pltpu.MemorySpace.HBM)


def params(collective_id=None):
    if collective_id is None:
        return pltpu.CompilerParams(vmem_limit_bytes=LIMIT)
    return pltpu.CompilerParams(collective_id=collective_id, has_side_effects=True, vmem_limit_bytes=LIMIT)


def shards(grid, tables, object_field, probe, amplitudes, offsets, counts):
    f32, i32 = jnp.float32, jnp.int32
    shape = jax.ShapeDtypeStruct
    ext_shape, light_shape = shape((2, 512, 512), f32), shape((648, 640), f32)
    offsets = jnp.swapaxes(offsets, 2, 3)
    packs = [pltpu.VMEM((2, 2, 192, 128), f32), pltpu.VMEM((2, 2, 32, 128), f32)]
    folds = [pltpu.VMEM((2, 2, 64, 384), f32), pltpu.VMEM((2, 64, 128), f32)] + packs + packs
    sems = pltpu.SemaphoreType.DMA((2, 2, 9))
    ext, around, measured, tables, beams, power, update, light = pl.pallas_call(
        spread_kernel(grid),
        name="spread",
        out_shape=(
            ext_shape,
            shape((9, 8, 128), i32),
            shape(amplitudes.shape, f32),
            shape(tables.shape, tables.dtype),
            shape((12, 2, 128, 128), f32),
            shape((136, 128), f32),
            ext_shape,
            light_shape,
        ),
        in_specs=[HBM, HBM, SMEM, SMEM, HBM, HBM, HBM],
        out_specs=(VMEM,) * 8,
        scratch_shapes=[pltpu.VMEM((8, 128), i32), pltpu.VMEM((1, 1, 2, 12), i32), pltpu.VMEM((2, 136, 128), f32)]
        + packs
        + packs
        + [sems, pltpu.SemaphoreType.DMA((2, 8)), pltpu.SemaphoreType.DMA((6,))],
        compiler_params=params(0),
    )(hold(object_field), hold(offsets), counts, offsets, hold(amplitudes), hold(tables), hold(probe))
    update, light = pl.pallas_call(
        gradient_kernel(True),
        name="gradient_light",
        out_shape=(ext_shape, light_shape),
        in_specs=[SMEM] + [VMEM] * 7,
        out_specs=(VMEM,) * 2,
        input_output_aliases={5: 0, 7: 1},
        compiler_params=params(),
    )(around, ext, beams, measured, tables, update, power, light)
    ext, cleared, inverse = pl.pallas_call(
        between_kernel(grid),
        name="between",
        out_shape=(ext_shape, ext_shape, shape((384, 384), f32)),
        in_specs=[VMEM] * 3,
        out_specs=(VMEM,) * 3,
        scratch_shapes=folds + [sems] + packs + packs + [sems],
        compiler_params=params(1),
    )(update, light, ext)
    update = pl.pallas_call(
        gradient_kernel(False),
        name="gradient",
        out_shape=ext_shape,
        in_specs=[SMEM] + [VMEM] * 5,
        out_specs=VMEM,
        input_output_aliases={5: 0},
        compiler_params=params(),
    )(around, ext, beams, measured, tables, cleared)
    return pl.pallas_call(
        last_kernel(grid),
        name="last",
        out_shape=shape((2, 384, 384), f32),
        in_specs=[VMEM] * 3,
        out_specs=VMEM,
        scratch_shapes=folds + [sems],
        compiler_params=params(2),
    )(update, inverse, ext)


def solution(mesh):
    grid = (mesh.shape["row"], mesh.shape["col"])
    tables = dft_tables(128)
    placed = (
        P(None, "row", "col"),
        P(),
        P("row", "col", None, None, None),
        P("row", "col", None, None),
        P("row", "col"),
    )

    def body(*args):
        return shards(grid, jnp.asarray(tables), *args)

    return jax.shard_map(body, mesh=mesh, in_specs=placed, out_specs=P(None, "row", "col"), check_vma=False)
```

```python
import math

import jax
import jax.numpy as jnp
import numpy as np
from jax import lax
from jax.experimental import pallas as pl
from jax.experimental.pallas import tpu as pltpu
from jax.sharding import PartitionSpec as P

AROUND = ((-1, 0), (1, 0), (0, -1), (0, 1), (-1, -1), (-1, 1), (1, -1), (1, 1))
MESH = pl.DeviceIdType.MESH
VMEM = pl.BlockSpec(memory_space=pltpu.VMEM)
SMEM = pl.BlockSpec(memory_space=pltpu.SMEM)
HBM = pl.BlockSpec(memory_space=pltpu.MemorySpace.HBM)
LIMIT = 24 << 20
GROUP = 6
NEAR, FAR, LEFT, RIGHT, FAR_LEFT, FAR_RIGHT, LEFT_NEXT, RIGHT_NEXT, RELAY, EDGE_LEFT, EDGE_RIGHT = range(11)
DIAGONAL = (FAR_LEFT, FAR_RIGHT, EDGE_LEFT, EDGE_RIGHT)


def dft_tables(length):
    index = np.arange(length)
    angle = (np.outer(index, index) % length) * (2.0 * math.pi / length)
    cosine, sine = np.cos(angle) / math.sqrt(length), np.sin(angle) / math.sqrt(length)
    table = np.block([[cosine, -sine], [sine, cosine]])
    high = table.astype(jnp.bfloat16)
    low = (table - high.astype(np.float64)).astype(jnp.bfloat16)
    return np.stack([high, low, high.T, low.T])


def swap(x):
    return pltpu.roll(x, 64, x.ndim - 1)


def lower(rows):
    return lax.broadcasted_iota(jnp.int32, (rows, 128), 1) < 64


def pack(x, keep_low):
    rows = x.shape[0] // 2
    keep = lower(rows) if keep_low else ~lower(rows)
    return jnp.where(keep, x[:rows], swap(x[rows:]))


def unpack(x):
    return jnp.concatenate([x, swap(x)], axis=0)


def merge(a, b):
    keep = lower(a.shape[0])
    return jnp.concatenate([jnp.where(keep, a, b), jnp.where(keep, swap(a), swap(b))], axis=0)


class Place:
    def __init__(self, grid):
        self.row, self.col = lax.axis_index("row"), lax.axis_index("col")
        self.odd = lax.rem(self.row, 2)
        self.near_row = self.row + 1 - 2 * self.odd
        self.far_row = self.row - 1 + 2 * self.odd
        self.grid = grid
        far = (self.far_row >= 0) & (self.far_row < grid[0])
        left, right = self.col > 0, self.col < grid[1] - 1
        self.far, self.left, self.right = far, left, right
        ends = (far & jnp.logical_not(left), far & jnp.logical_not(right))
        both = (None, far, left, right, far & left, far & right, left, right, None) + ends
        self.sends = both
        order = (NEAR, FAR, RIGHT, LEFT, FAR_RIGHT, FAR_LEFT, RIGHT_NEXT, LEFT_NEXT, RELAY, EDGE_LEFT, EDGE_RIGHT)
        self.gets = tuple(both[i] for i in order)
        self.near_border = self.pick(320, 0)
        self.far_border = self.pick(0, 320)
        self.near_halo = self.pick(448, 0)
        self.far_halo = self.pick(0, 448)
        self.near_part = self.pick(256, 0)
        self.far_part = self.pick(0, 256)

    def pick(self, even, odd):
        return pl.multiple_of(even + self.odd * (odd - even), 64)

    def target(self, which):
        row = {NEAR: self.near_row, RELAY: self.near_row, FAR: self.far_row}
        row.update({which: self.far_row for which in DIAGONAL})
        side = {LEFT: -1, FAR_LEFT: -1, LEFT_NEXT: -1, RIGHT: 1, FAR_RIGHT: 1, RIGHT_NEXT: 1}
        return {"row": row.get(which, self.row), "col": self.col + side.get(which, 0)}


def when(condition, body):
    if condition is None:
        body()
    else:
        pl.when(condition)(body)


def greet(place):
    barrier = pltpu.get_barrier_semaphore()
    for which in (NEAR, FAR, LEFT, RIGHT, FAR_LEFT, FAR_RIGHT):
        when(
            place.sends[which],
            lambda: pl.semaphore_signal(
                barrier, inc=1, device_id=place.target(which), device_id_type=MESH
            ),
        )


def greeted(place):
    far, left, right = (jnp.where(x, 1, 0) for x in (place.far, place.left, place.right))
    pl.semaphore_wait(pltpu.get_barrier_semaphore(), 1 + far + (left + right) * (1 + far))


def greet_all(place):
    barrier = pltpu.get_barrier_semaphore()
    count = 0
    for d in AROUND:
        count += jnp.where(beside(place, d), 1, 0)

        @pl.when(beside(place, d))
        def _():
            pl.semaphore_signal(
                barrier, inc=1, device_id={"row": place.row + d[0], "col": place.col + d[1]}, device_id_type=MESH
            )

    return count


def beside(place, d):
    row, col = place.row + d[0], place.col + d[1]
    return (row >= 0) & (row < place.grid[0]) & (col >= 0) & (col < place.grid[1])


def remote(place, which, src, dst, sems, p):
    return pltpu.make_async_remote_copy(
        src, dst, sems.at[0, p, which], sems.at[1, p, which], device_id=place.target(which), device_id_type=MESH
    )


def start(place, copies, *which):
    for i in which:
        when(place.sends[i], copies[i].start)


def wait_recv(place, copies, *which):
    for i in which:
        when(place.gets[i], copies[i].wait_recv)


def wait_send(place, copies):
    for i, copy in enumerate(copies):
        when(place.sends[i], copy.wait_send)


def strips(far, far_in, side, side_in, corner, corner_in, p):
    return {
        FAR: (far.at[p], far_in.at[p]),
        FAR_LEFT: (corner.at[0, p], corner_in.at[0, p]),
        FAR_RIGHT: (corner.at[1, p], corner_in.at[1, p]),
        EDGE_LEFT: (corner.at[0, p], corner_in.at[1, p]),
        EDGE_RIGHT: (corner.at[1, p], corner_in.at[0, p]),
        LEFT: (side.at[0, p, 0:128], side_in.at[0, p, 0:128]),
        RIGHT: (side.at[1, p, 0:128], side_in.at[1, p, 0:128]),
        LEFT_NEXT: (side.at[0, p, 128:192], side_in.at[0, p, 128:192]),
        RIGHT_NEXT: (side.at[1, p, 128:192], side_in.at[1, p, 128:192]),
    }


def at_rows(first, rows):
    return pl.ds(pl.multiple_of(first, 64), rows)


class Halo:
    def __init__(self, place, ext, far, side, corner, far_in, side_in, corner_in, sems):
        self.place, self.ext, self.far, self.far_in = place, ext, far, far_in
        self.side, self.corner, self.side_in, self.corner_in = side, corner, side_in, corner_in
        near, target = at_rows(place.near_border + 64, 64), at_rows(place.far_halo, 64)
        self.copies = []
        for p in range(2):
            ends = strips(far, far_in, side, side_in, corner, corner_in, p)
            ends[NEAR] = (ext.at[p, near, 0:384], ext.at[p, target, 0:384])
            ends[RELAY] = (ext.at[p, near, 384:512], ext.at[p, target, 384:512])
            self.copies.append([remote(place, i, *ends[i], sems, p) for i in range(11)])

    def clear(self):
        place = self.place

        @pl.when(jnp.logical_not(place.far))
        def _():
            self.far_in[...] = jnp.zeros((2, 64, 256), jnp.float32)
            self.corner_in[...] = jnp.zeros((2, 2, 64, 128), jnp.float32)

        for k, side in enumerate((place.right, place.left)):

            @pl.when(jnp.logical_not(side))
            def _():
                self.side_in[k] = jnp.zeros((2, 192, 128), jnp.float32)

    def pack(self, p):
        place, ext = self.place, self.ext
        for k, lane in enumerate((0, 256)):
            for i, first in enumerate((place.near_part, place.far_part, 128)):
                self.side[k, p, 64 * i : 64 * i + 64] = pack(ext[p, at_rows(first + 64, 128), lane : lane + 128], k == 0)
        rows = at_rows(place.far_border + 64, 64)
        self.far[p, :, 0:128] = ext[p, rows, 128:256]
        self.far[p, :, 128:256] = jnp.where(lower(64), ext[p, rows, 256:384], ext[p, rows, 0:128])

    def start(self, p):
        start(self.place, self.copies[p], LEFT, RIGHT, FAR, NEAR, LEFT_NEXT, RIGHT_NEXT)

    def finish(self):
        place, ext, low = self.place, self.ext, lower(64)
        for p in range(2):
            wait_recv(place, self.copies[p], LEFT, RIGHT)
            for i, first in enumerate((place.near_part, place.far_part)):
                parts = [self.side_in[k, p, 64 * i : 64 * i + 64] for k in range(2)]
                ext[p, at_rows(first + 64, 128), 384:512] = merge(*parts)
            start(place, self.copies[p], RELAY)
            rows = at_rows(place.far_border + 64, 64)
            self.corner[0, p] = jnp.where(low, ext[p, rows, 0:128], ext[p, rows, 384:512])
            self.corner[1, p] = jnp.where(low, ext[p, rows, 384:512], ext[p, rows, 256:384])
            start(place, self.copies[p], *DIAGONAL)
        for p in range(2):
            wait_recv(place, self.copies[p], LEFT_NEXT, RIGHT_NEXT)
            ext[p, 192:320, 384:512] = merge(self.side_in[0, p, 128:192], self.side_in[1, p, 128:192])
            wait_recv(place, self.copies[p], FAR, *DIAGONAL)
            rows = at_rows(place.far_halo, 64)
            right, left = self.corner_in[0, p], self.corner_in[1, p]
            mixed = self.far_in[p, :, 128:256]
            ext[p, rows, 0:128] = jnp.where(low, left, mixed)
            ext[p, rows, 128:256] = self.far_in[p, :, 0:128]
            ext[p, rows, 256:384] = jnp.where(low, mixed, right)
            ext[p, rows, 384:512] = jnp.where(low, right, left)
        for p in range(2):
            wait_recv(place, self.copies[p], NEAR, RELAY)
            wait_send(place, self.copies[p])


class Fold:
    def __init__(self, place, update, near_in, relay_in, far, side, corner, far_in, side_in, corner_in, sems):
        self.place, self.update, self.near_in, self.relay_in = place, update, near_in, relay_in
        self.far, self.far_in = far, far_in
        self.side, self.corner, self.side_in, self.corner_in = side, corner, side_in, corner_in
        near = at_rows(place.near_halo, 64)
        self.copies = []
        for p in range(2):
            ends = strips(far, far_in, side, side_in, corner, corner_in, p)
            ends[NEAR] = (update.at[p, near, 0:384], near_in.at[p])
            ends[RELAY] = (update.at[p, near, 384:512], relay_in.at[p])
            self.copies.append([remote(place, i, *ends[i], sems, p) for i in range(11)])

    def pack(self):
        place, update, low = self.place, self.update, lower(64)

        @pl.when(jnp.logical_not(place.far))
        def _():
            self.corner_in[...] = jnp.zeros((2, 2, 64, 128), jnp.float32)

        rows = at_rows(place.far_halo, 64)
        for p in range(2):
            tiles = [update[p, rows, 128 * t : 128 * t + 128] for t in range(4)]
            self.corner[0, p] = jnp.where(low, tiles[0], tiles[3])
            self.corner[1, p] = jnp.where(low, tiles[3], tiles[2])
            self.far[p, :, 0:128] = tiles[1]
            self.far[p, :, 128:256] = jnp.where(low, tiles[2], tiles[0])
            for k in range(2):
                self.side[k, p, 128:192] = pack(update[p, 192:320, 384:512], k == 1)

    def start(self):
        place, update = self.place, self.update
        odd = place.odd.astype(jnp.float32)
        for p in range(2):
            start(place, self.copies[p], *DIAGONAL, RELAY)
        start(place, self.copies[0], FAR, LEFT_NEXT, RIGHT_NEXT, NEAR)
        start(place, self.copies[1], FAR)
        for p in range(2):
            wait_recv(place, self.copies[p], RELAY, *DIAGONAL)
            extra = (self.relay_in[p], jnp.where(lower(64), self.corner_in[0, p], self.corner_in[1, p]))
            for i, first in enumerate((place.near_part, place.far_part)):
                part = update[p, at_rows(first + 64, 128), 384:512]
                here = odd if i == 0 else 1.0 - odd
                part = jnp.concatenate([part[:64] + extra[i] * here, part[64:] + extra[i] * (1.0 - here)], axis=0)
                for k in range(2):
                    self.side[k, p, 64 * i : 64 * i + 64] = pack(part, k == 1)
            start(place, self.copies[p], LEFT, RIGHT)
            if p == 0:
                start(place, self.copies[1], LEFT_NEXT, RIGHT_NEXT, NEAR)

    def finish(self, p, dest, base, inverse):
        place = self.place

        def add(first, lane, value):
            lanes, rows = pl.ds(lane, value.shape[1]), value.shape[0]
            dest[p, at_rows(first + base, rows), lanes] += value * inverse[at_rows(first, rows), lanes]

        def lowest(value):
            return jnp.where(lower(value.shape[0]), value, 0.0)

        def highest(value):
            return jnp.where(lower(value.shape[0]), 0.0, value)

        wait_recv(place, self.copies[p], NEAR)
        add(place.near_border, 0, self.near_in[p])

        @pl.when(place.far)
        def _():
            self.copies[p][FAR].wait_recv()
            mixed = self.far_in[p, :, 128:256]
            add(place.far_border, 0, jnp.where(lower(64), self.corner_in[1, p], mixed))
            add(place.far_border, 128, self.far_in[p, :, 0:128])
            add(place.far_border, 256, jnp.where(lower(64), mixed, self.corner_in[0, p]))

        for k, (here, lane, keep) in enumerate(((place.right, 256, highest), (place.left, 0, lowest))):

            @pl.when(here)
            def _():
                self.copies[p][LEFT_NEXT + k].wait_recv()
                add(128, lane, keep(unpack(self.side_in[k, p, 128:192])))
                self.copies[p][LEFT + k].wait_recv()
                add(place.near_part, lane, keep(unpack(self.side_in[k, p, 0:64])))
                add(place.far_part, lane, keep(unpack(self.side_in[k, p, 64:128])))

    def close(self):
        for p in range(2):
            wait_send(self.place, self.copies[p])


def spread_kernel(grid):
    def kernel(
        field, offsets, counts, places, measured, tables, probe,
        ext, around, measured_here, tables_here, beams, power, update, light,
        mine, offsets_here, tall, far, side, corner, far_in, side_in, corner_in, sems, notes, local,
    ):
        place = Place(grid)
        peers = greet_all(place)
        pulls = [pltpu.make_async_copy(offsets, offsets_here, local.at[0])]
        pulls += [pltpu.make_async_copy(field.at[p], ext.at[p, 64:448, 0:384], local.at[1 + p]) for p in range(2)]
        later = [
            pltpu.make_async_copy(measured, measured_here, local.at[3]),
            pltpu.make_async_copy(tables, tables_here, local.at[4]),
        ]
        pulls.append(pltpu.make_async_copy(probe, tall.at[:, 8:136], local.at[5]))
        for pull in pulls:
            pull.start()
        halo = Halo(place, ext, far, side, corner, far_in, side_in, corner_in, sems)
        halo.clear()
        for i, d in enumerate(AROUND):

            @pl.when(jnp.logical_not(beside(place, d)))
            def _():
                around[i] = jnp.zeros((8, 128), jnp.int32)

        pulls[0].wait()
        mine[0:2, 0:12] = offsets_here[0, 0]
        mine[2:3, 0:1] = jnp.full((1, 1), counts[0, 0], jnp.int32)
        around[8] = mine[...]
        letters = []
        for i, d in enumerate(AROUND):
            letter = pltpu.make_async_remote_copy(
                mine,
                around.at[AROUND.index((-d[0], -d[1]))],
                notes.at[0, i],
                notes.at[1, i],
                device_id={"row": place.row + d[0], "col": place.col + d[1]},
                device_id_type=MESH,
            )
            letters.append(letter)
        pulls[1].wait()
        halo.pack(0)
        pl.semaphore_wait(pltpu.get_barrier_semaphore(), peers)
        for i, d in enumerate(AROUND):
            pl.when(beside(place, d))(letters[i].start)
        halo.start(0)
        pulls[2].wait()
        halo.pack(1)
        halo.start(1)
        for pull in later:
            pull.start()
        update[...] = jnp.zeros_like(update)
        light[...] = jnp.zeros_like(light)
        pulls[3].wait()
        for p in range(2):
            tall[p, 0:8] = tall[p, 128:136]
        power[...] = tall[0] * tall[0] + tall[1] * tall[1]

        def turn(slot, carry):
            live = (slot < counts[0, 0]).astype(jnp.float32)
            low_row, low_col = places[0, 0, 0, slot] & 7, places[0, 0, 1, slot] & 127
            for p in range(2):
                beams[slot, p] = pltpu.roll(tall[p, pl.ds(8 - low_row, 128), :], low_col, 1) * live
            return carry

        lax.fori_loop(0, 12, turn, 0)
        halo.finish()
        for i, d in enumerate(AROUND):
            pl.when(beside(place, d))(letters[i].wait_send)
            pl.when(beside(place, (-d[0], -d[1])))(letters[i].wait_recv)
        for pull in later:
            pull.wait()

    return kernel


def split(x):
    high = x.astype(jnp.bfloat16)
    return high, (x - high.astype(jnp.float32)).astype(jnp.bfloat16)


def dot(a, b):
    return jnp.dot(a, b, preferred_element_type=jnp.float32)


def right_mul(x, high, low):
    xh, xl = split(x)
    return dot(xh, high) + dot(xl, high) + dot(xh, low)


def left_mul(high, low, x):
    xh, xl = split(x)
    return dot(high, xh) + dot(high, xl) + dot(low, xh)


def cross(x):
    return jnp.concatenate(
        [
            jnp.concatenate([x[:128, :128], x[128:, :128]], axis=1),
            jnp.concatenate([x[:128, 128:], x[128:, 128:]], axis=1),
        ],
        axis=0,
    )


def gradient_kernel(with_light):
    def kernel(*refs):
        if with_light:
            around, ext, beams, measured, tables, _, power, _, update, light = refs
        else:
            around, ext, beams, measured, tables, _, update = refs
        count = around[8, 2, 0]
        lane = lax.broadcasted_iota(jnp.int32, (128, 128), 1)
        sub = lax.broadcasted_iota(jnp.int32, (8, 128), 0)

        def turned(source, shift_rows, shift_lanes):
            return pltpu.roll(source[pl.ds(8 - shift_rows, 128), :], shift_lanes, 1)

        def scatter(dest, first, lanes, shift_rows, shift_lanes, value):
            head = jnp.where(sub >= shift_rows, value[:8], 0.0)
            main = jnp.concatenate([head, value[8:]], axis=0)
            tail = jnp.where(sub < shift_rows, value[:8], 0.0)
            for which, at in enumerate(lanes):
                keep = lane >= shift_lanes if which == 0 else lane < shift_lanes
                dest[pl.ds(first, 128), at] += jnp.where(keep, main, 0.0)
                dest[pl.ds(first + 128, 8), at] += jnp.where(keep[:8], tail, 0.0)

        def tiles_of(col, base, wrap):
            tile = lax.shift_right_arithmetic(col, 7) + base
            first = lax.rem(tile + wrap, wrap)
            second = lax.rem(tile + wrap + 1, wrap)
            return [pl.ds(pl.multiple_of(t * 128, 128), 128) for t in (first, second)]

        def brighten(row, col, value):
            low_row, low_col = jnp.bitwise_and(row, 7), jnp.bitwise_and(col, 127)
            first = pl.multiple_of(row - low_row + 128, 8)
            scatter(light, first, tiles_of(col, 1, 5), low_row, low_col, value)

        def gather(slot):
            row, col = around[8, 0, slot], around[8, 1, slot]
            low_row, low_col = jnp.bitwise_and(row, 7), jnp.bitwise_and(col, 127)
            first = pl.multiple_of(row - low_row + 64, 8)
            lanes = tiles_of(col, 0, 4)
            beam = [beams[slot, p] for p in range(2)]
            window = []
            for p in range(2):
                main = jnp.where(
                    lane >= low_col, ext[p, pl.ds(first, 128), lanes[0]], ext[p, pl.ds(first, 128), lanes[1]]
                )
                tail = jnp.where(
                    lane[:8] >= low_col,
                    ext[p, pl.ds(first + 128, 8), lanes[0]],
                    ext[p, pl.ds(first + 128, 8), lanes[1]],
                )
                window.append(jnp.concatenate([jnp.where(sub >= low_row, main[:8], tail), main[8:]], axis=0))
            real = beam[0] * window[0] - beam[1] * window[1]
            imag = beam[0] * window[1] + beam[1] * window[0]
            return jnp.concatenate([real, imag], axis=1), (slot, first, lanes, low_row, low_col, row, col)

        def put(back, at):
            slot, first, lanes, low_row, low_col, row, col = at
            beam = [beams[slot, p] for p in range(2)]
            real, imag = back[:, :128], back[:, 128:]
            scatter(update.at[0], first, lanes, low_row, low_col, beam[0] * real + beam[1] * imag)
            scatter(update.at[1], first, lanes, low_row, low_col, beam[0] * imag - beam[1] * real)
            if with_light:
                brighten(row, col, beam[0] * beam[0] + beam[1] * beam[1])

        def some(step, carry):
            slots = [step * GROUP + k for k in range(GROUP)]
            pairs = [(k, k + 1) for k in range(0, GROUP, 2)]
            gathered = [gather(slot) for slot in slots]
            waves = [jnp.concatenate([gathered[a][0], gathered[b][0]], axis=0) for a, b in pairs]
            half = [cross(right_mul(wave, tables[0], tables[1])) for wave in waves]
            far = [left_mul(tables[2], tables[3], x) for x in half]
            change = []
            for x, (a, b) in zip(far, pairs):
                real, imag = x[:128], x[128:]
                known = jnp.concatenate([measured[0, 0, slots[a]], measured[0, 0, slots[b]]], axis=1)
                ratio = known * lax.rsqrt(real * real + imag * imag + 0.25) - 1.0
                change.append(jnp.concatenate([real * ratio, imag * ratio], axis=0))
            half = [cross(left_mul(tables[0], tables[1], x)) for x in change]
            back = [right_mul(x, tables[2], tables[3]) for x in half]
            for x, (a, b) in zip(back, pairs):
                put(x[:128], gathered[a][1])
                put(x[128:], gathered[b][1])
            return carry

        lax.fori_loop(0, (count + GROUP - 1) // GROUP, some, 0)
        if with_light:
            for i, d in enumerate(AROUND):

                def other(slot, carry):
                    row = around[i, 0, slot] + d[0] * 384
                    col = around[i, 1, slot] + d[1] * 384
                    touches = (row > -128) & (row < 384) & (col > -128) & (col < 384)

                    @pl.when(touches)
                    def _():
                        low_row, low_col = jnp.bitwise_and(row, 7), jnp.bitwise_and(col, 127)
                        brighten(row, col, turned(power, low_row, low_col))

                    return carry

                lax.fori_loop(0, around[i, 2, 0], other, 0)

    return kernel


def between_kernel(grid):
    def kernel(
        update, light, field,
        ext, cleared, inverse,
        near_in, relay_in, far, side, corner, far_in, side_in, corner_in, sems,
        halo_far, halo_side, halo_corner, halo_far_in, halo_side_in, halo_corner_in, more,
    ):
        place = Place(grid)
        greet(place)
        fold = Fold(place, update, near_in, relay_in, far, side, corner, far_in, side_in, corner_in, sems)
        halo = Halo(place, ext, halo_far, halo_side, halo_corner, halo_far_in, halo_side_in, halo_corner_in, more)
        fold.pack()
        greeted(place)
        fold.start()
        halo.clear()
        inverse[...] = 1.0 / (light[128:512, 128:512] + 1.0)
        for p in range(2):
            ext[p, 64:448, 0:384] = field[p, 64:448, 0:384] + update[p, 64:448, 0:384] * inverse[...]
        cleared[...] = jnp.zeros_like(cleared)
        for p in range(2):
            fold.finish(p, ext, 64, inverse)
            halo.pack(p)
            halo.start(p)
        halo.finish()
        fold.close()

    return kernel


def last_kernel(grid):
    def kernel(update, inverse, ext, out, near_in, relay_in, far, side, corner, far_in, side_in, corner_in, sems):
        place = Place(grid)
        greet(place)
        fold = Fold(place, update, near_in, relay_in, far, side, corner, far_in, side_in, corner_in, sems)
        fold.pack()
        greeted(place)
        fold.start()
        for p in range(2):
            out[p] = ext[p, 64:448, 0:384] + update[p, 64:448, 0:384] * inverse[...]
        for p in range(2):
            fold.finish(p, out, 0, inverse)
        fold.close()

    return kernel


def hold(x):
    return pltpu.with_memory_space_constraint(x, pltpu.MemorySpace.HBM)


def params(collective_id=None):
    if collective_id is None:
        return pltpu.CompilerParams(vmem_limit_bytes=LIMIT)
    return pltpu.CompilerParams(collective_id=collective_id, has_side_effects=True, vmem_limit_bytes=LIMIT)


def shards(grid, tables, object_field, probe, amplitudes, offsets, counts):
    f32, i32 = jnp.float32, jnp.int32
    shape = jax.ShapeDtypeStruct
    ext_shape, light_shape = shape((2, 512, 512), f32), shape((648, 640), f32)
    offsets = jnp.swapaxes(offsets, 2, 3)
    packs = [pltpu.VMEM((2, 64, 256), f32), pltpu.VMEM((2, 2, 192, 128), f32), pltpu.VMEM((2, 2, 64, 128), f32)]
    folds = [pltpu.VMEM((2, 64, 384), f32), pltpu.VMEM((2, 64, 128), f32)] + packs + packs
    sems = pltpu.SemaphoreType.DMA((2, 2, 11))
    ext, around, measured, tables, beams, power, update, light = pl.pallas_call(
        spread_kernel(grid),
        name="spread",
        out_shape=(
            ext_shape,
            shape((9, 8, 128), i32),
            shape(amplitudes.shape, f32),
            shape(tables.shape, tables.dtype),
            shape((12, 2, 128, 128), f32),
            shape((136, 128), f32),
            ext_shape,
            light_shape,
        ),
        in_specs=[HBM, HBM, SMEM, SMEM, HBM, HBM, HBM],
        out_specs=(VMEM,) * 8,
        scratch_shapes=[pltpu.VMEM((8, 128), i32), pltpu.VMEM((1, 1, 2, 12), i32), pltpu.VMEM((2, 136, 128), f32)]
        + packs
        + packs
        + [sems, pltpu.SemaphoreType.DMA((2, 8)), pltpu.SemaphoreType.DMA((6,))],
        compiler_params=params(0),
    )(hold(object_field), hold(offsets), counts, offsets, hold(amplitudes), hold(tables), hold(probe))
    update, light = pl.pallas_call(
        gradient_kernel(True),
        name="gradient_light",
        out_shape=(ext_shape, light_shape),
        in_specs=[SMEM] + [VMEM] * 7,
        out_specs=(VMEM,) * 2,
        input_output_aliases={5: 0, 7: 1},
        compiler_params=params(),
    )(around, ext, beams, measured, tables, update, power, light)
    ext, cleared, inverse = pl.pallas_call(
        between_kernel(grid),
        name="between",
        out_shape=(ext_shape, ext_shape, shape((384, 384), f32)),
        in_specs=[VMEM] * 3,
        out_specs=(VMEM,) * 3,
        scratch_shapes=folds + [sems] + packs + packs + [sems],
        compiler_params=params(1),
    )(update, light, ext)
    update = pl.pallas_call(
        gradient_kernel(False),
        name="gradient",
        out_shape=ext_shape,
        in_specs=[SMEM] + [VMEM] * 5,
        out_specs=VMEM,
        input_output_aliases={5: 0},
        compiler_params=params(),
    )(around, ext, beams, measured, tables, cleared)
    return pl.pallas_call(
        last_kernel(grid),
        name="last",
        out_shape=shape((2, 384, 384), f32),
        in_specs=[VMEM] * 3,
        out_specs=VMEM,
        scratch_shapes=folds + [sems],
        compiler_params=params(2),
    )(update, inverse, ext)


def solution(mesh):
    grid = (mesh.shape["row"], mesh.shape["col"])
    tables = dft_tables(128)
    placed = (
        P(None, "row", "col"),
        P(),
        P("row", "col", None, None, None),
        P("row", "col", None, None),
        P("row", "col"),
    )

    def body(*args):
        return shards(grid, jnp.asarray(tables), *args)

    return jax.shard_map(body, mesh=mesh, in_specs=placed, out_specs=P(None, "row", "col"), check_vma=False)
```

```python
import math

import jax
import jax.numpy as jnp
import numpy as np
from jax import lax
from jax.experimental import pallas as pl
from jax.experimental.pallas import tpu as pltpu
from jax.sharding import PartitionSpec as P

AROUND = ((-1, 0), (1, 0), (0, -1), (0, 1), (-1, -1), (-1, 1), (1, -1), (1, 1))
MESH = pl.DeviceIdType.MESH
VMEM = pl.BlockSpec(memory_space=pltpu.VMEM)
SMEM = pl.BlockSpec(memory_space=pltpu.SMEM)
HBM = pl.BlockSpec(memory_space=pltpu.MemorySpace.HBM)
LIMIT = 24 << 20
GROUP = 6
NEAR, FAR, LEFT, RIGHT, FAR_LEFT, FAR_RIGHT, LEFT_NEXT, RIGHT_NEXT, RELAY, EDGE_LEFT, EDGE_RIGHT = range(11)
DIAGONAL = (FAR_LEFT, FAR_RIGHT, EDGE_LEFT, EDGE_RIGHT)


def dft_tables(length):
    index = np.arange(length)
    angle = (np.outer(index, index) % length) * (2.0 * math.pi / length)
    cosine, sine = np.cos(angle) / math.sqrt(length), np.sin(angle) / math.sqrt(length)
    table = np.block([[cosine, -sine], [sine, cosine]])
    high = table.astype(jnp.bfloat16)
    low = (table - high.astype(np.float64)).astype(jnp.bfloat16)
    return np.stack([high, low, high.T, low.T])


def swap(x):
    return pltpu.roll(x, 64, x.ndim - 1)


def lower(rows):
    return lax.broadcasted_iota(jnp.int32, (rows, 128), 1) < 64


def pack(x, keep_low):
    rows = x.shape[0] // 2
    keep = lower(rows) if keep_low else ~lower(rows)
    return jnp.where(keep, x[:rows], swap(x[rows:]))


def unpack(x):
    return jnp.concatenate([x, swap(x)], axis=0)


def merge(a, b):
    keep = lower(a.shape[0])
    return jnp.concatenate([jnp.where(keep, a, b), jnp.where(keep, swap(a), swap(b))], axis=0)


class Place:
    def __init__(self, grid):
        self.row, self.col = lax.axis_index("row"), lax.axis_index("col")
        self.odd = lax.rem(self.row, 2)
        self.near_row = self.row + 1 - 2 * self.odd
        self.far_row = self.row - 1 + 2 * self.odd
        self.grid = grid
        far = (self.far_row >= 0) & (self.far_row < grid[0])
        left, right = self.col > 0, self.col < grid[1] - 1
        self.far, self.left, self.right = far, left, right
        ends = (far & jnp.logical_not(left), far & jnp.logical_not(right))
        both = (None, far, left, right, far & left, far & right, left, right, None) + ends
        self.sends = both
        order = (NEAR, FAR, RIGHT, LEFT, FAR_RIGHT, FAR_LEFT, RIGHT_NEXT, LEFT_NEXT, RELAY, EDGE_LEFT, EDGE_RIGHT)
        self.gets = tuple(both[i] for i in order)
        self.near_border = self.pick(320, 0)
        self.far_border = self.pick(0, 320)
        self.near_halo = self.pick(448, 0)
        self.far_halo = self.pick(0, 448)
        self.near_part = self.pick(256, 0)
        self.far_part = self.pick(0, 256)

    def pick(self, even, odd):
        return pl.multiple_of(even + self.odd * (odd - even), 64)

    def target(self, which):
        row = {NEAR: self.near_row, RELAY: self.near_row, FAR: self.far_row}
        row.update({which: self.far_row for which in DIAGONAL})
        side = {LEFT: -1, FAR_LEFT: -1, LEFT_NEXT: -1, RIGHT: 1, FAR_RIGHT: 1, RIGHT_NEXT: 1}
        return {"row": row.get(which, self.row), "col": self.col + side.get(which, 0)}


def when(condition, body):
    if condition is None:
        body()
    else:
        pl.when(condition)(body)


def greet(place):
    barrier = pltpu.get_barrier_semaphore()
    for which in (NEAR, FAR, LEFT, RIGHT, FAR_LEFT, FAR_RIGHT):
        when(
            place.sends[which],
            lambda: pl.semaphore_signal(
                barrier, inc=1, device_id=place.target(which), device_id_type=MESH
            ),
        )


def greeted(place):
    far, left, right = (jnp.where(x, 1, 0) for x in (place.far, place.left, place.right))
    pl.semaphore_wait(pltpu.get_barrier_semaphore(), 1 + far + (left + right) * (1 + far))


def greet_all(place):
    barrier = pltpu.get_barrier_semaphore()
    count = 0
    for d in AROUND:
        count += jnp.where(beside(place, d), 1, 0)

        @pl.when(beside(place, d))
        def _():
            pl.semaphore_signal(
                barrier, inc=1, device_id={"row": place.row + d[0], "col": place.col + d[1]}, device_id_type=MESH
            )

    return count


def beside(place, d):
    row, col = place.row + d[0], place.col + d[1]
    return (row >= 0) & (row < place.grid[0]) & (col >= 0) & (col < place.grid[1])


def remote(place, which, src, dst, sems, p):
    return pltpu.make_async_remote_copy(
        src, dst, sems.at[0, p, which], sems.at[1, p, which], device_id=place.target(which), device_id_type=MESH
    )


def start(place, copies, *which):
    for i in which:
        when(place.sends[i], copies[i].start)


def wait_recv(place, copies, *which):
    for i in which:
        when(place.gets[i], copies[i].wait_recv)


def wait_send(place, copies):
    for i, copy in enumerate(copies):
        when(place.sends[i], copy.wait_send)


def strips(far, far_in, side, side_in, corner, corner_in, p):
    return {
        FAR: (far.at[p], far_in.at[p]),
        FAR_LEFT: (corner.at[0, p], corner_in.at[0, p]),
        FAR_RIGHT: (corner.at[1, p], corner_in.at[1, p]),
        EDGE_LEFT: (corner.at[0, p], corner_in.at[1, p]),
        EDGE_RIGHT: (corner.at[1, p], corner_in.at[0, p]),
        LEFT: (side.at[0, p, 0:128], side_in.at[0, p, 0:128]),
        RIGHT: (side.at[1, p, 0:128], side_in.at[1, p, 0:128]),
        LEFT_NEXT: (side.at[0, p, 128:192], side_in.at[0, p, 128:192]),
        RIGHT_NEXT: (side.at[1, p, 128:192], side_in.at[1, p, 128:192]),
    }


def at_rows(first, rows):
    return pl.ds(pl.multiple_of(first, 64), rows)


class Halo:
    def __init__(self, place, ext, far, side, corner, far_in, side_in, corner_in, sems):
        self.place, self.ext, self.far, self.far_in = place, ext, far, far_in
        self.side, self.corner, self.side_in, self.corner_in = side, corner, side_in, corner_in
        near, target = at_rows(place.near_border + 64, 64), at_rows(place.far_halo, 64)
        self.copies = []
        for p in range(2):
            ends = strips(far, far_in, side, side_in, corner, corner_in, p)
            ends[NEAR] = (ext.at[p, near, 0:384], ext.at[p, target, 0:384])
            ends[RELAY] = (ext.at[p, near, 384:512], ext.at[p, target, 384:512])
            self.copies.append([remote(place, i, *ends[i], sems, p) for i in range(11)])

    def clear(self):
        place = self.place

        @pl.when(jnp.logical_not(place.far))
        def _():
            self.far_in[...] = jnp.zeros((2, 64, 256), jnp.float32)
            self.corner_in[...] = jnp.zeros((2, 2, 64, 128), jnp.float32)

        for k, side in enumerate((place.right, place.left)):

            @pl.when(jnp.logical_not(side))
            def _():
                self.side_in[k] = jnp.zeros((2, 192, 128), jnp.float32)

    def pack(self, p):
        place, ext = self.place, self.ext
        for k, lane in enumerate((0, 256)):
            for i, first in enumerate((place.near_part, place.far_part, 128)):
                self.side[k, p, 64 * i : 64 * i + 64] = pack(ext[p, at_rows(first + 64, 128), lane : lane + 128], k == 0)
        rows = at_rows(place.far_border + 64, 64)
        self.far[p, :, 0:128] = ext[p, rows, 128:256]
        self.far[p, :, 128:256] = jnp.where(lower(64), ext[p, rows, 256:384], ext[p, rows, 0:128])

    def start(self, p):
        start(self.place, self.copies[p], LEFT, RIGHT, FAR)

    def start_rest(self):
        for p in range(2):
            start(self.place, self.copies[p], LEFT_NEXT, RIGHT_NEXT, NEAR)

    def finish(self):
        place, ext, low = self.place, self.ext, lower(64)
        for p in range(2):
            wait_recv(place, self.copies[p], LEFT, RIGHT)
            for i, first in enumerate((place.near_part, place.far_part)):
                parts = [self.side_in[k, p, 64 * i : 64 * i + 64] for k in range(2)]
                ext[p, at_rows(first + 64, 128), 384:512] = merge(*parts)
            start(place, self.copies[p], RELAY)
            rows = at_rows(place.far_border + 64, 64)
            self.corner[0, p] = jnp.where(low, ext[p, rows, 0:128], ext[p, rows, 384:512])
            self.corner[1, p] = jnp.where(low, ext[p, rows, 384:512], ext[p, rows, 256:384])
            start(place, self.copies[p], *DIAGONAL)
        for p in range(2):
            wait_recv(place, self.copies[p], LEFT_NEXT, RIGHT_NEXT)
            ext[p, 192:320, 384:512] = merge(self.side_in[0, p, 128:192], self.side_in[1, p, 128:192])
            wait_recv(place, self.copies[p], FAR, *DIAGONAL)
            rows = at_rows(place.far_halo, 64)
            right, left = self.corner_in[0, p], self.corner_in[1, p]
            mixed = self.far_in[p, :, 128:256]
            ext[p, rows, 0:128] = jnp.where(low, left, mixed)
            ext[p, rows, 128:256] = self.far_in[p, :, 0:128]
            ext[p, rows, 256:384] = jnp.where(low, mixed, right)
            ext[p, rows, 384:512] = jnp.where(low, right, left)
        for p in range(2):
            wait_recv(place, self.copies[p], NEAR, RELAY)
            wait_send(place, self.copies[p])


class Fold:
    def __init__(self, place, update, near_in, relay_in, far, side, corner, far_in, side_in, corner_in, sems):
        self.place, self.update, self.near_in, self.relay_in = place, update, near_in, relay_in
        self.far, self.far_in = far, far_in
        self.side, self.corner, self.side_in, self.corner_in = side, corner, side_in, corner_in
        near = at_rows(place.near_halo, 64)
        self.copies = []
        for p in range(2):
            ends = strips(far, far_in, side, side_in, corner, corner_in, p)
            ends[NEAR] = (update.at[p, near, 0:384], near_in.at[p])
            ends[RELAY] = (update.at[p, near, 384:512], relay_in.at[p])
            self.copies.append([remote(place, i, *ends[i], sems, p) for i in range(11)])

    def pack(self):
        place, update, low = self.place, self.update, lower(64)

        @pl.when(jnp.logical_not(place.far))
        def _():
            self.corner_in[...] = jnp.zeros((2, 2, 64, 128), jnp.float32)

        rows = at_rows(place.far_halo, 64)
        for p in range(2):
            tiles = [update[p, rows, 128 * t : 128 * t + 128] for t in range(4)]
            self.corner[0, p] = jnp.where(low, tiles[0], tiles[3])
            self.corner[1, p] = jnp.where(low, tiles[3], tiles[2])
            self.far[p, :, 0:128] = tiles[1]
            self.far[p, :, 128:256] = jnp.where(low, tiles[2], tiles[0])
            for k in range(2):
                self.side[k, p, 128:192] = pack(update[p, 192:320, 384:512], k == 1)

    def start(self):
        place, update = self.place, self.update
        odd = place.odd.astype(jnp.float32)
        for p in range(2):
            start(place, self.copies[p], *DIAGONAL, RELAY, FAR, LEFT_NEXT, RIGHT_NEXT)
        for p in range(2):
            start(place, self.copies[p], NEAR)
        for p in range(2):
            wait_recv(place, self.copies[p], RELAY, *DIAGONAL)
            extra = (self.relay_in[p], jnp.where(lower(64), self.corner_in[0, p], self.corner_in[1, p]))
            for i, first in enumerate((place.near_part, place.far_part)):
                part = update[p, at_rows(first + 64, 128), 384:512]
                here = odd if i == 0 else 1.0 - odd
                part = jnp.concatenate([part[:64] + extra[i] * here, part[64:] + extra[i] * (1.0 - here)], axis=0)
                for k in range(2):
                    self.side[k, p, 64 * i : 64 * i + 64] = pack(part, k == 1)
            start(place, self.copies[p], LEFT, RIGHT)

    def finish(self, p, dest, base, inverse):
        place = self.place

        def add(first, lane, value):
            lanes, rows = pl.ds(lane, value.shape[1]), value.shape[0]
            dest[p, at_rows(first + base, rows), lanes] += value * inverse[at_rows(first, rows), lanes]

        def lowest(value):
            return jnp.where(lower(value.shape[0]), value, 0.0)

        def highest(value):
            return jnp.where(lower(value.shape[0]), 0.0, value)

        wait_recv(place, self.copies[p], NEAR)
        add(place.near_border, 0, self.near_in[p])

        @pl.when(place.far)
        def _():
            self.copies[p][FAR].wait_recv()
            mixed = self.far_in[p, :, 128:256]
            add(place.far_border, 0, jnp.where(lower(64), self.corner_in[1, p], mixed))
            add(place.far_border, 128, self.far_in[p, :, 0:128])
            add(place.far_border, 256, jnp.where(lower(64), mixed, self.corner_in[0, p]))

        for k, (here, lane, keep) in enumerate(((place.right, 256, highest), (place.left, 0, lowest))):

            @pl.when(here)
            def _():
                self.copies[p][LEFT_NEXT + k].wait_recv()
                add(128, lane, keep(unpack(self.side_in[k, p, 128:192])))
                self.copies[p][LEFT + k].wait_recv()
                add(place.near_part, lane, keep(unpack(self.side_in[k, p, 0:64])))
                add(place.far_part, lane, keep(unpack(self.side_in[k, p, 64:128])))

    def close(self):
        for p in range(2):
            wait_send(self.place, self.copies[p])


def spread_kernel(grid):
    def kernel(
        field, offsets, counts, places, measured, tables, probe,
        ext, around, measured_here, tables_here, beams, power, update, light,
        mine, offsets_here, tall, far, side, corner, far_in, side_in, corner_in, sems, notes, local,
    ):
        place = Place(grid)
        peers = greet_all(place)
        pulls = [pltpu.make_async_copy(offsets, offsets_here, local.at[0])]
        pulls += [pltpu.make_async_copy(field.at[p], ext.at[p, 64:448, 0:384], local.at[1 + p]) for p in range(2)]
        later = [
            pltpu.make_async_copy(measured, measured_here, local.at[3]),
            pltpu.make_async_copy(tables, tables_here, local.at[4]),
        ]
        pulls.append(pltpu.make_async_copy(probe, tall.at[:, 8:136], local.at[5]))
        for pull in pulls:
            pull.start()
        halo = Halo(place, ext, far, side, corner, far_in, side_in, corner_in, sems)
        halo.clear()
        for i, d in enumerate(AROUND):

            @pl.when(jnp.logical_not(beside(place, d)))
            def _():
                around[i] = jnp.zeros((8, 128), jnp.int32)

        pulls[0].wait()
        mine[0:2, 0:12] = offsets_here[0, 0]
        mine[2:3, 0:1] = jnp.full((1, 1), counts[0, 0], jnp.int32)
        around[8] = mine[...]
        letters = []
        for i, d in enumerate(AROUND):
            letter = pltpu.make_async_remote_copy(
                mine,
                around.at[AROUND.index((-d[0], -d[1]))],
                notes.at[0, i],
                notes.at[1, i],
                device_id={"row": place.row + d[0], "col": place.col + d[1]},
                device_id_type=MESH,
            )
            letters.append(letter)
        pulls[1].wait()
        halo.pack(0)
        pl.semaphore_wait(pltpu.get_barrier_semaphore(), peers)
        for i, d in enumerate(AROUND):
            pl.when(beside(place, d))(letters[i].start)
        halo.start(0)
        pulls[2].wait()
        halo.pack(1)
        halo.start(1)
        halo.start_rest()
        for pull in later:
            pull.start()
        update[...] = jnp.zeros_like(update)
        light[...] = jnp.zeros_like(light)
        pulls[3].wait()
        for p in range(2):
            tall[p, 0:8] = tall[p, 128:136]
        power[...] = tall[0] * tall[0] + tall[1] * tall[1]

        def turn(slot, carry):
            live = (slot < counts[0, 0]).astype(jnp.float32)
            low_row, low_col = places[0, 0, 0, slot] & 7, places[0, 0, 1, slot] & 127
            for p in range(2):
                beams[slot, p] = pltpu.roll(tall[p, pl.ds(8 - low_row, 128), :], low_col, 1) * live
            return carry

        lax.fori_loop(0, 12, turn, 0)
        halo.finish()
        for i, d in enumerate(AROUND):
            pl.when(beside(place, d))(letters[i].wait_send)
            pl.when(beside(place, (-d[0], -d[1])))(letters[i].wait_recv)
        for pull in later:
            pull.wait()

    return kernel


def split(x):
    high = x.astype(jnp.bfloat16)
    return high, (x - high.astype(jnp.float32)).astype(jnp.bfloat16)


def dot(a, b):
    return jnp.dot(a, b, preferred_element_type=jnp.float32)


def right_mul(x, high, low):
    xh, xl = split(x)
    return dot(xh, high) + dot(xl, high) + dot(xh, low)


def left_mul(high, low, x):
    xh, xl = split(x)
    return dot(high, xh) + dot(high, xl) + dot(low, xh)


def cross(x):
    return jnp.concatenate(
        [
            jnp.concatenate([x[:128, :128], x[128:, :128]], axis=1),
            jnp.concatenate([x[:128, 128:], x[128:, 128:]], axis=1),
        ],
        axis=0,
    )


def gradient_kernel(with_light):
    def kernel(*refs):
        if with_light:
            around, ext, beams, measured, tables, _, power, _, update, light = refs
        else:
            around, ext, beams, measured, tables, _, update = refs
        count = around[8, 2, 0]
        lane = lax.broadcasted_iota(jnp.int32, (128, 128), 1)
        sub = lax.broadcasted_iota(jnp.int32, (8, 128), 0)

        def turned(source, shift_rows, shift_lanes):
            return pltpu.roll(source[pl.ds(8 - shift_rows, 128), :], shift_lanes, 1)

        def scatter(dest, first, lanes, shift_rows, shift_lanes, value):
            head = jnp.where(sub >= shift_rows, value[:8], 0.0)
            main = jnp.concatenate([head, value[8:]], axis=0)
            tail = jnp.where(sub < shift_rows, value[:8], 0.0)
            for which, at in enumerate(lanes):
                keep = lane >= shift_lanes if which == 0 else lane < shift_lanes
                dest[pl.ds(first, 128), at] += jnp.where(keep, main, 0.0)
                dest[pl.ds(first + 128, 8), at] += jnp.where(keep[:8], tail, 0.0)

        def tiles_of(col, base, wrap):
            tile = lax.shift_right_arithmetic(col, 7) + base
            first = lax.rem(tile + wrap, wrap)
            second = lax.rem(tile + wrap + 1, wrap)
            return [pl.ds(pl.multiple_of(t * 128, 128), 128) for t in (first, second)]

        def brighten(row, col, value):
            low_row, low_col = jnp.bitwise_and(row, 7), jnp.bitwise_and(col, 127)
            first = pl.multiple_of(row - low_row + 128, 8)
            scatter(light, first, tiles_of(col, 1, 5), low_row, low_col, value)

        def gather(slot):
            row, col = around[8, 0, slot], around[8, 1, slot]
            low_row, low_col = jnp.bitwise_and(row, 7), jnp.bitwise_and(col, 127)
            first = pl.multiple_of(row - low_row + 64, 8)
            lanes = tiles_of(col, 0, 4)
            beam = [beams[slot, p] for p in range(2)]
            window = []
            for p in range(2):
                main = jnp.where(
                    lane >= low_col, ext[p, pl.ds(first, 128), lanes[0]], ext[p, pl.ds(first, 128), lanes[1]]
                )
                tail = jnp.where(
                    lane[:8] >= low_col,
                    ext[p, pl.ds(first + 128, 8), lanes[0]],
                    ext[p, pl.ds(first + 128, 8), lanes[1]],
                )
                window.append(jnp.concatenate([jnp.where(sub >= low_row, main[:8], tail), main[8:]], axis=0))
            real = beam[0] * window[0] - beam[1] * window[1]
            imag = beam[0] * window[1] + beam[1] * window[0]
            return jnp.concatenate([real, imag], axis=1), (slot, first, lanes, low_row, low_col, row, col)

        def put(back, at):
            slot, first, lanes, low_row, low_col, row, col = at
            beam = [beams[slot, p] for p in range(2)]
            real, imag = back[:, :128], back[:, 128:]
            scatter(update.at[0], first, lanes, low_row, low_col, beam[0] * real + beam[1] * imag)
            scatter(update.at[1], first, lanes, low_row, low_col, beam[0] * imag - beam[1] * real)
            if with_light:
                brighten(row, col, beam[0] * beam[0] + beam[1] * beam[1])

        def some(step, carry):
            slots = [step * GROUP + k for k in range(GROUP)]
            pairs = [(k, k + 1) for k in range(0, GROUP, 2)]
            gathered = [gather(slot) for slot in slots]
            waves = [jnp.concatenate([gathered[a][0], gathered[b][0]], axis=0) for a, b in pairs]
            half = [cross(right_mul(wave, tables[0], tables[1])) for wave in waves]
            far = [left_mul(tables[2], tables[3], x) for x in half]
            change = []
            for x, (a, b) in zip(far, pairs):
                real, imag = x[:128], x[128:]
                known = jnp.concatenate([measured[0, 0, slots[a]], measured[0, 0, slots[b]]], axis=1)
                ratio = known * lax.rsqrt(real * real + imag * imag + 0.25) - 1.0
                change.append(jnp.concatenate([real * ratio, imag * ratio], axis=0))
            half = [cross(left_mul(tables[0], tables[1], x)) for x in change]
            back = [right_mul(x, tables[2], tables[3]) for x in half]
            for x, (a, b) in zip(back, pairs):
                put(x[:128], gathered[a][1])
                put(x[128:], gathered[b][1])
            return carry

        lax.fori_loop(0, (count + GROUP - 1) // GROUP, some, 0)
        if with_light:
            for i, d in enumerate(AROUND):

                def other(slot, carry):
                    row = around[i, 0, slot] + d[0] * 384
                    col = around[i, 1, slot] + d[1] * 384
                    touches = (row > -128) & (row < 384) & (col > -128) & (col < 384)

                    @pl.when(touches)
                    def _():
                        low_row, low_col = jnp.bitwise_and(row, 7), jnp.bitwise_and(col, 127)
                        brighten(row, col, turned(power, low_row, low_col))

                    return carry

                lax.fori_loop(0, around[i, 2, 0], other, 0)

    return kernel


def between_kernel(grid):
    def kernel(
        update, light, field,
        ext, cleared, inverse,
        near_in, relay_in, far, side, corner, far_in, side_in, corner_in, sems,
        halo_far, halo_side, halo_corner, halo_far_in, halo_side_in, halo_corner_in, more,
    ):
        place = Place(grid)
        greet(place)
        fold = Fold(place, update, near_in, relay_in, far, side, corner, far_in, side_in, corner_in, sems)
        halo = Halo(place, ext, halo_far, halo_side, halo_corner, halo_far_in, halo_side_in, halo_corner_in, more)
        fold.pack()
        greeted(place)
        fold.start()
        halo.clear()
        inverse[...] = 1.0 / (light[128:512, 128:512] + 1.0)
        for p in range(2):
            ext[p, 64:448, 0:384] = field[p, 64:448, 0:384] + update[p, 64:448, 0:384] * inverse[...]
        cleared[...] = jnp.zeros_like(cleared)
        for p in range(2):
            fold.finish(p, ext, 64, inverse)
            halo.pack(p)
            halo.start(p)
        halo.start_rest()
        halo.finish()
        fold.close()

    return kernel


def last_kernel(grid):
    def kernel(update, inverse, ext, out, near_in, relay_in, far, side, corner, far_in, side_in, corner_in, sems):
        place = Place(grid)
        greet(place)
        fold = Fold(place, update, near_in, relay_in, far, side, corner, far_in, side_in, corner_in, sems)
        fold.pack()
        greeted(place)
        fold.start()
        for p in range(2):
            out[p] = ext[p, 64:448, 0:384] + update[p, 64:448, 0:384] * inverse[...]
        for p in range(2):
            fold.finish(p, out, 0, inverse)
        fold.close()

    return kernel


def hold(x):
    return pltpu.with_memory_space_constraint(x, pltpu.MemorySpace.HBM)


def params(collective_id=None):
    if collective_id is None:
        return pltpu.CompilerParams(vmem_limit_bytes=LIMIT)
    return pltpu.CompilerParams(collective_id=collective_id, has_side_effects=True, vmem_limit_bytes=LIMIT)


def shards(grid, tables, object_field, probe, amplitudes, offsets, counts):
    f32, i32 = jnp.float32, jnp.int32
    shape = jax.ShapeDtypeStruct
    ext_shape, light_shape = shape((2, 512, 512), f32), shape((648, 640), f32)
    offsets = jnp.swapaxes(offsets, 2, 3)
    packs = [pltpu.VMEM((2, 64, 256), f32), pltpu.VMEM((2, 2, 192, 128), f32), pltpu.VMEM((2, 2, 64, 128), f32)]
    folds = [pltpu.VMEM((2, 64, 384), f32), pltpu.VMEM((2, 64, 128), f32)] + packs + packs
    sems = pltpu.SemaphoreType.DMA((2, 2, 11))
    ext, around, measured, tables, beams, power, update, light = pl.pallas_call(
        spread_kernel(grid),
        name="spread",
        out_shape=(
            ext_shape,
            shape((9, 8, 128), i32),
            shape(amplitudes.shape, f32),
            shape(tables.shape, tables.dtype),
            shape((12, 2, 128, 128), f32),
            shape((136, 128), f32),
            ext_shape,
            light_shape,
        ),
        in_specs=[HBM, HBM, SMEM, SMEM, HBM, HBM, HBM],
        out_specs=(VMEM,) * 8,
        scratch_shapes=[pltpu.VMEM((8, 128), i32), pltpu.VMEM((1, 1, 2, 12), i32), pltpu.VMEM((2, 136, 128), f32)]
        + packs
        + packs
        + [sems, pltpu.SemaphoreType.DMA((2, 8)), pltpu.SemaphoreType.DMA((6,))],
        compiler_params=params(0),
    )(hold(object_field), hold(offsets), counts, offsets, hold(amplitudes), hold(tables), hold(probe))
    update, light = pl.pallas_call(
        gradient_kernel(True),
        name="gradient_light",
        out_shape=(ext_shape, light_shape),
        in_specs=[SMEM] + [VMEM] * 7,
        out_specs=(VMEM,) * 2,
        input_output_aliases={5: 0, 7: 1},
        compiler_params=params(),
    )(around, ext, beams, measured, tables, update, power, light)
    ext, cleared, inverse = pl.pallas_call(
        between_kernel(grid),
        name="between",
        out_shape=(ext_shape, ext_shape, shape((384, 384), f32)),
        in_specs=[VMEM] * 3,
        out_specs=(VMEM,) * 3,
        scratch_shapes=folds + [sems] + packs + packs + [sems],
        compiler_params=params(1),
    )(update, light, ext)
    update = pl.pallas_call(
        gradient_kernel(False),
        name="gradient",
        out_shape=ext_shape,
        in_specs=[SMEM] + [VMEM] * 5,
        out_specs=VMEM,
        input_output_aliases={5: 0},
        compiler_params=params(),
    )(around, ext, beams, measured, tables, cleared)
    return pl.pallas_call(
        last_kernel(grid),
        name="last",
        out_shape=shape((2, 384, 384), f32),
        in_specs=[VMEM] * 3,
        out_specs=VMEM,
        scratch_shapes=folds + [sems],
        compiler_params=params(2),
    )(update, inverse, ext)


def solution(mesh):
    grid = (mesh.shape["row"], mesh.shape["col"])
    tables = dft_tables(128)
    placed = (
        P(None, "row", "col"),
        P(),
        P("row", "col", None, None, None),
        P("row", "col", None, None),
        P("row", "col"),
    )

    def body(*args):
        return shards(grid, jnp.asarray(tables), *args)

    return jax.shard_map(body, mesh=mesh, in_specs=placed, out_specs=P(None, "row", "col"), check_vma=False)
```

```python
import math

import jax
import jax.numpy as jnp
import numpy as np
from jax import lax
from jax.experimental import pallas as pl
from jax.experimental.pallas import tpu as pltpu
from jax.sharding import PartitionSpec as P

AROUND = ((-1, 0), (1, 0), (0, -1), (0, 1), (-1, -1), (-1, 1), (1, -1), (1, 1))
MESH = pl.DeviceIdType.MESH
VMEM = pl.BlockSpec(memory_space=pltpu.VMEM)
SMEM = pl.BlockSpec(memory_space=pltpu.SMEM)
HBM = pl.BlockSpec(memory_space=pltpu.MemorySpace.HBM)
LIMIT = 24 << 20
GROUP = 6
NEAR, FAR, LEFT, RIGHT, FAR_LEFT, FAR_RIGHT, LEFT_NEXT, RIGHT_NEXT, RELAY, EDGE_LEFT, EDGE_RIGHT = range(11)
DIAGONAL = (FAR_LEFT, FAR_RIGHT, EDGE_LEFT, EDGE_RIGHT)


def dft_tables(length):
    index = np.arange(length)
    angle = (np.outer(index, index) % length) * (2.0 * math.pi / length)
    cosine, sine = np.cos(angle) / math.sqrt(length), np.sin(angle) / math.sqrt(length)
    table = np.block([[cosine, -sine], [sine, cosine]])
    high = table.astype(jnp.bfloat16)
    low = (table - high.astype(np.float64)).astype(jnp.bfloat16)
    return np.stack([high, low, high.T, low.T])


def swap(x):
    return pltpu.roll(x, 64, x.ndim - 1)


def lower(rows):
    return lax.broadcasted_iota(jnp.int32, (rows, 128), 1) < 64


def pack(x, keep_low):
    rows = x.shape[0] // 2
    keep = lower(rows) if keep_low else ~lower(rows)
    return jnp.where(keep, x[:rows], swap(x[rows:]))


def unpack(x):
    return jnp.concatenate([x, swap(x)], axis=0)


def merge(a, b):
    keep = lower(a.shape[0])
    return jnp.concatenate([jnp.where(keep, a, b), jnp.where(keep, swap(a), swap(b))], axis=0)


class Place:
    def __init__(self, grid):
        self.row, self.col = lax.axis_index("row"), lax.axis_index("col")
        self.odd = lax.rem(self.row, 2)
        self.near_row = self.row + 1 - 2 * self.odd
        self.far_row = self.row - 1 + 2 * self.odd
        self.grid = grid
        far = (self.far_row >= 0) & (self.far_row < grid[0])
        left, right = self.col > 0, self.col < grid[1] - 1
        self.far, self.left, self.right = far, left, right
        ends = (far & jnp.logical_not(left), far & jnp.logical_not(right))
        both = (None, far, left, right, far & left, far & right, left, right, None) + ends
        self.sends = both
        order = (NEAR, FAR, RIGHT, LEFT, FAR_RIGHT, FAR_LEFT, RIGHT_NEXT, LEFT_NEXT, RELAY, EDGE_LEFT, EDGE_RIGHT)
        self.gets = tuple(both[i] for i in order)
        self.near_border = self.pick(320, 0)
        self.far_border = self.pick(0, 320)
        self.near_halo = self.pick(448, 0)
        self.far_halo = self.pick(0, 448)

    def pick(self, even, odd):
        return pl.multiple_of(even + self.odd * (odd - even), 64)

    def target(self, which):
        row = {NEAR: self.near_row, RELAY: self.near_row, FAR: self.far_row}
        row.update({which: self.far_row for which in DIAGONAL})
        side = {LEFT: -1, FAR_LEFT: -1, LEFT_NEXT: -1, RIGHT: 1, FAR_RIGHT: 1, RIGHT_NEXT: 1}
        return {"row": row.get(which, self.row), "col": self.col + side.get(which, 0)}


def when(condition, body):
    if condition is None:
        body()
    else:
        pl.when(condition)(body)


def greet(place):
    barrier = pltpu.get_barrier_semaphore()
    for which in (NEAR, FAR, LEFT, RIGHT, FAR_LEFT, FAR_RIGHT):
        when(
            place.sends[which],
            lambda: pl.semaphore_signal(
                barrier, inc=1, device_id=place.target(which), device_id_type=MESH
            ),
        )


def greeted(place):
    far, left, right = (jnp.where(x, 1, 0) for x in (place.far, place.left, place.right))
    pl.semaphore_wait(pltpu.get_barrier_semaphore(), 1 + far + (left + right) * (1 + far))


def greet_all(place):
    barrier = pltpu.get_barrier_semaphore()
    count = 0
    for d in AROUND:
        count += jnp.where(beside(place, d), 1, 0)

        @pl.when(beside(place, d))
        def _():
            pl.semaphore_signal(
                barrier, inc=1, device_id={"row": place.row + d[0], "col": place.col + d[1]}, device_id_type=MESH
            )

    return count


def beside(place, d):
    row, col = place.row + d[0], place.col + d[1]
    return (row >= 0) & (row < place.grid[0]) & (col >= 0) & (col < place.grid[1])


def remote(place, which, src, dst, sems, p):
    return pltpu.make_async_remote_copy(
        src, dst, sems.at[0, p, which], sems.at[1, p, which], device_id=place.target(which), device_id_type=MESH
    )


def start(place, copies, *which):
    for i in which:
        when(place.sends[i], copies[i].start)


def wait_recv(place, copies, *which):
    for i in which:
        when(place.gets[i], copies[i].wait_recv)


def wait_send(place, copies):
    for i, copy in enumerate(copies):
        when(place.sends[i], copy.wait_send)


def strips(far, far_in, side, side_in, corner, corner_in, p):
    return {
        FAR: (far.at[p], far_in.at[p]),
        FAR_LEFT: (corner.at[0, p], corner_in.at[0, p]),
        FAR_RIGHT: (corner.at[1, p], corner_in.at[1, p]),
        EDGE_LEFT: (corner.at[0, p], corner_in.at[1, p]),
        EDGE_RIGHT: (corner.at[1, p], corner_in.at[0, p]),
        LEFT: (side.at[0, p, 0:64], side_in.at[0, p, 0:64]),
        RIGHT: (side.at[1, p, 0:64], side_in.at[1, p, 0:64]),
        LEFT_NEXT: (side.at[0, p, 64:192], side_in.at[0, p, 64:192]),
        RIGHT_NEXT: (side.at[1, p, 64:192], side_in.at[1, p, 64:192]),
    }


def at_rows(first, rows):
    return pl.ds(pl.multiple_of(first, 64), rows)


class Halo:
    def __init__(self, place, ext, far, side, corner, far_in, side_in, corner_in, sems):
        self.place, self.ext, self.far, self.far_in = place, ext, far, far_in
        self.side, self.corner, self.side_in, self.corner_in = side, corner, side_in, corner_in
        near, target = at_rows(place.near_border + 64, 64), at_rows(place.far_halo, 64)
        self.copies = []
        for p in range(2):
            ends = strips(far, far_in, side, side_in, corner, corner_in, p)
            ends[NEAR] = (ext.at[p, near, 0:384], ext.at[p, target, 0:384])
            ends[RELAY] = (ext.at[p, near, 384:512], ext.at[p, target, 384:512])
            self.copies.append([remote(place, i, *ends[i], sems, p) for i in range(11)])

    def clear(self):
        place = self.place

        @pl.when(jnp.logical_not(place.far))
        def _():
            self.far_in[...] = jnp.zeros((2, 64, 256), jnp.float32)
            self.corner_in[...] = jnp.zeros((2, 2, 64, 128), jnp.float32)

        for k, side in enumerate((place.right, place.left)):

            @pl.when(jnp.logical_not(side))
            def _():
                self.side_in[k] = jnp.zeros((2, 192, 128), jnp.float32)

    def pack(self, p):
        place, ext = self.place, self.ext
        for k, lane in enumerate((0, 256)):
            for i, first in enumerate((place.near_border, place.far_border)):
                self.side[k, p, 32 * i : 32 * i + 32] = pack(ext[p, at_rows(first + 64, 64), lane : lane + 128], k == 0)
            self.side[k, p, 64:192] = pack(ext[p, 128:384, lane : lane + 128], k == 0)
        rows = at_rows(place.far_border + 64, 64)
        self.far[p, :, 0:128] = ext[p, rows, 128:256]
        self.far[p, :, 128:256] = jnp.where(lower(64), ext[p, rows, 256:384], ext[p, rows, 0:128])

    def start(self, p):
        start(self.place, self.copies[p], LEFT, RIGHT, FAR)

    def start_rest(self):
        for p in range(2):
            start(self.place, self.copies[p], LEFT_NEXT, RIGHT_NEXT, NEAR)

    def finish(self):
        place, ext, low = self.place, self.ext, lower(64)
        for p in range(2):
            wait_recv(place, self.copies[p], LEFT, RIGHT)
            for i, first in enumerate((place.near_border, place.far_border)):
                parts = [self.side_in[k, p, 32 * i : 32 * i + 32] for k in range(2)]
                ext[p, at_rows(first + 64, 64), 384:512] = merge(*parts)
            start(place, self.copies[p], RELAY)
            rows = at_rows(place.far_border + 64, 64)
            self.corner[0, p] = jnp.where(low, ext[p, rows, 0:128], ext[p, rows, 384:512])
            self.corner[1, p] = jnp.where(low, ext[p, rows, 384:512], ext[p, rows, 256:384])
            start(place, self.copies[p], *DIAGONAL)
        for p in range(2):
            wait_recv(place, self.copies[p], LEFT_NEXT, RIGHT_NEXT)
            ext[p, 128:384, 384:512] = merge(self.side_in[0, p, 64:192], self.side_in[1, p, 64:192])
            wait_recv(place, self.copies[p], FAR, *DIAGONAL)
            rows = at_rows(place.far_halo, 64)
            right, left = self.corner_in[0, p], self.corner_in[1, p]
            mixed = self.far_in[p, :, 128:256]
            ext[p, rows, 0:128] = jnp.where(low, left, mixed)
            ext[p, rows, 128:256] = self.far_in[p, :, 0:128]
            ext[p, rows, 256:384] = jnp.where(low, mixed, right)
            ext[p, rows, 384:512] = jnp.where(low, right, left)
        for p in range(2):
            wait_recv(place, self.copies[p], NEAR, RELAY)
            wait_send(place, self.copies[p])


class Fold:
    def __init__(self, place, update, near_in, relay_in, far, side, corner, far_in, side_in, corner_in, sems):
        self.place, self.update, self.near_in, self.relay_in = place, update, near_in, relay_in
        self.far, self.far_in = far, far_in
        self.side, self.corner, self.side_in, self.corner_in = side, corner, side_in, corner_in
        near = at_rows(place.near_halo, 64)
        self.copies = []
        for p in range(2):
            ends = strips(far, far_in, side, side_in, corner, corner_in, p)
            ends[NEAR] = (update.at[p, near, 0:384], near_in.at[p])
            ends[RELAY] = (update.at[p, near, 384:512], relay_in.at[p])
            self.copies.append([remote(place, i, *ends[i], sems, p) for i in range(11)])

    def pack(self):
        place, update, low = self.place, self.update, lower(64)

        @pl.when(jnp.logical_not(place.far))
        def _():
            self.corner_in[...] = jnp.zeros((2, 2, 64, 128), jnp.float32)

        rows = at_rows(place.far_halo, 64)
        for p in range(2):
            tiles = [update[p, rows, 128 * t : 128 * t + 128] for t in range(4)]
            self.corner[0, p] = jnp.where(low, tiles[0], tiles[3])
            self.corner[1, p] = jnp.where(low, tiles[3], tiles[2])
            self.far[p, :, 0:128] = tiles[1]
            self.far[p, :, 128:256] = jnp.where(low, tiles[2], tiles[0])
            for k in range(2):
                self.side[k, p, 64:192] = pack(update[p, 128:384, 384:512], k == 1)

    def start(self):
        place, update = self.place, self.update
        for p in range(2):
            start(place, self.copies[p], *DIAGONAL, RELAY)
            if p == 0:
                start(place, self.copies[p], FAR, LEFT_NEXT, RIGHT_NEXT)
        start(place, self.copies[1], FAR)
        for p in range(2):
            wait_recv(place, self.copies[p], RELAY, *DIAGONAL)
            extra = (self.relay_in[p], jnp.where(lower(64), self.corner_in[0, p], self.corner_in[1, p]))
            for i, first in enumerate((place.near_border, place.far_border)):
                part = update[p, at_rows(first + 64, 64), 384:512] + extra[i]
                for k in range(2):
                    self.side[k, p, 32 * i : 32 * i + 32] = pack(part, k == 1)
            start(place, self.copies[p], LEFT, RIGHT)
            if p == 0:
                start(place, self.copies[1], LEFT_NEXT, RIGHT_NEXT)
        for p in range(2):
            start(place, self.copies[p], NEAR)

    def finish(self, p, dest, base, inverse):
        place = self.place

        def add(first, lane, value):
            lanes, rows = pl.ds(lane, value.shape[1]), value.shape[0]
            dest[p, at_rows(first + base, rows), lanes] += value * inverse[at_rows(first, rows), lanes]

        def lowest(value):
            return jnp.where(lower(value.shape[0]), value, 0.0)

        def highest(value):
            return jnp.where(lower(value.shape[0]), 0.0, value)

        wait_recv(place, self.copies[p], NEAR)
        add(place.near_border, 0, self.near_in[p])

        @pl.when(place.far)
        def _():
            self.copies[p][FAR].wait_recv()
            mixed = self.far_in[p, :, 128:256]
            add(place.far_border, 0, jnp.where(lower(64), self.corner_in[1, p], mixed))
            add(place.far_border, 128, self.far_in[p, :, 0:128])
            add(place.far_border, 256, jnp.where(lower(64), mixed, self.corner_in[0, p]))

        for k, (here, lane, keep) in enumerate(((place.right, 256, highest), (place.left, 0, lowest))):

            @pl.when(here)
            def _():
                self.copies[p][LEFT_NEXT + k].wait_recv()
                add(64, lane, keep(unpack(self.side_in[k, p, 64:192])))
                self.copies[p][LEFT + k].wait_recv()
                add(place.near_border, lane, keep(unpack(self.side_in[k, p, 0:32])))
                add(place.far_border, lane, keep(unpack(self.side_in[k, p, 32:64])))

    def close(self):
        for p in range(2):
            wait_send(self.place, self.copies[p])


def spread_kernel(grid):
    def kernel(
        field, offsets, counts, places, measured, tables, probe,
        ext, around, measured_here, tables_here, beams, power, update, light,
        mine, offsets_here, tall, far, side, corner, far_in, side_in, corner_in, sems, notes, local,
    ):
        place = Place(grid)
        peers = greet_all(place)
        pulls = [pltpu.make_async_copy(offsets, offsets_here, local.at[0])]
        pulls += [pltpu.make_async_copy(field.at[p], ext.at[p, 64:448, 0:384], local.at[1 + p]) for p in range(2)]
        later = [
            pltpu.make_async_copy(measured, measured_here, local.at[3]),
            pltpu.make_async_copy(tables, tables_here, local.at[4]),
        ]
        pulls.append(pltpu.make_async_copy(probe, tall.at[:, 8:136], local.at[5]))
        for pull in pulls:
            pull.start()
        halo = Halo(place, ext, far, side, corner, far_in, side_in, corner_in, sems)
        halo.clear()
        for i, d in enumerate(AROUND):

            @pl.when(jnp.logical_not(beside(place, d)))
            def _():
                around[i] = jnp.zeros((8, 128), jnp.int32)

        pulls[0].wait()
        mine[0:2, 0:12] = offsets_here[0, 0]
        mine[2:3, 0:1] = jnp.full((1, 1), counts[0, 0], jnp.int32)
        around[8] = mine[...]
        letters = []
        for i, d in enumerate(AROUND):
            letter = pltpu.make_async_remote_copy(
                mine,
                around.at[AROUND.index((-d[0], -d[1]))],
                notes.at[0, i],
                notes.at[1, i],
                device_id={"row": place.row + d[0], "col": place.col + d[1]},
                device_id_type=MESH,
            )
            letters.append(letter)
        pulls[1].wait()
        halo.pack(0)
        pl.semaphore_wait(pltpu.get_barrier_semaphore(), peers)
        for i, d in enumerate(AROUND):
            pl.when(beside(place, d))(letters[i].start)
        halo.start(0)
        pulls[2].wait()
        halo.pack(1)
        halo.start(1)
        halo.start_rest()
        for pull in later:
            pull.start()
        update[...] = jnp.zeros_like(update)
        light[...] = jnp.zeros_like(light)
        pulls[3].wait()
        for p in range(2):
            tall[p, 0:8] = tall[p, 128:136]
        power[...] = tall[0] * tall[0] + tall[1] * tall[1]

        def turn(slot, carry):
            live = (slot < counts[0, 0]).astype(jnp.float32)
            low_row, low_col = places[0, 0, 0, slot] & 7, places[0, 0, 1, slot] & 127
            for p in range(2):
                beams[slot, p] = pltpu.roll(tall[p, pl.ds(8 - low_row, 128), :], low_col, 1) * live
            return carry

        lax.fori_loop(0, 12, turn, 0)
        halo.finish()
        for i, d in enumerate(AROUND):
            pl.when(beside(place, d))(letters[i].wait_send)
            pl.when(beside(place, (-d[0], -d[1])))(letters[i].wait_recv)
        for pull in later:
            pull.wait()

    return kernel


def split(x):
    high = x.astype(jnp.bfloat16)
    return high, (x - high.astype(jnp.float32)).astype(jnp.bfloat16)


def dot(a, b):
    return jnp.dot(a, b, preferred_element_type=jnp.float32)


def right_mul(x, high, low):
    xh, xl = split(x)
    return dot(xh, high) + dot(xl, high) + dot(xh, low)


def left_mul(high, low, x):
    xh, xl = split(x)
    return dot(high, xh) + dot(high, xl) + dot(low, xh)


def cross(x):
    return jnp.concatenate(
        [
            jnp.concatenate([x[:128, :128], x[128:, :128]], axis=1),
            jnp.concatenate([x[:128, 128:], x[128:, 128:]], axis=1),
        ],
        axis=0,
    )


def gradient_kernel(with_light):
    def kernel(*refs):
        if with_light:
            around, ext, beams, measured, tables, _, power, _, update, light = refs
        else:
            around, ext, beams, measured, tables, _, update = refs
        count = around[8, 2, 0]
        lane = lax.broadcasted_iota(jnp.int32, (128, 128), 1)
        sub = lax.broadcasted_iota(jnp.int32, (8, 128), 0)

        def turned(source, shift_rows, shift_lanes):
            return pltpu.roll(source[pl.ds(8 - shift_rows, 128), :], shift_lanes, 1)

        def scatter(dest, first, lanes, shift_rows, shift_lanes, value):
            head = jnp.where(sub >= shift_rows, value[:8], 0.0)
            main = jnp.concatenate([head, value[8:]], axis=0)
            tail = jnp.where(sub < shift_rows, value[:8], 0.0)
            for which, at in enumerate(lanes):
                keep = lane >= shift_lanes if which == 0 else lane < shift_lanes
                dest[pl.ds(first, 128), at] += jnp.where(keep, main, 0.0)
                dest[pl.ds(first + 128, 8), at] += jnp.where(keep[:8], tail, 0.0)

        def tiles_of(col, base, wrap):
            tile = lax.shift_right_arithmetic(col, 7) + base
            first = lax.rem(tile + wrap, wrap)
            second = lax.rem(tile + wrap + 1, wrap)
            return [pl.ds(pl.multiple_of(t * 128, 128), 128) for t in (first, second)]

        def brighten(row, col, value):
            low_row, low_col = jnp.bitwise_and(row, 7), jnp.bitwise_and(col, 127)
            first = pl.multiple_of(row - low_row + 128, 8)
            scatter(light, first, tiles_of(col, 1, 5), low_row, low_col, value)

        def gather(slot):
            row, col = around[8, 0, slot], around[8, 1, slot]
            low_row, low_col = jnp.bitwise_and(row, 7), jnp.bitwise_and(col, 127)
            first = pl.multiple_of(row - low_row + 64, 8)
            lanes = tiles_of(col, 0, 4)
            beam = [beams[slot, p] for p in range(2)]
            window = []
            for p in range(2):
                main = jnp.where(
                    lane >= low_col, ext[p, pl.ds(first, 128), lanes[0]], ext[p, pl.ds(first, 128), lanes[1]]
                )
                tail = jnp.where(
                    lane[:8] >= low_col,
                    ext[p, pl.ds(first + 128, 8), lanes[0]],
                    ext[p, pl.ds(first + 128, 8), lanes[1]],
                )
                window.append(jnp.concatenate([jnp.where(sub >= low_row, main[:8], tail), main[8:]], axis=0))
            real = beam[0] * window[0] - beam[1] * window[1]
            imag = beam[0] * window[1] + beam[1] * window[0]
            return jnp.concatenate([real, imag], axis=1), (slot, first, lanes, low_row, low_col, row, col)

        def put(back, at):
            slot, first, lanes, low_row, low_col, row, col = at
            beam = [beams[slot, p] for p in range(2)]
            real, imag = back[:, :128], back[:, 128:]
            scatter(update.at[0], first, lanes, low_row, low_col, beam[0] * real + beam[1] * imag)
            scatter(update.at[1], first, lanes, low_row, low_col, beam[0] * imag - beam[1] * real)
            if with_light:
                brighten(row, col, beam[0] * beam[0] + beam[1] * beam[1])

        def some(step, carry):
            slots = [step * GROUP + k for k in range(GROUP)]
            pairs = [(k, k + 1) for k in range(0, GROUP, 2)]
            gathered = [gather(slot) for slot in slots]
            waves = [jnp.concatenate([gathered[a][0], gathered[b][0]], axis=0) for a, b in pairs]
            half = [cross(right_mul(wave, tables[0], tables[1])) for wave in waves]
            far = [left_mul(tables[2], tables[3], x) for x in half]
            change = []
            for x, (a, b) in zip(far, pairs):
                real, imag = x[:128], x[128:]
                known = jnp.concatenate([measured[0, 0, slots[a]], measured[0, 0, slots[b]]], axis=1)
                ratio = known * lax.rsqrt(real * real + imag * imag + 0.25) - 1.0
                change.append(jnp.concatenate([real * ratio, imag * ratio], axis=0))
            half = [cross(left_mul(tables[0], tables[1], x)) for x in change]
            back = [right_mul(x, tables[2], tables[3]) for x in half]
            for x, (a, b) in zip(back, pairs):
                put(x[:128], gathered[a][1])
                put(x[128:], gathered[b][1])
            return carry

        lax.fori_loop(0, (count + GROUP - 1) // GROUP, some, 0)
        if with_light:
            for i, d in enumerate(AROUND):

                def other(slot, carry):
                    row = around[i, 0, slot] + d[0] * 384
                    col = around[i, 1, slot] + d[1] * 384
                    touches = (row > -128) & (row < 384) & (col > -128) & (col < 384)

                    @pl.when(touches)
                    def _():
                        low_row, low_col = jnp.bitwise_and(row, 7), jnp.bitwise_and(col, 127)
                        brighten(row, col, turned(power, low_row, low_col))

                    return carry

                lax.fori_loop(0, around[i, 2, 0], other, 0)

    return kernel


def between_kernel(grid):
    def kernel(
        update, light, field,
        ext, cleared, inverse,
        near_in, relay_in, far, side, corner, far_in, side_in, corner_in, sems,
        halo_far, halo_side, halo_corner, halo_far_in, halo_side_in, halo_corner_in, more,
    ):
        place = Place(grid)
        greet(place)
        fold = Fold(place, update, near_in, relay_in, far, side, corner, far_in, side_in, corner_in, sems)
        halo = Halo(place, ext, halo_far, halo_side, halo_corner, halo_far_in, halo_side_in, halo_corner_in, more)
        fold.pack()
        greeted(place)
        fold.start()
        halo.clear()
        inverse[...] = 1.0 / (light[128:512, 128:512] + 1.0)
        for p in range(2):
            ext[p, 64:448, 0:384] = field[p, 64:448, 0:384] + update[p, 64:448, 0:384] * inverse[...]
        cleared[...] = jnp.zeros_like(cleared)
        for p in range(2):
            fold.finish(p, ext, 64, inverse)
            halo.pack(p)
            halo.start(p)
        halo.start_rest()
        halo.finish()
        fold.close()

    return kernel


def last_kernel(grid):
    def kernel(update, inverse, ext, out, near_in, relay_in, far, side, corner, far_in, side_in, corner_in, sems):
        place = Place(grid)
        greet(place)
        fold = Fold(place, update, near_in, relay_in, far, side, corner, far_in, side_in, corner_in, sems)
        fold.pack()
        greeted(place)
        fold.start()
        for p in range(2):
            out[p] = ext[p, 64:448, 0:384] + update[p, 64:448, 0:384] * inverse[...]
        for p in range(2):
            fold.finish(p, out, 0, inverse)
        fold.close()

    return kernel


def hold(x):
    return pltpu.with_memory_space_constraint(x, pltpu.MemorySpace.HBM)


def params(collective_id=None):
    if collective_id is None:
        return pltpu.CompilerParams(vmem_limit_bytes=LIMIT)
    return pltpu.CompilerParams(collective_id=collective_id, has_side_effects=True, vmem_limit_bytes=LIMIT)


def shards(grid, tables, object_field, probe, amplitudes, offsets, counts):
    f32, i32 = jnp.float32, jnp.int32
    shape = jax.ShapeDtypeStruct
    ext_shape, light_shape = shape((2, 512, 512), f32), shape((648, 640), f32)
    offsets = jnp.swapaxes(offsets, 2, 3)
    packs = [pltpu.VMEM((2, 64, 256), f32), pltpu.VMEM((2, 2, 192, 128), f32), pltpu.VMEM((2, 2, 64, 128), f32)]
    folds = [pltpu.VMEM((2, 64, 384), f32), pltpu.VMEM((2, 64, 128), f32)] + packs + packs
    sems = pltpu.SemaphoreType.DMA((2, 2, 11))
    ext, around, measured, tables, beams, power, update, light = pl.pallas_call(
        spread_kernel(grid),
        name="spread",
        out_shape=(
            ext_shape,
            shape((9, 8, 128), i32),
            shape(amplitudes.shape, f32),
            shape(tables.shape, tables.dtype),
            shape((12, 2, 128, 128), f32),
            shape((136, 128), f32),
            ext_shape,
            light_shape,
        ),
        in_specs=[HBM, HBM, SMEM, SMEM, HBM, HBM, HBM],
        out_specs=(VMEM,) * 8,
        scratch_shapes=[pltpu.VMEM((8, 128), i32), pltpu.VMEM((1, 1, 2, 12), i32), pltpu.VMEM((2, 136, 128), f32)]
        + packs
        + packs
        + [sems, pltpu.SemaphoreType.DMA((2, 8)), pltpu.SemaphoreType.DMA((6,))],
        compiler_params=params(0),
    )(hold(object_field), hold(offsets), counts, offsets, hold(amplitudes), hold(tables), hold(probe))
    update, light = pl.pallas_call(
        gradient_kernel(True),
        name="gradient_light",
        out_shape=(ext_shape, light_shape),
        in_specs=[SMEM] + [VMEM] * 7,
        out_specs=(VMEM,) * 2,
        input_output_aliases={5: 0, 7: 1},
        compiler_params=params(),
    )(around, ext, beams, measured, tables, update, power, light)
    ext, cleared, inverse = pl.pallas_call(
        between_kernel(grid),
        name="between",
        out_shape=(ext_shape, ext_shape, shape((384, 384), f32)),
        in_specs=[VMEM] * 3,
        out_specs=(VMEM,) * 3,
        scratch_shapes=folds + [sems] + packs + packs + [sems],
        compiler_params=params(1),
    )(update, light, ext)
    update = pl.pallas_call(
        gradient_kernel(False),
        name="gradient",
        out_shape=ext_shape,
        in_specs=[SMEM] + [VMEM] * 5,
        out_specs=VMEM,
        input_output_aliases={5: 0},
        compiler_params=params(),
    )(around, ext, beams, measured, tables, cleared)
    return pl.pallas_call(
        last_kernel(grid),
        name="last",
        out_shape=shape((2, 384, 384), f32),
        in_specs=[VMEM] * 3,
        out_specs=VMEM,
        scratch_shapes=folds + [sems],
        compiler_params=params(2),
    )(update, inverse, ext)


def solution(mesh):
    grid = (mesh.shape["row"], mesh.shape["col"])
    tables = dft_tables(128)
    placed = (
        P(None, "row", "col"),
        P(),
        P("row", "col", None, None, None),
        P("row", "col", None, None),
        P("row", "col"),
    )

    def body(*args):
        return shards(grid, jnp.asarray(tables), *args)

    return jax.shard_map(body, mesh=mesh, in_specs=placed, out_specs=P(None, "row", "col"), check_vma=False)
```

```python
import math

import jax
import jax.numpy as jnp
import numpy as np
from jax import lax
from jax.experimental import pallas as pl
from jax.experimental.pallas import tpu as pltpu
from jax.sharding import PartitionSpec as P

AROUND = ((-1, 0), (1, 0), (0, -1), (0, 1), (-1, -1), (-1, 1), (1, -1), (1, 1))
MESH = pl.DeviceIdType.MESH
VMEM = pl.BlockSpec(memory_space=pltpu.VMEM)
SMEM = pl.BlockSpec(memory_space=pltpu.SMEM)
HBM = pl.BlockSpec(memory_space=pltpu.MemorySpace.HBM)
LIMIT = 24 << 20
GROUP = 6
NEAR, FAR, LEFT, RIGHT, FAR_LEFT, FAR_RIGHT, LEFT_NEXT, RIGHT_NEXT, RELAY, EDGE_LEFT, EDGE_RIGHT = range(11)
DIAGONAL = (FAR_LEFT, FAR_RIGHT, EDGE_LEFT, EDGE_RIGHT)


def dft_tables(length):
    index = np.arange(length)
    angle = (np.outer(index, index) % length) * (2.0 * math.pi / length)
    cosine, sine = np.cos(angle) / math.sqrt(length), np.sin(angle) / math.sqrt(length)
    table = np.block([[cosine, -sine], [sine, cosine]])
    high = table.astype(jnp.bfloat16)
    low = (table - high.astype(np.float64)).astype(jnp.bfloat16)
    return np.stack([high, low, high.T, low.T])


def swap(x):
    return pltpu.roll(x, 64, x.ndim - 1)


def lower(rows):
    return lax.broadcasted_iota(jnp.int32, (rows, 128), 1) < 64


def pack(x, keep_low):
    rows = x.shape[0] // 2
    keep = lower(rows) if keep_low else ~lower(rows)
    return jnp.where(keep, x[:rows], swap(x[rows:]))


def unpack(x):
    return jnp.concatenate([x, swap(x)], axis=0)


def merge(a, b):
    keep = lower(a.shape[0])
    return jnp.concatenate([jnp.where(keep, a, b), jnp.where(keep, swap(a), swap(b))], axis=0)


class Place:
    def __init__(self, grid):
        self.row, self.col = lax.axis_index("row"), lax.axis_index("col")
        self.odd = lax.rem(self.row, 2)
        self.near_row = self.row + 1 - 2 * self.odd
        self.far_row = self.row - 1 + 2 * self.odd
        self.grid = grid
        far = (self.far_row >= 0) & (self.far_row < grid[0])
        left, right = self.col > 0, self.col < grid[1] - 1
        self.far, self.left, self.right = far, left, right
        ends = (far & jnp.logical_not(left), far & jnp.logical_not(right))
        both = (None, far, left, right, far & left, far & right, left, right, None) + ends
        self.sends = both
        order = (NEAR, FAR, RIGHT, LEFT, FAR_RIGHT, FAR_LEFT, RIGHT_NEXT, LEFT_NEXT, RELAY, EDGE_LEFT, EDGE_RIGHT)
        self.gets = tuple(both[i] for i in order)
        self.near_border = self.pick(320, 0)
        self.far_border = self.pick(0, 320)
        self.near_halo = self.pick(448, 0)
        self.far_halo = self.pick(0, 448)

    def pick(self, even, odd):
        return pl.multiple_of(even + self.odd * (odd - even), 64)

    def target(self, which):
        row = {NEAR: self.near_row, RELAY: self.near_row, FAR: self.far_row}
        row.update({which: self.far_row for which in DIAGONAL})
        side = {LEFT: -1, FAR_LEFT: -1, LEFT_NEXT: -1, RIGHT: 1, FAR_RIGHT: 1, RIGHT_NEXT: 1}
        return {"row": row.get(which, self.row), "col": self.col + side.get(which, 0)}


def when(condition, body):
    if condition is None:
        body()
    else:
        pl.when(condition)(body)


def greet(place):
    barrier = pltpu.get_barrier_semaphore()
    for which in (NEAR, FAR, LEFT, RIGHT, FAR_LEFT, FAR_RIGHT):
        when(
            place.sends[which],
            lambda: pl.semaphore_signal(
                barrier, inc=1, device_id=place.target(which), device_id_type=MESH
            ),
        )


def greeted(place):
    far, left, right = (jnp.where(x, 1, 0) for x in (place.far, place.left, place.right))
    pl.semaphore_wait(pltpu.get_barrier_semaphore(), 1 + far + (left + right) * (1 + far))


def greet_all(place):
    barrier = pltpu.get_barrier_semaphore()
    count = 0
    for d in AROUND:
        count += jnp.where(beside(place, d), 1, 0)

        @pl.when(beside(place, d))
        def _():
            pl.semaphore_signal(
                barrier, inc=1, device_id={"row": place.row + d[0], "col": place.col + d[1]}, device_id_type=MESH
            )

    return count


def beside(place, d):
    row, col = place.row + d[0], place.col + d[1]
    return (row >= 0) & (row < place.grid[0]) & (col >= 0) & (col < place.grid[1])


def remote(place, which, src, dst, sems, p):
    return pltpu.make_async_remote_copy(
        src, dst, sems.at[0, p, which], sems.at[1, p, which], device_id=place.target(which), device_id_type=MESH
    )


def start(place, copies, *which):
    for i in which:
        when(place.sends[i], copies[i].start)


def wait_recv(place, copies, *which):
    for i in which:
        when(place.gets[i], copies[i].wait_recv)


def wait_send(place, copies):
    for i, copy in enumerate(copies):
        when(place.sends[i], copy.wait_send)


def strips(far, far_in, side, side_in, corner, corner_in, p):
    return {
        FAR: (far.at[p], far_in.at[p]),
        FAR_LEFT: (corner.at[0, p], corner_in.at[0, p]),
        FAR_RIGHT: (corner.at[1, p], corner_in.at[1, p]),
        EDGE_LEFT: (corner.at[0, p], corner_in.at[1, p]),
        EDGE_RIGHT: (corner.at[1, p], corner_in.at[0, p]),
        LEFT: (side.at[0, p, 0:64], side_in.at[0, p, 0:64]),
        RIGHT: (side.at[1, p, 0:64], side_in.at[1, p, 0:64]),
        LEFT_NEXT: (side.at[0, p, 64:192], side_in.at[0, p, 64:192]),
        RIGHT_NEXT: (side.at[1, p, 64:192], side_in.at[1, p, 64:192]),
    }


def at_rows(first, rows):
    return pl.ds(pl.multiple_of(first, 64), rows)


class Halo:
    def __init__(self, place, ext, far, side, corner, far_in, side_in, corner_in, sems):
        self.place, self.ext, self.far, self.far_in = place, ext, far, far_in
        self.side, self.corner, self.side_in, self.corner_in = side, corner, side_in, corner_in
        near, target = at_rows(place.near_border + 64, 64), at_rows(place.far_halo, 64)
        self.copies = []
        for p in range(2):
            ends = strips(far, far_in, side, side_in, corner, corner_in, p)
            ends[NEAR] = (ext.at[p, near, 0:384], ext.at[p, target, 0:384])
            ends[RELAY] = (ext.at[p, near, 384:512], ext.at[p, target, 384:512])
            self.copies.append([remote(place, i, *ends[i], sems, p) for i in range(11)])

    def clear(self):
        place = self.place

        @pl.when(jnp.logical_not(place.far))
        def _():
            self.far_in[...] = jnp.zeros((2, 64, 256), jnp.float32)
            self.corner_in[...] = jnp.zeros((2, 2, 64, 128), jnp.float32)

        for k, side in enumerate((place.right, place.left)):

            @pl.when(jnp.logical_not(side))
            def _():
                self.side_in[k] = jnp.zeros((2, 192, 128), jnp.float32)

    def pack(self, p):
        place, ext = self.place, self.ext
        for k, lane in enumerate((0, 256)):
            for i, first in enumerate((place.near_border, place.far_border)):
                self.side[k, p, 32 * i : 32 * i + 32] = pack(ext[p, at_rows(first + 64, 64), lane : lane + 128], k == 0)
            self.side[k, p, 64:192] = pack(ext[p, 128:384, lane : lane + 128], k == 0)
        rows = at_rows(place.far_border + 64, 64)
        self.far[p, :, 0:128] = ext[p, rows, 128:256]
        self.far[p, :, 128:256] = jnp.where(lower(64), ext[p, rows, 256:384], ext[p, rows, 0:128])

    def start(self, p):
        start(self.place, self.copies[p], LEFT, RIGHT, FAR)

    def start_rest(self):
        for p in range(2):
            start(self.place, self.copies[p], LEFT_NEXT, RIGHT_NEXT, NEAR)

    def forward(self):
        place, ext, low = self.place, self.ext, lower(64)
        for p in range(2):
            wait_recv(place, self.copies[p], LEFT, RIGHT)
            for i, first in enumerate((place.near_border, place.far_border)):
                parts = [self.side_in[k, p, 32 * i : 32 * i + 32] for k in range(2)]
                ext[p, at_rows(first + 64, 64), 384:512] = merge(*parts)
            start(place, self.copies[p], RELAY)
            rows = at_rows(place.far_border + 64, 64)
            self.corner[0, p] = jnp.where(low, ext[p, rows, 0:128], ext[p, rows, 384:512])
            self.corner[1, p] = jnp.where(low, ext[p, rows, 384:512], ext[p, rows, 256:384])
            start(place, self.copies[p], *DIAGONAL)

    def finish(self):
        place, ext, low = self.place, self.ext, lower(64)
        for p in range(2):
            wait_recv(place, self.copies[p], LEFT_NEXT, RIGHT_NEXT)
            ext[p, 128:384, 384:512] = merge(self.side_in[0, p, 64:192], self.side_in[1, p, 64:192])
            wait_recv(place, self.copies[p], FAR, *DIAGONAL)
            rows = at_rows(place.far_halo, 64)
            right, left = self.corner_in[0, p], self.corner_in[1, p]
            mixed = self.far_in[p, :, 128:256]
            ext[p, rows, 0:128] = jnp.where(low, left, mixed)
            ext[p, rows, 128:256] = self.far_in[p, :, 0:128]
            ext[p, rows, 256:384] = jnp.where(low, mixed, right)
            ext[p, rows, 384:512] = jnp.where(low, right, left)
        for p in range(2):
            wait_recv(place, self.copies[p], NEAR, RELAY)
            wait_send(place, self.copies[p])


class Fold:
    def __init__(self, place, update, near_in, relay_in, far, side, corner, far_in, side_in, corner_in, sems):
        self.place, self.update, self.near_in, self.relay_in = place, update, near_in, relay_in
        self.far, self.far_in = far, far_in
        self.side, self.corner, self.side_in, self.corner_in = side, corner, side_in, corner_in
        near = at_rows(place.near_halo, 64)
        self.copies = []
        for p in range(2):
            ends = strips(far, far_in, side, side_in, corner, corner_in, p)
            ends[NEAR] = (update.at[p, near, 0:384], near_in.at[p])
            ends[RELAY] = (update.at[p, near, 384:512], relay_in.at[p])
            self.copies.append([remote(place, i, *ends[i], sems, p) for i in range(11)])

    def pack(self):
        place, update, low = self.place, self.update, lower(64)

        @pl.when(jnp.logical_not(place.far))
        def _():
            self.corner_in[...] = jnp.zeros((2, 2, 64, 128), jnp.float32)

        rows = at_rows(place.far_halo, 64)
        for p in range(2):
            tiles = [update[p, rows, 128 * t : 128 * t + 128] for t in range(4)]
            self.corner[0, p] = jnp.where(low, tiles[0], tiles[3])
            self.corner[1, p] = jnp.where(low, tiles[3], tiles[2])
            self.far[p, :, 0:128] = tiles[1]
            self.far[p, :, 128:256] = jnp.where(low, tiles[2], tiles[0])
            for k in range(2):
                self.side[k, p, 64:192] = pack(update[p, 128:384, 384:512], k == 1)

    def start(self):
        place, update = self.place, self.update
        for p in range(2):
            start(place, self.copies[p], *DIAGONAL, RELAY)
            if p == 0:
                start(place, self.copies[p], FAR, LEFT_NEXT, RIGHT_NEXT)
        start(place, self.copies[1], FAR)
        for p in range(2):
            wait_recv(place, self.copies[p], RELAY, *DIAGONAL)
            extra = (self.relay_in[p], jnp.where(lower(64), self.corner_in[0, p], self.corner_in[1, p]))
            for i, first in enumerate((place.near_border, place.far_border)):
                part = update[p, at_rows(first + 64, 64), 384:512] + extra[i]
                for k in range(2):
                    self.side[k, p, 32 * i : 32 * i + 32] = pack(part, k == 1)
            start(place, self.copies[p], LEFT, RIGHT)
            if p == 0:
                start(place, self.copies[1], LEFT_NEXT, RIGHT_NEXT)
        for p in range(2):
            start(place, self.copies[p], NEAR)

    def finish(self, p, dest, base, inverse):
        place = self.place

        def add(first, lane, value):
            lanes, rows = pl.ds(lane, value.shape[1]), value.shape[0]
            dest[p, at_rows(first + base, rows), lanes] += value * inverse[at_rows(first, rows), lanes]

        def lowest(value):
            return jnp.where(lower(value.shape[0]), value, 0.0)

        def highest(value):
            return jnp.where(lower(value.shape[0]), 0.0, value)

        wait_recv(place, self.copies[p], NEAR)
        add(place.near_border, 0, self.near_in[p])

        @pl.when(place.far)
        def _():
            self.copies[p][FAR].wait_recv()
            mixed = self.far_in[p, :, 128:256]
            add(place.far_border, 0, jnp.where(lower(64), self.corner_in[1, p], mixed))
            add(place.far_border, 128, self.far_in[p, :, 0:128])
            add(place.far_border, 256, jnp.where(lower(64), mixed, self.corner_in[0, p]))

        for k, (here, lane, keep) in enumerate(((place.right, 256, highest), (place.left, 0, lowest))):

            @pl.when(here)
            def _():
                self.copies[p][LEFT_NEXT + k].wait_recv()
                add(64, lane, keep(unpack(self.side_in[k, p, 64:192])))
                self.copies[p][LEFT + k].wait_recv()
                add(place.near_border, lane, keep(unpack(self.side_in[k, p, 0:32])))
                add(place.far_border, lane, keep(unpack(self.side_in[k, p, 32:64])))

    def close(self):
        for p in range(2):
            wait_send(self.place, self.copies[p])


def spread_kernel(grid):
    def kernel(
        field, offsets, counts, places, measured, tables, probe,
        ext, around, measured_here, tables_here, beams, power, update, light,
        mine, offsets_here, tall, far, side, corner, far_in, side_in, corner_in, sems, notes, local,
    ):
        place = Place(grid)
        peers = greet_all(place)
        pulls = [pltpu.make_async_copy(offsets, offsets_here, local.at[0])]
        pulls += [pltpu.make_async_copy(field.at[p], ext.at[p, 64:448, 0:384], local.at[1 + p]) for p in range(2)]
        later = [
            pltpu.make_async_copy(measured, measured_here, local.at[3]),
            pltpu.make_async_copy(tables, tables_here, local.at[4]),
        ]
        pulls.append(pltpu.make_async_copy(probe, tall.at[:, 8:136], local.at[5]))
        for pull in pulls:
            pull.start()
        halo = Halo(place, ext, far, side, corner, far_in, side_in, corner_in, sems)
        halo.clear()
        for i, d in enumerate(AROUND):

            @pl.when(jnp.logical_not(beside(place, d)))
            def _():
                around[i] = jnp.zeros((8, 128), jnp.int32)

        pulls[0].wait()
        mine[0:2, 0:12] = offsets_here[0, 0]
        mine[2:3, 0:1] = jnp.full((1, 1), counts[0, 0], jnp.int32)
        around[8] = mine[...]
        letters = []
        for i, d in enumerate(AROUND):
            letter = pltpu.make_async_remote_copy(
                mine,
                around.at[AROUND.index((-d[0], -d[1]))],
                notes.at[0, i],
                notes.at[1, i],
                device_id={"row": place.row + d[0], "col": place.col + d[1]},
                device_id_type=MESH,
            )
            letters.append(letter)
        pulls[1].wait()
        halo.pack(0)
        pl.semaphore_wait(pltpu.get_barrier_semaphore(), peers)
        for i, d in enumerate(AROUND):
            pl.when(beside(place, d))(letters[i].start)
        halo.start(0)
        pulls[2].wait()
        halo.pack(1)
        halo.start(1)
        halo.start_rest()
        for pull in later:
            pull.start()
        update[...] = jnp.zeros_like(update)
        halo.forward()
        light[...] = jnp.zeros_like(light)
        pulls[3].wait()
        for p in range(2):
            tall[p, 0:8] = tall[p, 128:136]
        power[...] = tall[0] * tall[0] + tall[1] * tall[1]

        def turn(slot, carry):
            live = (slot < counts[0, 0]).astype(jnp.float32)
            low_row, low_col = places[0, 0, 0, slot] & 7, places[0, 0, 1, slot] & 127
            for p in range(2):
                beams[slot, p] = pltpu.roll(tall[p, pl.ds(8 - low_row, 128), :], low_col, 1) * live
            return carry

        lax.fori_loop(0, 12, turn, 0)
        halo.finish()
        for i, d in enumerate(AROUND):
            pl.when(beside(place, d))(letters[i].wait_send)
            pl.when(beside(place, (-d[0], -d[1])))(letters[i].wait_recv)
        for pull in later:
            pull.wait()

    return kernel


def split(x):
    high = x.astype(jnp.bfloat16)
    return high, (x - high.astype(jnp.float32)).astype(jnp.bfloat16)


def dot(a, b):
    return jnp.dot(a, b, preferred_element_type=jnp.float32)


def right_mul(x, high, low):
    xh, xl = split(x)
    return dot(xh, high) + dot(xl, high) + dot(xh, low)


def left_mul(high, low, x):
    xh, xl = split(x)
    return dot(high, xh) + dot(high, xl) + dot(low, xh)


def cross(x):
    return jnp.concatenate(
        [
            jnp.concatenate([x[:128, :128], x[128:, :128]], axis=1),
            jnp.concatenate([x[:128, 128:], x[128:, 128:]], axis=1),
        ],
        axis=0,
    )


def gradient_kernel(with_light):
    def kernel(*refs):
        if with_light:
            around, ext, beams, measured, tables, _, power, _, update, light = refs
        else:
            around, ext, beams, measured, tables, _, update = refs
        count = around[8, 2, 0]
        lane = lax.broadcasted_iota(jnp.int32, (128, 128), 1)
        sub = lax.broadcasted_iota(jnp.int32, (8, 128), 0)

        def turned(source, shift_rows, shift_lanes):
            return pltpu.roll(source[pl.ds(8 - shift_rows, 128), :], shift_lanes, 1)

        def scatter(dest, first, lanes, shift_rows, shift_lanes, value):
            head = jnp.where(sub >= shift_rows, value[:8], 0.0)
            main = jnp.concatenate([head, value[8:]], axis=0)
            tail = jnp.where(sub < shift_rows, value[:8], 0.0)
            for which, at in enumerate(lanes):
                keep = lane >= shift_lanes if which == 0 else lane < shift_lanes
                dest[pl.ds(first, 128), at] += jnp.where(keep, main, 0.0)
                dest[pl.ds(first + 128, 8), at] += jnp.where(keep[:8], tail, 0.0)

        def tiles_of(col, base, wrap):
            tile = lax.shift_right_arithmetic(col, 7) + base
            first = lax.rem(tile + wrap, wrap)
            second = lax.rem(tile + wrap + 1, wrap)
            return [pl.ds(pl.multiple_of(t * 128, 128), 128) for t in (first, second)]

        def brighten(row, col, value):
            low_row, low_col = jnp.bitwise_and(row, 7), jnp.bitwise_and(col, 127)
            first = pl.multiple_of(row - low_row + 128, 8)
            scatter(light, first, tiles_of(col, 1, 5), low_row, low_col, value)

        def gather(slot):
            row, col = around[8, 0, slot], around[8, 1, slot]
            low_row, low_col = jnp.bitwise_and(row, 7), jnp.bitwise_and(col, 127)
            first = pl.multiple_of(row - low_row + 64, 8)
            lanes = tiles_of(col, 0, 4)
            beam = [beams[slot, p] for p in range(2)]
            window = []
            for p in range(2):
                main = jnp.where(
                    lane >= low_col, ext[p, pl.ds(first, 128), lanes[0]], ext[p, pl.ds(first, 128), lanes[1]]
                )
                tail = jnp.where(
                    lane[:8] >= low_col,
                    ext[p, pl.ds(first + 128, 8), lanes[0]],
                    ext[p, pl.ds(first + 128, 8), lanes[1]],
                )
                window.append(jnp.concatenate([jnp.where(sub >= low_row, main[:8], tail), main[8:]], axis=0))
            real = beam[0] * window[0] - beam[1] * window[1]
            imag = beam[0] * window[1] + beam[1] * window[0]
            return jnp.concatenate([real, imag], axis=1), (slot, first, lanes, low_row, low_col, row, col)

        def put(back, at):
            slot, first, lanes, low_row, low_col, row, col = at
            beam = [beams[slot, p] for p in range(2)]
            real, imag = back[:, :128], back[:, 128:]
            scatter(update.at[0], first, lanes, low_row, low_col, beam[0] * real + beam[1] * imag)
            scatter(update.at[1], first, lanes, low_row, low_col, beam[0] * imag - beam[1] * real)
            if with_light:
                brighten(row, col, beam[0] * beam[0] + beam[1] * beam[1])

        def some(step, carry):
            slots = [step * GROUP + k for k in range(GROUP)]
            pairs = [(k, k + 1) for k in range(0, GROUP, 2)]
            gathered = [gather(slot) for slot in slots]
            waves = [jnp.concatenate([gathered[a][0], gathered[b][0]], axis=0) for a, b in pairs]
            half = [cross(right_mul(wave, tables[0], tables[1])) for wave in waves]
            far = [left_mul(tables[2], tables[3], x) for x in half]
            change = []
            for x, (a, b) in zip(far, pairs):
                real, imag = x[:128], x[128:]
                known = jnp.concatenate([measured[0, 0, slots[a]], measured[0, 0, slots[b]]], axis=1)
                ratio = known * lax.rsqrt(real * real + imag * imag + 0.25) - 1.0
                change.append(jnp.concatenate([real * ratio, imag * ratio], axis=0))
            half = [cross(left_mul(tables[0], tables[1], x)) for x in change]
            back = [right_mul(x, tables[2], tables[3]) for x in half]
            for x, (a, b) in zip(back, pairs):
                put(x[:128], gathered[a][1])
                put(x[128:], gathered[b][1])
            return carry

        lax.fori_loop(0, (count + GROUP - 1) // GROUP, some, 0)
        if with_light:
            for i, d in enumerate(AROUND):

                def other(slot, carry):
                    row = around[i, 0, slot] + d[0] * 384
                    col = around[i, 1, slot] + d[1] * 384
                    touches = (row > -128) & (row < 384) & (col > -128) & (col < 384)

                    @pl.when(touches)
                    def _():
                        low_row, low_col = jnp.bitwise_and(row, 7), jnp.bitwise_and(col, 127)
                        brighten(row, col, turned(power, low_row, low_col))

                    return carry

                lax.fori_loop(0, around[i, 2, 0], other, 0)

    return kernel


def between_kernel(grid):
    def kernel(
        update, light, field,
        ext, cleared, inverse,
        near_in, relay_in, far, side, corner, far_in, side_in, corner_in, sems,
        halo_far, halo_side, halo_corner, halo_far_in, halo_side_in, halo_corner_in, more,
    ):
        place = Place(grid)
        greet(place)
        fold = Fold(place, update, near_in, relay_in, far, side, corner, far_in, side_in, corner_in, sems)
        halo = Halo(place, ext, halo_far, halo_side, halo_corner, halo_far_in, halo_side_in, halo_corner_in, more)
        fold.pack()
        greeted(place)
        fold.start()
        halo.clear()
        inverse[...] = 1.0 / (light[128:512, 128:512] + 1.0)
        for p in range(2):
            ext[p, 64:448, 0:384] = field[p, 64:448, 0:384] + update[p, 64:448, 0:384] * inverse[...]
        cleared[...] = jnp.zeros_like(cleared)
        for p in range(2):
            fold.finish(p, ext, 64, inverse)
            halo.pack(p)
            halo.start(p)
        halo.start_rest()
        halo.forward()
        halo.finish()
        fold.close()

    return kernel


def last_kernel(grid):
    def kernel(update, inverse, ext, out, near_in, relay_in, far, side, corner, far_in, side_in, corner_in, sems):
        place = Place(grid)
        greet(place)
        fold = Fold(place, update, near_in, relay_in, far, side, corner, far_in, side_in, corner_in, sems)
        fold.pack()
        greeted(place)
        fold.start()
        for p in range(2):
            out[p] = ext[p, 64:448, 0:384] + update[p, 64:448, 0:384] * inverse[...]
        for p in range(2):
            fold.finish(p, out, 0, inverse)
        fold.close()

    return kernel


def hold(x):
    return pltpu.with_memory_space_constraint(x, pltpu.MemorySpace.HBM)


def params(collective_id=None):
    if collective_id is None:
        return pltpu.CompilerParams(vmem_limit_bytes=LIMIT)
    return pltpu.CompilerParams(collective_id=collective_id, has_side_effects=True, vmem_limit_bytes=LIMIT)


def shards(grid, tables, object_field, probe, amplitudes, offsets, counts):
    f32, i32 = jnp.float32, jnp.int32
    shape = jax.ShapeDtypeStruct
    ext_shape, light_shape = shape((2, 512, 512), f32), shape((648, 640), f32)
    offsets = jnp.swapaxes(offsets, 2, 3)
    packs = [pltpu.VMEM((2, 64, 256), f32), pltpu.VMEM((2, 2, 192, 128), f32), pltpu.VMEM((2, 2, 64, 128), f32)]
    folds = [pltpu.VMEM((2, 64, 384), f32), pltpu.VMEM((2, 64, 128), f32)] + packs + packs
    sems = pltpu.SemaphoreType.DMA((2, 2, 11))
    ext, around, measured, tables, beams, power, update, light = pl.pallas_call(
        spread_kernel(grid),
        name="spread",
        out_shape=(
            ext_shape,
            shape((9, 8, 128), i32),
            shape(amplitudes.shape, f32),
            shape(tables.shape, tables.dtype),
            shape((12, 2, 128, 128), f32),
            shape((136, 128), f32),
            ext_shape,
            light_shape,
        ),
        in_specs=[HBM, HBM, SMEM, SMEM, HBM, HBM, HBM],
        out_specs=(VMEM,) * 8,
        scratch_shapes=[pltpu.VMEM((8, 128), i32), pltpu.VMEM((1, 1, 2, 12), i32), pltpu.VMEM((2, 136, 128), f32)]
        + packs
        + packs
        + [sems, pltpu.SemaphoreType.DMA((2, 8)), pltpu.SemaphoreType.DMA((6,))],
        compiler_params=params(0),
    )(hold(object_field), hold(offsets), counts, offsets, hold(amplitudes), hold(tables), hold(probe))
    update, light = pl.pallas_call(
        gradient_kernel(True),
        name="gradient_light",
        out_shape=(ext_shape, light_shape),
        in_specs=[SMEM] + [VMEM] * 7,
        out_specs=(VMEM,) * 2,
        input_output_aliases={5: 0, 7: 1},
        compiler_params=params(),
    )(around, ext, beams, measured, tables, update, power, light)
    ext, cleared, inverse = pl.pallas_call(
        between_kernel(grid),
        name="between",
        out_shape=(ext_shape, ext_shape, shape((384, 384), f32)),
        in_specs=[VMEM] * 3,
        out_specs=(VMEM,) * 3,
        scratch_shapes=folds + [sems] + packs + packs + [sems],
        compiler_params=params(1),
    )(update, light, ext)
    update = pl.pallas_call(
        gradient_kernel(False),
        name="gradient",
        out_shape=ext_shape,
        in_specs=[SMEM] + [VMEM] * 5,
        out_specs=VMEM,
        input_output_aliases={5: 0},
        compiler_params=params(),
    )(around, ext, beams, measured, tables, cleared)
    return pl.pallas_call(
        last_kernel(grid),
        name="last",
        out_shape=shape((2, 384, 384), f32),
        in_specs=[VMEM] * 3,
        out_specs=VMEM,
        scratch_shapes=folds + [sems],
        compiler_params=params(2),
    )(update, inverse, ext)


def solution(mesh):
    grid = (mesh.shape["row"], mesh.shape["col"])
    tables = dft_tables(128)
    placed = (
        P(None, "row", "col"),
        P(),
        P("row", "col", None, None, None),
        P("row", "col", None, None),
        P("row", "col"),
    )

    def body(*args):
        return shards(grid, jnp.asarray(tables), *args)

    return jax.shard_map(body, mesh=mesh, in_specs=placed, out_specs=P(None, "row", "col"), check_vma=False)
```

```python
import math

import jax
import jax.numpy as jnp
import numpy as np
from jax import lax
from jax.experimental import pallas as pl
from jax.experimental.pallas import tpu as pltpu
from jax.sharding import PartitionSpec as P

AROUND = ((-1, 0), (1, 0), (0, -1), (0, 1), (-1, -1), (-1, 1), (1, -1), (1, 1))
MESH = pl.DeviceIdType.MESH
VMEM = pl.BlockSpec(memory_space=pltpu.VMEM)
SMEM = pl.BlockSpec(memory_space=pltpu.SMEM)
HBM = pl.BlockSpec(memory_space=pltpu.MemorySpace.HBM)
LIMIT = 24 << 20
GROUP = 6
NEAR, FAR, LEFT, RIGHT, FAR_LEFT, FAR_RIGHT, LEFT_NEXT, RIGHT_NEXT, RELAY, EDGE_LEFT, EDGE_RIGHT = range(11)
DIAGONAL = (FAR_LEFT, FAR_RIGHT, EDGE_LEFT, EDGE_RIGHT)


def dft_tables(length):
    index = np.arange(length)
    angle = (np.outer(index, index) % length) * (2.0 * math.pi / length)
    cosine, sine = np.cos(angle) / math.sqrt(length), np.sin(angle) / math.sqrt(length)
    table = np.block([[cosine, -sine], [sine, cosine]])
    high = table.astype(jnp.bfloat16)
    low = (table - high.astype(np.float64)).astype(jnp.bfloat16)
    return np.stack([high, low, high.T, low.T])


def swap(x):
    return pltpu.roll(x, 64, x.ndim - 1)


def lower(rows):
    return lax.broadcasted_iota(jnp.int32, (rows, 128), 1) < 64


def pack(x, keep_low):
    rows = x.shape[0] // 2
    keep = lower(rows) if keep_low else ~lower(rows)
    return jnp.where(keep, x[:rows], swap(x[rows:]))


def unpack(x):
    return jnp.concatenate([x, swap(x)], axis=0)


def merge(a, b):
    keep = lower(a.shape[0])
    return jnp.concatenate([jnp.where(keep, a, b), jnp.where(keep, swap(a), swap(b))], axis=0)


class Place:
    def __init__(self, grid):
        self.row, self.col = lax.axis_index("row"), lax.axis_index("col")
        self.odd = lax.rem(self.row, 2)
        self.near_row = self.row + 1 - 2 * self.odd
        self.far_row = self.row - 1 + 2 * self.odd
        self.grid = grid
        far = (self.far_row >= 0) & (self.far_row < grid[0])
        left, right = self.col > 0, self.col < grid[1] - 1
        self.far, self.left, self.right = far, left, right
        ends = (far & jnp.logical_not(left), far & jnp.logical_not(right))
        both = (None, far, left, right, far & left, far & right, left, right, None) + ends
        self.sends = both
        order = (NEAR, FAR, RIGHT, LEFT, FAR_RIGHT, FAR_LEFT, RIGHT_NEXT, LEFT_NEXT, RELAY, EDGE_LEFT, EDGE_RIGHT)
        self.gets = tuple(both[i] for i in order)
        self.near_border = self.pick(320, 0)
        self.far_border = self.pick(0, 320)
        self.near_halo = self.pick(448, 0)
        self.far_halo = self.pick(0, 448)

    def pick(self, even, odd):
        return pl.multiple_of(even + self.odd * (odd - even), 64)

    def target(self, which):
        row = {NEAR: self.near_row, RELAY: self.near_row, FAR: self.far_row}
        row.update({which: self.far_row for which in DIAGONAL})
        side = {LEFT: -1, FAR_LEFT: -1, LEFT_NEXT: -1, RIGHT: 1, FAR_RIGHT: 1, RIGHT_NEXT: 1}
        return {"row": row.get(which, self.row), "col": self.col + side.get(which, 0)}


def when(condition, body):
    if condition is None:
        body()
    else:
        pl.when(condition)(body)


def greet(place):
    barrier = pltpu.get_barrier_semaphore()
    for which in (NEAR, FAR, LEFT, RIGHT, FAR_LEFT, FAR_RIGHT):
        when(
            place.sends[which],
            lambda: pl.semaphore_signal(
                barrier, inc=1, device_id=place.target(which), device_id_type=MESH
            ),
        )


def greeted(place):
    far, left, right = (jnp.where(x, 1, 0) for x in (place.far, place.left, place.right))
    pl.semaphore_wait(pltpu.get_barrier_semaphore(), 1 + far + (left + right) * (1 + far))


def greet_all(place):
    barrier = pltpu.get_barrier_semaphore()
    count = 0
    for d in AROUND:
        count += jnp.where(beside(place, d), 1, 0)

        @pl.when(beside(place, d))
        def _():
            pl.semaphore_signal(
                barrier, inc=1, device_id={"row": place.row + d[0], "col": place.col + d[1]}, device_id_type=MESH
            )

    return count


def beside(place, d):
    row, col = place.row + d[0], place.col + d[1]
    return (row >= 0) & (row < place.grid[0]) & (col >= 0) & (col < place.grid[1])


def remote(place, which, src, dst, sems, p):
    return pltpu.make_async_remote_copy(
        src, dst, sems.at[0, p, which], sems.at[1, p, which], device_id=place.target(which), device_id_type=MESH
    )


def start(place, copies, *which):
    for i in which:
        when(place.sends[i], copies[i].start)


def wait_recv(place, copies, *which):
    for i in which:
        when(place.gets[i], copies[i].wait_recv)


def wait_send(place, copies, gone, *which):
    for i in which or range(len(copies)):
        if i not in gone:
            when(place.sends[i], copies[i].wait_send)
    gone.update(which or range(len(copies)))


def strips(far, far_in, side, side_in, corner, corner_in, p):
    return {
        FAR: (far.at[p], far_in.at[p]),
        FAR_LEFT: (corner.at[0, p], corner_in.at[0, p]),
        FAR_RIGHT: (corner.at[1, p], corner_in.at[1, p]),
        EDGE_LEFT: (corner.at[0, p], corner_in.at[1, p]),
        EDGE_RIGHT: (corner.at[1, p], corner_in.at[0, p]),
        LEFT: (side.at[0, p, 0:64], side_in.at[0, p, 0:64]),
        RIGHT: (side.at[1, p, 0:64], side_in.at[1, p, 0:64]),
        LEFT_NEXT: (side.at[0, p, 64:192], side_in.at[0, p, 64:192]),
        RIGHT_NEXT: (side.at[1, p, 64:192], side_in.at[1, p, 64:192]),
    }


def at_rows(first, rows):
    return pl.ds(pl.multiple_of(first, 64), rows)


class Halo:
    def __init__(self, place, ext, far, side, corner, far_in, side_in, corner_in, sems):
        self.place, self.ext, self.far, self.far_in = place, ext, far, far_in
        self.gone = (set(), set())
        self.side, self.corner, self.side_in, self.corner_in = side, corner, side_in, corner_in
        near, target = at_rows(place.near_border + 64, 64), at_rows(place.far_halo, 64)
        self.copies = []
        for p in range(2):
            ends = strips(far, far_in, side, side_in, corner, corner_in, p)
            ends[NEAR] = (ext.at[p, near, 0:384], ext.at[p, target, 0:384])
            ends[RELAY] = (ext.at[p, near, 384:512], ext.at[p, target, 384:512])
            self.copies.append([remote(place, i, *ends[i], sems, p) for i in range(11)])

    def clear(self):
        place = self.place

        @pl.when(jnp.logical_not(place.far))
        def _():
            self.far_in[...] = jnp.zeros((2, 64, 256), jnp.float32)
            self.corner_in[...] = jnp.zeros((2, 2, 64, 128), jnp.float32)

        for k, side in enumerate((place.right, place.left)):

            @pl.when(jnp.logical_not(side))
            def _():
                self.side_in[k] = jnp.zeros((2, 192, 128), jnp.float32)

    def pack(self, p):
        place, ext = self.place, self.ext
        for k, lane in enumerate((0, 256)):
            for i, first in enumerate((place.near_border, place.far_border)):
                self.side[k, p, 32 * i : 32 * i + 32] = pack(ext[p, at_rows(first + 64, 64), lane : lane + 128], k == 0)
            self.side[k, p, 64:192] = pack(ext[p, 128:384, lane : lane + 128], k == 0)
        rows = at_rows(place.far_border + 64, 64)
        self.far[p, :, 0:128] = ext[p, rows, 128:256]
        self.far[p, :, 128:256] = jnp.where(lower(64), ext[p, rows, 256:384], ext[p, rows, 0:128])

    def start(self, p):
        start(self.place, self.copies[p], LEFT, RIGHT, FAR)

    def start_rest(self, p):
        wait_send(self.place, self.copies[p], self.gone[p], LEFT, RIGHT)
        start(self.place, self.copies[p], LEFT_NEXT, RIGHT_NEXT, NEAR)

    def forward(self):
        place, ext, low = self.place, self.ext, lower(64)
        for p in range(2):
            wait_recv(place, self.copies[p], LEFT, RIGHT)
            for i, first in enumerate((place.near_border, place.far_border)):
                parts = [self.side_in[k, p, 32 * i : 32 * i + 32] for k in range(2)]
                ext[p, at_rows(first + 64, 64), 384:512] = merge(*parts)
            start(place, self.copies[p], RELAY)
            rows = at_rows(place.far_border + 64, 64)
            self.corner[0, p] = jnp.where(low, ext[p, rows, 0:128], ext[p, rows, 384:512])
            self.corner[1, p] = jnp.where(low, ext[p, rows, 384:512], ext[p, rows, 256:384])
            start(place, self.copies[p], *DIAGONAL)

    def finish(self):
        place, ext, low = self.place, self.ext, lower(64)
        for p in range(2):
            wait_recv(place, self.copies[p], LEFT_NEXT, RIGHT_NEXT)
            ext[p, 128:384, 384:512] = merge(self.side_in[0, p, 64:192], self.side_in[1, p, 64:192])
            wait_recv(place, self.copies[p], FAR, *DIAGONAL)
            rows = at_rows(place.far_halo, 64)
            right, left = self.corner_in[0, p], self.corner_in[1, p]
            mixed = self.far_in[p, :, 128:256]
            ext[p, rows, 0:128] = jnp.where(low, left, mixed)
            ext[p, rows, 128:256] = self.far_in[p, :, 0:128]
            ext[p, rows, 256:384] = jnp.where(low, mixed, right)
            ext[p, rows, 384:512] = jnp.where(low, right, left)
        for p in range(2):
            wait_recv(place, self.copies[p], NEAR, RELAY)
            wait_send(place, self.copies[p], self.gone[p])


class Fold:
    def __init__(self, place, update, near_in, relay_in, far, side, corner, far_in, side_in, corner_in, sems):
        self.place, self.update, self.near_in, self.relay_in = place, update, near_in, relay_in
        self.far, self.far_in = far, far_in
        self.gone = (set(), set())
        self.side, self.corner, self.side_in, self.corner_in = side, corner, side_in, corner_in
        near = at_rows(place.near_halo, 64)
        self.copies = []
        for p in range(2):
            ends = strips(far, far_in, side, side_in, corner, corner_in, p)
            ends[NEAR] = (update.at[p, near, 0:384], near_in.at[p])
            ends[RELAY] = (update.at[p, near, 384:512], relay_in.at[p])
            self.copies.append([remote(place, i, *ends[i], sems, p) for i in range(11)])

    def pack(self):
        place, update, low = self.place, self.update, lower(64)

        @pl.when(jnp.logical_not(place.far))
        def _():
            self.corner_in[...] = jnp.zeros((2, 2, 64, 128), jnp.float32)

        rows = at_rows(place.far_halo, 64)
        for p in range(2):
            tiles = [update[p, rows, 128 * t : 128 * t + 128] for t in range(4)]
            self.corner[0, p] = jnp.where(low, tiles[0], tiles[3])
            self.corner[1, p] = jnp.where(low, tiles[3], tiles[2])
            self.far[p, :, 0:128] = tiles[1]
            self.far[p, :, 128:256] = jnp.where(low, tiles[2], tiles[0])
            for k in range(2):
                self.side[k, p, 64:192] = pack(update[p, 128:384, 384:512], k == 1)

    def start(self, paced):
        place, update = self.place, self.update
        for p in range(2):
            start(place, self.copies[p], *DIAGONAL, RELAY)
        start(place, self.copies[0], FAR, LEFT_NEXT, RIGHT_NEXT)
        if not paced:
            start(place, self.copies[1], FAR)
        for p in range(2):
            wait_recv(place, self.copies[p], RELAY, *DIAGONAL)
            extra = (self.relay_in[p], jnp.where(lower(64), self.corner_in[0, p], self.corner_in[1, p]))
            for i, first in enumerate((place.near_border, place.far_border)):
                part = update[p, at_rows(first + 64, 64), 384:512] + extra[i]
                for k in range(2):
                    self.side[k, p, 32 * i : 32 * i + 32] = pack(part, k == 1)
            start(place, self.copies[p], LEFT, RIGHT)
            if p == 0 and paced:
                start(place, self.copies[0], NEAR)
                wait_send(place, self.copies[0], self.gone[0], FAR, LEFT_NEXT, RIGHT_NEXT)
                start(place, self.copies[1], FAR)
            if p == 0:
                start(place, self.copies[1], LEFT_NEXT, RIGHT_NEXT)
        if not paced:
            start(place, self.copies[0], NEAR)
        start(place, self.copies[1], NEAR)

    def finish(self, p, dest, base, inverse, between=None):
        place = self.place
        sides = ((place.right, 256, lambda x: jnp.where(lower(x.shape[0]), 0.0, x)), (place.left, 0, lambda x: jnp.where(lower(x.shape[0]), x, 0.0)))

        def add(first, lane, value):
            lanes, rows = pl.ds(lane, value.shape[1]), value.shape[0]
            dest[p, at_rows(first + base, rows), lanes] += value * inverse[at_rows(first, rows), lanes]

        wait_recv(place, self.copies[p], NEAR)
        add(place.near_border, 0, self.near_in[p])

        @pl.when(place.far)
        def _():
            self.copies[p][FAR].wait_recv()
            mixed = self.far_in[p, :, 128:256]
            add(place.far_border, 0, jnp.where(lower(64), self.corner_in[1, p], mixed))
            add(place.far_border, 128, self.far_in[p, :, 0:128])
            add(place.far_border, 256, jnp.where(lower(64), mixed, self.corner_in[0, p]))

        for k, (here, lane, keep) in enumerate(sides):

            @pl.when(here)
            def _():
                self.copies[p][LEFT_NEXT + k].wait_recv()
                add(64, lane, keep(unpack(self.side_in[k, p, 64:192])))

        if between is not None:
            between()
        for k, (here, lane, keep) in enumerate(sides):

            @pl.when(here)
            def _():
                self.copies[p][LEFT + k].wait_recv()
                add(place.near_border, lane, keep(unpack(self.side_in[k, p, 0:32])))
                add(place.far_border, lane, keep(unpack(self.side_in[k, p, 32:64])))

    def close(self):
        for p in range(2):
            wait_send(self.place, self.copies[p], self.gone[p])


def spread_kernel(grid):
    def kernel(
        field, offsets, counts, places, measured, tables, probe,
        ext, around, measured_here, tables_here, beams, power, update, light,
        mine, offsets_here, tall, far, side, corner, far_in, side_in, corner_in, sems, notes, local,
    ):
        place = Place(grid)
        peers = greet_all(place)
        pulls = [pltpu.make_async_copy(offsets, offsets_here, local.at[0])]
        pulls += [pltpu.make_async_copy(field.at[p], ext.at[p, 64:448, 0:384], local.at[1 + p]) for p in range(2)]
        later = [
            pltpu.make_async_copy(measured, measured_here, local.at[3]),
            pltpu.make_async_copy(tables, tables_here, local.at[4]),
        ]
        pulls.append(pltpu.make_async_copy(probe, tall.at[:, 8:136], local.at[5]))
        for pull in pulls:
            pull.start()
        halo = Halo(place, ext, far, side, corner, far_in, side_in, corner_in, sems)
        halo.clear()
        for i, d in enumerate(AROUND):

            @pl.when(jnp.logical_not(beside(place, d)))
            def _():
                around[i] = jnp.zeros((8, 128), jnp.int32)

        pulls[0].wait()
        mine[0:2, 0:12] = offsets_here[0, 0]
        mine[2:3, 0:1] = jnp.full((1, 1), counts[0, 0], jnp.int32)
        around[8] = mine[...]
        letters = []
        for i, d in enumerate(AROUND):
            letter = pltpu.make_async_remote_copy(
                mine,
                around.at[AROUND.index((-d[0], -d[1]))],
                notes.at[0, i],
                notes.at[1, i],
                device_id={"row": place.row + d[0], "col": place.col + d[1]},
                device_id_type=MESH,
            )
            letters.append(letter)
        pulls[1].wait()
        halo.pack(0)
        pl.semaphore_wait(pltpu.get_barrier_semaphore(), peers)
        for i, d in enumerate(AROUND):
            pl.when(beside(place, d))(letters[i].start)
        halo.start(0)
        pulls[2].wait()
        halo.pack(1)
        halo.start(1)
        halo.start_rest(0)
        halo.start_rest(1)
        for pull in later:
            pull.start()
        update[...] = jnp.zeros_like(update)
        halo.forward()
        light[...] = jnp.zeros_like(light)
        pulls[3].wait()
        for p in range(2):
            tall[p, 0:8] = tall[p, 128:136]
        power[...] = tall[0] * tall[0] + tall[1] * tall[1]

        def turn(slot, carry):
            live = (slot < counts[0, 0]).astype(jnp.float32)
            low_row, low_col = places[0, 0, 0, slot] & 7, places[0, 0, 1, slot] & 127
            for p in range(2):
                beams[slot, p] = pltpu.roll(tall[p, pl.ds(8 - low_row, 128), :], low_col, 1) * live
            return carry

        lax.fori_loop(0, 12, turn, 0)
        halo.finish()
        for i, d in enumerate(AROUND):
            pl.when(beside(place, d))(letters[i].wait_send)
            pl.when(beside(place, (-d[0], -d[1])))(letters[i].wait_recv)
        for pull in later:
            pull.wait()

    return kernel


def split(x):
    high = x.astype(jnp.bfloat16)
    return high, (x - high.astype(jnp.float32)).astype(jnp.bfloat16)


def dot(a, b):
    return jnp.dot(a, b, preferred_element_type=jnp.float32)


def right_mul(x, high, low):
    xh, xl = split(x)
    return dot(xh, high) + dot(xl, high) + dot(xh, low)


def left_mul(high, low, x):
    xh, xl = split(x)
    return dot(high, xh) + dot(high, xl) + dot(low, xh)


def cross(x):
    return jnp.concatenate(
        [
            jnp.concatenate([x[:128, :128], x[128:, :128]], axis=1),
            jnp.concatenate([x[:128, 128:], x[128:, 128:]], axis=1),
        ],
        axis=0,
    )


def gradient_kernel(with_light):
    def kernel(*refs):
        if with_light:
            around, ext, beams, measured, tables, _, power, _, update, light = refs
        else:
            around, ext, beams, measured, tables, _, update = refs
        count = around[8, 2, 0]
        lane = lax.broadcasted_iota(jnp.int32, (128, 128), 1)
        sub = lax.broadcasted_iota(jnp.int32, (8, 128), 0)

        def turned(source, shift_rows, shift_lanes):
            return pltpu.roll(source[pl.ds(8 - shift_rows, 128), :], shift_lanes, 1)

        def scatter(dest, first, lanes, shift_rows, shift_lanes, value):
            head = jnp.where(sub >= shift_rows, value[:8], 0.0)
            main = jnp.concatenate([head, value[8:]], axis=0)
            tail = jnp.where(sub < shift_rows, value[:8], 0.0)
            for which, at in enumerate(lanes):
                keep = lane >= shift_lanes if which == 0 else lane < shift_lanes
                dest[pl.ds(first, 128), at] += jnp.where(keep, main, 0.0)
                dest[pl.ds(first + 128, 8), at] += jnp.where(keep[:8], tail, 0.0)

        def tiles_of(col, base, wrap):
            tile = lax.shift_right_arithmetic(col, 7) + base
            first = lax.rem(tile + wrap, wrap)
            second = lax.rem(tile + wrap + 1, wrap)
            return [pl.ds(pl.multiple_of(t * 128, 128), 128) for t in (first, second)]

        def brighten(row, col, value):
            low_row, low_col = jnp.bitwise_and(row, 7), jnp.bitwise_and(col, 127)
            first = pl.multiple_of(row - low_row + 128, 8)
            scatter(light, first, tiles_of(col, 1, 5), low_row, low_col, value)

        def gather(slot):
            row, col = around[8, 0, slot], around[8, 1, slot]
            low_row, low_col = jnp.bitwise_and(row, 7), jnp.bitwise_and(col, 127)
            first = pl.multiple_of(row - low_row + 64, 8)
            lanes = tiles_of(col, 0, 4)
            beam = [beams[slot, p] for p in range(2)]
            window = []
            for p in range(2):
                main = jnp.where(
                    lane >= low_col, ext[p, pl.ds(first, 128), lanes[0]], ext[p, pl.ds(first, 128), lanes[1]]
                )
                tail = jnp.where(
                    lane[:8] >= low_col,
                    ext[p, pl.ds(first + 128, 8), lanes[0]],
                    ext[p, pl.ds(first + 128, 8), lanes[1]],
                )
                window.append(jnp.concatenate([jnp.where(sub >= low_row, main[:8], tail), main[8:]], axis=0))
            real = beam[0] * window[0] - beam[1] * window[1]
            imag = beam[0] * window[1] + beam[1] * window[0]
            return jnp.concatenate([real, imag], axis=1), (slot, first, lanes, low_row, low_col, row, col)

        def put(back, at):
            slot, first, lanes, low_row, low_col, row, col = at
            beam = [beams[slot, p] for p in range(2)]
            real, imag = back[:, :128], back[:, 128:]
            scatter(update.at[0], first, lanes, low_row, low_col, beam[0] * real + beam[1] * imag)
            scatter(update.at[1], first, lanes, low_row, low_col, beam[0] * imag - beam[1] * real)
            if with_light:
                brighten(row, col, beam[0] * beam[0] + beam[1] * beam[1])

        def some(step, carry):
            slots = [step * GROUP + k for k in range(GROUP)]
            pairs = [(k, k + 1) for k in range(0, GROUP, 2)]
            gathered = [gather(slot) for slot in slots]
            waves = [jnp.concatenate([gathered[a][0], gathered[b][0]], axis=0) for a, b in pairs]
            half = [cross(right_mul(wave, tables[0], tables[1])) for wave in waves]
            far = [left_mul(tables[2], tables[3], x) for x in half]
            change = []
            for x, (a, b) in zip(far, pairs):
                real, imag = x[:128], x[128:]
                known = jnp.concatenate([measured[0, 0, slots[a]], measured[0, 0, slots[b]]], axis=1)
                ratio = known * lax.rsqrt(real * real + imag * imag + 0.25) - 1.0
                change.append(jnp.concatenate([real * ratio, imag * ratio], axis=0))
            half = [cross(left_mul(tables[0], tables[1], x)) for x in change]
            back = [right_mul(x, tables[2], tables[3]) for x in half]
            for x, (a, b) in zip(back, pairs):
                put(x[:128], gathered[a][1])
                put(x[128:], gathered[b][1])
            return carry

        lax.fori_loop(0, (count + GROUP - 1) // GROUP, some, 0)
        if with_light:
            for i, d in enumerate(AROUND):

                def other(slot, carry):
                    row = around[i, 0, slot] + d[0] * 384
                    col = around[i, 1, slot] + d[1] * 384
                    touches = (row > -128) & (row < 384) & (col > -128) & (col < 384)

                    @pl.when(touches)
                    def _():
                        low_row, low_col = jnp.bitwise_and(row, 7), jnp.bitwise_and(col, 127)
                        brighten(row, col, turned(power, low_row, low_col))

                    return carry

                lax.fori_loop(0, around[i, 2, 0], other, 0)

    return kernel


def between_kernel(grid):
    def kernel(
        update, light, field,
        ext, cleared, inverse,
        near_in, relay_in, far, side, corner, far_in, side_in, corner_in, sems,
        halo_far, halo_side, halo_corner, halo_far_in, halo_side_in, halo_corner_in, more,
    ):
        place = Place(grid)
        greet(place)
        fold = Fold(place, update, near_in, relay_in, far, side, corner, far_in, side_in, corner_in, sems)
        halo = Halo(place, ext, halo_far, halo_side, halo_corner, halo_far_in, halo_side_in, halo_corner_in, more)
        fold.pack()
        greeted(place)
        fold.start(True)
        halo.clear()
        inverse[...] = 1.0 / (light[128:512, 128:512] + 1.0)
        for p in range(2):
            ext[p, 64:448, 0:384] = field[p, 64:448, 0:384] + update[p, 64:448, 0:384] * inverse[...]
        cleared[...] = jnp.zeros_like(cleared)
        fold.finish(0, ext, 64, inverse)
        halo.pack(0)
        halo.start(0)
        fold.finish(1, ext, 64, inverse, lambda: halo.start_rest(0))
        halo.pack(1)
        halo.start(1)
        halo.start_rest(1)
        halo.forward()
        halo.finish()
        fold.close()

    return kernel


def last_kernel(grid):
    def kernel(update, inverse, ext, out, near_in, relay_in, far, side, corner, far_in, side_in, corner_in, sems):
        place = Place(grid)
        greet(place)
        fold = Fold(place, update, near_in, relay_in, far, side, corner, far_in, side_in, corner_in, sems)
        fold.pack()
        greeted(place)
        fold.start(False)
        for p in range(2):
            out[p] = ext[p, 64:448, 0:384] + update[p, 64:448, 0:384] * inverse[...]
        for p in range(2):
            fold.finish(p, out, 0, inverse)
        fold.close()

    return kernel


def hold(x):
    return pltpu.with_memory_space_constraint(x, pltpu.MemorySpace.HBM)


def params(collective_id=None):
    if collective_id is None:
        return pltpu.CompilerParams(vmem_limit_bytes=LIMIT)
    return pltpu.CompilerParams(collective_id=collective_id, has_side_effects=True, vmem_limit_bytes=LIMIT)


def shards(grid, tables, object_field, probe, amplitudes, offsets, counts):
    f32, i32 = jnp.float32, jnp.int32
    shape = jax.ShapeDtypeStruct
    ext_shape, light_shape = shape((2, 512, 512), f32), shape((648, 640), f32)
    offsets = jnp.swapaxes(offsets, 2, 3)
    packs = [pltpu.VMEM((2, 64, 256), f32), pltpu.VMEM((2, 2, 192, 128), f32), pltpu.VMEM((2, 2, 64, 128), f32)]
    folds = [pltpu.VMEM((2, 64, 384), f32), pltpu.VMEM((2, 64, 128), f32)] + packs + packs
    sems = pltpu.SemaphoreType.DMA((2, 2, 11))
    ext, around, measured, tables, beams, power, update, light = pl.pallas_call(
        spread_kernel(grid),
        name="spread",
        out_shape=(
            ext_shape,
            shape((9, 8, 128), i32),
            shape(amplitudes.shape, f32),
            shape(tables.shape, tables.dtype),
            shape((12, 2, 128, 128), f32),
            shape((136, 128), f32),
            ext_shape,
            light_shape,
        ),
        in_specs=[HBM, HBM, SMEM, SMEM, HBM, HBM, HBM],
        out_specs=(VMEM,) * 8,
        scratch_shapes=[pltpu.VMEM((8, 128), i32), pltpu.VMEM((1, 1, 2, 12), i32), pltpu.VMEM((2, 136, 128), f32)]
        + packs
        + packs
        + [sems, pltpu.SemaphoreType.DMA((2, 8)), pltpu.SemaphoreType.DMA((6,))],
        compiler_params=params(0),
    )(hold(object_field), hold(offsets), counts, offsets, hold(amplitudes), hold(tables), hold(probe))
    update, light = pl.pallas_call(
        gradient_kernel(True),
        name="gradient_light",
        out_shape=(ext_shape, light_shape),
        in_specs=[SMEM] + [VMEM] * 7,
        out_specs=(VMEM,) * 2,
        input_output_aliases={5: 0, 7: 1},
        compiler_params=params(),
    )(around, ext, beams, measured, tables, update, power, light)
    ext, cleared, inverse = pl.pallas_call(
        between_kernel(grid),
        name="between",
        out_shape=(ext_shape, ext_shape, shape((384, 384), f32)),
        in_specs=[VMEM] * 3,
        out_specs=(VMEM,) * 3,
        scratch_shapes=folds + [sems] + packs + packs + [sems],
        compiler_params=params(1),
    )(update, light, ext)
    update = pl.pallas_call(
        gradient_kernel(False),
        name="gradient",
        out_shape=ext_shape,
        in_specs=[SMEM] + [VMEM] * 5,
        out_specs=VMEM,
        input_output_aliases={5: 0},
        compiler_params=params(),
    )(around, ext, beams, measured, tables, cleared)
    return pl.pallas_call(
        last_kernel(grid),
        name="last",
        out_shape=shape((2, 384, 384), f32),
        in_specs=[VMEM] * 3,
        out_specs=VMEM,
        scratch_shapes=folds + [sems],
        compiler_params=params(2),
    )(update, inverse, ext)


def solution(mesh):
    grid = (mesh.shape["row"], mesh.shape["col"])
    tables = dft_tables(128)
    placed = (
        P(None, "row", "col"),
        P(),
        P("row", "col", None, None, None),
        P("row", "col", None, None),
        P("row", "col"),
    )

    def body(*args):
        return shards(grid, jnp.asarray(tables), *args)

    return jax.shard_map(body, mesh=mesh, in_specs=placed, out_specs=P(None, "row", "col"), check_vma=False)
```

```python
import math

import jax
import jax.numpy as jnp
import numpy as np
from jax import lax
from jax.experimental import pallas as pl
from jax.experimental.pallas import tpu as pltpu
from jax.sharding import PartitionSpec as P

AROUND = ((-1, 0), (1, 0), (0, -1), (0, 1), (-1, -1), (-1, 1), (1, -1), (1, 1))
MESH = pl.DeviceIdType.MESH
VMEM = pl.BlockSpec(memory_space=pltpu.VMEM)
SMEM = pl.BlockSpec(memory_space=pltpu.SMEM)
HBM = pl.BlockSpec(memory_space=pltpu.MemorySpace.HBM)
LIMIT = 24 << 20
GROUP = 6
NEAR, FAR, LEFT, RIGHT, FAR_LEFT, FAR_RIGHT, LEFT_NEXT, RIGHT_NEXT, RELAY, EDGE_LEFT, EDGE_RIGHT = range(11)
DIAGONAL = (FAR_LEFT, FAR_RIGHT, EDGE_LEFT, EDGE_RIGHT)


def dft_tables(length):
    index = np.arange(length)
    angle = (np.outer(index, index) % length) * (2.0 * math.pi / length)
    cosine, sine = np.cos(angle) / math.sqrt(length), np.sin(angle) / math.sqrt(length)
    table = np.block([[cosine, -sine], [sine, cosine]])
    high = table.astype(jnp.bfloat16)
    low = (table - high.astype(np.float64)).astype(jnp.bfloat16)
    return np.stack([high, low, high.T, low.T])


def swap(x):
    return pltpu.roll(x, 64, x.ndim - 1)


def lower(rows):
    return lax.broadcasted_iota(jnp.int32, (rows, 128), 1) < 64


def pack(x, keep_low):
    rows = x.shape[0] // 2
    keep = lower(rows) if keep_low else ~lower(rows)
    return jnp.where(keep, x[:rows], swap(x[rows:]))


def unpack(x):
    return jnp.concatenate([x, swap(x)], axis=0)


def merge(a, b):
    keep = lower(a.shape[0])
    return jnp.concatenate([jnp.where(keep, a, b), jnp.where(keep, swap(a), swap(b))], axis=0)


class Place:
    def __init__(self, grid):
        self.row, self.col = lax.axis_index("row"), lax.axis_index("col")
        self.odd = lax.rem(self.row, 2)
        self.near_row = self.row + 1 - 2 * self.odd
        self.far_row = self.row - 1 + 2 * self.odd
        self.grid = grid
        far = (self.far_row >= 0) & (self.far_row < grid[0])
        left, right = self.col > 0, self.col < grid[1] - 1
        self.far, self.left, self.right = far, left, right
        ends = (far & jnp.logical_not(left), far & jnp.logical_not(right))
        both = (None, far, left, right, far & left, far & right, left, right, None) + ends
        self.sends = both
        order = (NEAR, FAR, RIGHT, LEFT, FAR_RIGHT, FAR_LEFT, RIGHT_NEXT, LEFT_NEXT, RELAY, EDGE_LEFT, EDGE_RIGHT)
        self.gets = tuple(both[i] for i in order)
        self.near_border = self.pick(320, 0)
        self.far_border = self.pick(0, 320)
        self.near_halo = self.pick(448, 0)
        self.far_halo = self.pick(0, 448)

    def pick(self, even, odd):
        return pl.multiple_of(even + self.odd * (odd - even), 64)

    def target(self, which):
        row = {NEAR: self.near_row, RELAY: self.near_row, FAR: self.far_row}
        row.update({which: self.far_row for which in DIAGONAL})
        side = {LEFT: -1, FAR_LEFT: -1, LEFT_NEXT: -1, RIGHT: 1, FAR_RIGHT: 1, RIGHT_NEXT: 1}
        return {"row": row.get(which, self.row), "col": self.col + side.get(which, 0)}


def when(condition, body):
    if condition is None:
        body()
    else:
        pl.when(condition)(body)


def greet(place):
    barrier = pltpu.get_barrier_semaphore()
    for which in (NEAR, FAR, LEFT, RIGHT, FAR_LEFT, FAR_RIGHT):
        when(
            place.sends[which],
            lambda: pl.semaphore_signal(
                barrier, inc=1, device_id=place.target(which), device_id_type=MESH
            ),
        )


def greeted(place):
    far, left, right = (jnp.where(x, 1, 0) for x in (place.far, place.left, place.right))
    pl.semaphore_wait(pltpu.get_barrier_semaphore(), 1 + far + (left + right) * (1 + far))


def greet_all(place):
    barrier = pltpu.get_barrier_semaphore()
    count = 0
    for d in AROUND:
        count += jnp.where(beside(place, d), 1, 0)

        @pl.when(beside(place, d))
        def _():
            pl.semaphore_signal(
                barrier, inc=1, device_id={"row": place.row + d[0], "col": place.col + d[1]}, device_id_type=MESH
            )

    return count


def beside(place, d):
    row, col = place.row + d[0], place.col + d[1]
    return (row >= 0) & (row < place.grid[0]) & (col >= 0) & (col < place.grid[1])


def remote(place, which, src, dst, sems, p):
    return pltpu.make_async_remote_copy(
        src, dst, sems.at[0, p, which], sems.at[1, p, which], device_id=place.target(which), device_id_type=MESH
    )


def start(place, copies, *which):
    for i in which:
        when(place.sends[i], copies[i].start)


def wait_recv(place, copies, *which):
    for i in which:
        when(place.gets[i], copies[i].wait_recv)


def wait_send(place, copies, gone, *which):
    for i in which or range(len(copies)):
        if i not in gone:
            when(place.sends[i], copies[i].wait_send)
    gone.update(which or range(len(copies)))


def strips(far, far_in, side, side_in, corner, corner_in, p):
    return {
        FAR: (far.at[p], far_in.at[p]),
        FAR_LEFT: (corner.at[0, p], corner_in.at[0, p]),
        FAR_RIGHT: (corner.at[1, p], corner_in.at[1, p]),
        EDGE_LEFT: (corner.at[0, p], corner_in.at[1, p]),
        EDGE_RIGHT: (corner.at[1, p], corner_in.at[0, p]),
        LEFT: (side.at[0, p, 0:64], side_in.at[0, p, 0:64]),
        RIGHT: (side.at[1, p, 0:64], side_in.at[1, p, 0:64]),
        LEFT_NEXT: (side.at[0, p, 64:192], side_in.at[0, p, 64:192]),
        RIGHT_NEXT: (side.at[1, p, 64:192], side_in.at[1, p, 64:192]),
    }


def at_rows(first, rows):
    return pl.ds(pl.multiple_of(first, 64), rows)


class Halo:
    def __init__(self, place, ext, far, side, corner, far_in, side_in, corner_in, sems):
        self.place, self.ext, self.far, self.far_in = place, ext, far, far_in
        self.gone = (set(), set())
        self.side, self.corner, self.side_in, self.corner_in = side, corner, side_in, corner_in
        near, target = at_rows(place.near_border + 64, 64), at_rows(place.far_halo, 64)
        self.copies = []
        for p in range(2):
            ends = strips(far, far_in, side, side_in, corner, corner_in, p)
            ends[NEAR] = (ext.at[p, near, 0:384], ext.at[p, target, 0:384])
            ends[RELAY] = (ext.at[p, near, 384:512], ext.at[p, target, 384:512])
            self.copies.append([remote(place, i, *ends[i], sems, p) for i in range(11)])

    def clear(self):
        place = self.place

        @pl.when(jnp.logical_not(place.far))
        def _():
            self.far_in[...] = jnp.zeros((2, 64, 256), jnp.float32)
            self.corner_in[...] = jnp.zeros((2, 2, 64, 128), jnp.float32)

        for k, side in enumerate((place.right, place.left)):

            @pl.when(jnp.logical_not(side))
            def _():
                self.side_in[k] = jnp.zeros((2, 192, 128), jnp.float32)

    def pack(self, p):
        place, ext = self.place, self.ext
        for k, lane in enumerate((0, 256)):
            for i, first in enumerate((place.near_border, place.far_border)):
                self.side[k, p, 32 * i : 32 * i + 32] = pack(ext[p, at_rows(first + 64, 64), lane : lane + 128], k == 0)
            self.side[k, p, 64:192] = pack(ext[p, 128:384, lane : lane + 128], k == 0)
        rows = at_rows(place.far_border + 64, 64)
        self.far[p, :, 0:128] = ext[p, rows, 128:256]
        self.far[p, :, 128:256] = jnp.where(lower(64), ext[p, rows, 256:384], ext[p, rows, 0:128])

    def start(self, p):
        start(self.place, self.copies[p], LEFT, RIGHT, FAR)

    def start_rest(self, p):
        wait_send(self.place, self.copies[p], self.gone[p], LEFT, RIGHT)
        start(self.place, self.copies[p], LEFT_NEXT, RIGHT_NEXT, NEAR)

    def forward(self):
        place, ext, low = self.place, self.ext, lower(64)
        for p in range(2):
            wait_recv(place, self.copies[p], LEFT, RIGHT)
            for i, first in enumerate((place.near_border, place.far_border)):
                parts = [self.side_in[k, p, 32 * i : 32 * i + 32] for k in range(2)]
                ext[p, at_rows(first + 64, 64), 384:512] = merge(*parts)
            start(place, self.copies[p], RELAY)
            rows = at_rows(place.far_border + 64, 64)
            self.corner[0, p] = jnp.where(low, ext[p, rows, 0:128], ext[p, rows, 384:512])
            self.corner[1, p] = jnp.where(low, ext[p, rows, 384:512], ext[p, rows, 256:384])
            start(place, self.copies[p], *DIAGONAL)

    def finish(self):
        place, ext, low = self.place, self.ext, lower(64)
        for p in range(2):
            wait_recv(place, self.copies[p], LEFT_NEXT, RIGHT_NEXT)
            ext[p, 128:384, 384:512] = merge(self.side_in[0, p, 64:192], self.side_in[1, p, 64:192])
            wait_recv(place, self.copies[p], FAR, *DIAGONAL)
            rows = at_rows(place.far_halo, 64)
            right, left = self.corner_in[0, p], self.corner_in[1, p]
            mixed = self.far_in[p, :, 128:256]
            ext[p, rows, 0:128] = jnp.where(low, left, mixed)
            ext[p, rows, 128:256] = self.far_in[p, :, 0:128]
            ext[p, rows, 256:384] = jnp.where(low, mixed, right)
            ext[p, rows, 384:512] = jnp.where(low, right, left)
        for p in range(2):
            wait_recv(place, self.copies[p], NEAR, RELAY)
            wait_send(place, self.copies[p], self.gone[p])


class Fold:
    def __init__(self, place, update, near_in, relay_in, far, side, corner, far_in, side_in, corner_in, sems):
        self.place, self.update, self.near_in, self.relay_in = place, update, near_in, relay_in
        self.far, self.far_in = far, far_in
        self.gone = (set(), set())
        self.side, self.corner, self.side_in, self.corner_in = side, corner, side_in, corner_in
        near = at_rows(place.near_halo, 64)
        self.copies = []
        for p in range(2):
            ends = strips(far, far_in, side, side_in, corner, corner_in, p)
            ends[NEAR] = (update.at[p, near, 0:384], near_in.at[p])
            ends[RELAY] = (update.at[p, near, 384:512], relay_in.at[p])
            self.copies.append([remote(place, i, *ends[i], sems, p) for i in range(11)])

    def pack(self):
        place, update, low = self.place, self.update, lower(64)

        @pl.when(jnp.logical_not(place.far))
        def _():
            self.corner_in[...] = jnp.zeros((2, 2, 64, 128), jnp.float32)

        rows = at_rows(place.far_halo, 64)
        for p in range(2):
            tiles = [update[p, rows, 128 * t : 128 * t + 128] for t in range(4)]
            self.corner[0, p] = jnp.where(low, tiles[0], tiles[3])
            self.corner[1, p] = jnp.where(low, tiles[3], tiles[2])
            self.far[p, :, 0:128] = tiles[1]
            self.far[p, :, 128:256] = jnp.where(low, tiles[2], tiles[0])
            for k in range(2):
                self.side[k, p, 64:192] = pack(update[p, 128:384, 384:512], k == 1)

    def start(self, paced):
        place, update = self.place, self.update
        for p in range(2):
            start(place, self.copies[p], *DIAGONAL, RELAY)
        start(place, self.copies[0], FAR, LEFT_NEXT, RIGHT_NEXT)
        if not paced:
            start(place, self.copies[1], FAR)
        for p in range(2):
            wait_recv(place, self.copies[p], RELAY, *DIAGONAL)
            extra = (self.relay_in[p], jnp.where(lower(64), self.corner_in[0, p], self.corner_in[1, p]))
            for i, first in enumerate((place.near_border, place.far_border)):
                part = update[p, at_rows(first + 64, 64), 384:512] + extra[i]
                for k in range(2):
                    self.side[k, p, 32 * i : 32 * i + 32] = pack(part, k == 1)
            start(place, self.copies[p], LEFT, RIGHT)
            if p == 0 and paced:
                start(place, self.copies[0], NEAR)
                wait_send(place, self.copies[0], self.gone[0], FAR, LEFT_NEXT, RIGHT_NEXT)
                start(place, self.copies[1], FAR)
            if p == 0:
                start(place, self.copies[1], LEFT_NEXT, RIGHT_NEXT)
        if not paced:
            start(place, self.copies[0], NEAR)
        start(place, self.copies[1], NEAR)

    def finish(self, p, dest, base, inverse, between=None):
        place = self.place
        sides = ((place.right, 256, lambda x: jnp.where(lower(x.shape[0]), 0.0, x)), (place.left, 0, lambda x: jnp.where(lower(x.shape[0]), x, 0.0)))

        def add(first, lane, value):
            lanes, rows = pl.ds(lane, value.shape[1]), value.shape[0]
            dest[p, at_rows(first + base, rows), lanes] += value * inverse[at_rows(first, rows), lanes]

        wait_recv(place, self.copies[p], NEAR)
        add(place.near_border, 0, self.near_in[p])

        @pl.when(place.far)
        def _():
            self.copies[p][FAR].wait_recv()
            mixed = self.far_in[p, :, 128:256]
            add(place.far_border, 0, jnp.where(lower(64), self.corner_in[1, p], mixed))
            add(place.far_border, 128, self.far_in[p, :, 0:128])
            add(place.far_border, 256, jnp.where(lower(64), mixed, self.corner_in[0, p]))

        for k, (here, lane, keep) in enumerate(sides):

            @pl.when(here)
            def _():
                self.copies[p][LEFT_NEXT + k].wait_recv()
                add(64, lane, keep(unpack(self.side_in[k, p, 64:192])))

        if between is not None:
            between()
        for k, (here, lane, keep) in enumerate(sides):

            @pl.when(here)
            def _():
                self.copies[p][LEFT + k].wait_recv()
                add(place.near_border, lane, keep(unpack(self.side_in[k, p, 0:32])))
                add(place.far_border, lane, keep(unpack(self.side_in[k, p, 32:64])))

    def close(self):
        for p in range(2):
            wait_send(self.place, self.copies[p], self.gone[p])


def spread_kernel(grid):
    def kernel(
        field, offsets, counts, places, measured, tables, probe,
        ext, around, measured_here, tables_here, beams, power, update, light,
        mine, offsets_here, tall, far, side, corner, far_in, side_in, corner_in, sems, notes, local,
    ):
        place = Place(grid)
        peers = greet_all(place)
        pulls = [pltpu.make_async_copy(offsets, offsets_here, local.at[0])]
        pulls += [pltpu.make_async_copy(field.at[p], ext.at[p, 64:448, 0:384], local.at[1 + p]) for p in range(2)]
        later = [
            pltpu.make_async_copy(measured, measured_here, local.at[3]),
            pltpu.make_async_copy(tables, tables_here, local.at[4]),
        ]
        pulls.append(pltpu.make_async_copy(probe, tall.at[:, 8:136], local.at[5]))
        for pull in pulls:
            pull.start()
        halo = Halo(place, ext, far, side, corner, far_in, side_in, corner_in, sems)
        halo.clear()
        for i, d in enumerate(AROUND):

            @pl.when(jnp.logical_not(beside(place, d)))
            def _():
                around[i] = jnp.zeros((8, 128), jnp.int32)

        pulls[0].wait()
        mine[0:2, 0:12] = offsets_here[0, 0]
        mine[2:3, 0:1] = jnp.full((1, 1), counts[0, 0], jnp.int32)
        letters = []
        for i, d in enumerate(AROUND):
            letter = pltpu.make_async_remote_copy(
                mine,
                around.at[AROUND.index((-d[0], -d[1]))],
                notes.at[0, i],
                notes.at[1, i],
                device_id={"row": place.row + d[0], "col": place.col + d[1]},
                device_id_type=MESH,
            )
            letters.append(letter)
        pulls[1].wait()
        halo.pack(0)
        pl.semaphore_wait(pltpu.get_barrier_semaphore(), peers)
        for i, d in enumerate(AROUND):
            pl.when(beside(place, d))(letters[i].start)
        halo.start(0)
        pulls[2].wait()
        halo.pack(1)
        halo.start(1)
        halo.start_rest(0)
        halo.start_rest(1)
        for pull in later:
            pull.start()
        update[...] = jnp.zeros_like(update)
        halo.forward()
        light[...] = jnp.zeros_like(light)
        pulls[3].wait()
        for p in range(2):
            tall[p, 0:8] = tall[p, 128:136]
        power[...] = tall[0] * tall[0] + tall[1] * tall[1]

        def turn(slot, carry):
            live = (slot < counts[0, 0]).astype(jnp.float32)
            low_row, low_col = places[0, 0, 0, slot] & 7, places[0, 0, 1, slot] & 127
            for p in range(2):
                beams[slot, p] = pltpu.roll(tall[p, pl.ds(8 - low_row, 128), :], low_col, 1) * live
            return carry

        lax.fori_loop(0, 12, turn, 0)
        halo.finish()
        for i, d in enumerate(AROUND):
            pl.when(beside(place, d))(letters[i].wait_send)
            pl.when(beside(place, (-d[0], -d[1])))(letters[i].wait_recv)
        for pull in later:
            pull.wait()

    return kernel


def split(x):
    high = x.astype(jnp.bfloat16)
    return high, (x - high.astype(jnp.float32)).astype(jnp.bfloat16)


def dot(a, b):
    return jnp.dot(a, b, preferred_element_type=jnp.float32)


def right_mul(x, high, low):
    xh, xl = split(x)
    return dot(xh, high) + dot(xl, high) + dot(xh, low)


def left_mul(high, low, x):
    xh, xl = split(x)
    return dot(high, xh) + dot(high, xl) + dot(low, xh)


def cross(x):
    return jnp.concatenate(
        [
            jnp.concatenate([x[:128, :128], x[128:, :128]], axis=1),
            jnp.concatenate([x[:128, 128:], x[128:, 128:]], axis=1),
        ],
        axis=0,
    )


def gradient_kernel(with_light):
    def kernel(*refs):
        if with_light:
            offsets, counts, around, ext, beams, measured, tables, _, power, _, update, light, notes, arrived = refs
        else:
            offsets, counts, ext, beams, measured, tables, _, update = refs
        count = counts[0, 0]
        if with_light:
            bring = pltpu.make_async_copy(around, notes, arrived.at[0])
            bring.start()
        lane = lax.broadcasted_iota(jnp.int32, (128, 128), 1)
        sub = lax.broadcasted_iota(jnp.int32, (8, 128), 0)

        def turned(source, shift_rows, shift_lanes):
            return pltpu.roll(source[pl.ds(8 - shift_rows, 128), :], shift_lanes, 1)

        def scatter(dest, first, lanes, shift_rows, shift_lanes, value):
            head = jnp.where(sub >= shift_rows, value[:8], 0.0)
            main = jnp.concatenate([head, value[8:]], axis=0)
            tail = jnp.where(sub < shift_rows, value[:8], 0.0)
            for which, at in enumerate(lanes):
                keep = lane >= shift_lanes if which == 0 else lane < shift_lanes
                dest[pl.ds(first, 128), at] += jnp.where(keep, main, 0.0)
                dest[pl.ds(first + 128, 8), at] += jnp.where(keep[:8], tail, 0.0)

        def tiles_of(col, base, wrap):
            tile = lax.shift_right_arithmetic(col, 7) + base
            first = lax.rem(tile + wrap, wrap)
            second = lax.rem(tile + wrap + 1, wrap)
            return [pl.ds(pl.multiple_of(t * 128, 128), 128) for t in (first, second)]

        def brighten(row, col, value):
            low_row, low_col = jnp.bitwise_and(row, 7), jnp.bitwise_and(col, 127)
            first = pl.multiple_of(row - low_row + 128, 8)
            scatter(light, first, tiles_of(col, 1, 5), low_row, low_col, value)

        def gather(slot):
            row, col = offsets[0, 0, 0, slot], offsets[0, 0, 1, slot]
            low_row, low_col = jnp.bitwise_and(row, 7), jnp.bitwise_and(col, 127)
            first = pl.multiple_of(row - low_row + 64, 8)
            lanes = tiles_of(col, 0, 4)
            beam = [beams[slot, p] for p in range(2)]
            window = []
            for p in range(2):
                main = jnp.where(
                    lane >= low_col, ext[p, pl.ds(first, 128), lanes[0]], ext[p, pl.ds(first, 128), lanes[1]]
                )
                tail = jnp.where(
                    lane[:8] >= low_col,
                    ext[p, pl.ds(first + 128, 8), lanes[0]],
                    ext[p, pl.ds(first + 128, 8), lanes[1]],
                )
                window.append(jnp.concatenate([jnp.where(sub >= low_row, main[:8], tail), main[8:]], axis=0))
            real = beam[0] * window[0] - beam[1] * window[1]
            imag = beam[0] * window[1] + beam[1] * window[0]
            return jnp.concatenate([real, imag], axis=1), (slot, first, lanes, low_row, low_col, row, col)

        def put(back, at):
            slot, first, lanes, low_row, low_col, row, col = at
            beam = [beams[slot, p] for p in range(2)]
            real, imag = back[:, :128], back[:, 128:]
            scatter(update.at[0], first, lanes, low_row, low_col, beam[0] * real + beam[1] * imag)
            scatter(update.at[1], first, lanes, low_row, low_col, beam[0] * imag - beam[1] * real)
            if with_light:
                brighten(row, col, beam[0] * beam[0] + beam[1] * beam[1])

        def some(step, carry):
            slots = [step * GROUP + k for k in range(GROUP)]
            pairs = [(k, k + 1) for k in range(0, GROUP, 2)]
            gathered = [gather(slot) for slot in slots]
            waves = [jnp.concatenate([gathered[a][0], gathered[b][0]], axis=0) for a, b in pairs]
            half = [cross(right_mul(wave, tables[0], tables[1])) for wave in waves]
            far = [left_mul(tables[2], tables[3], x) for x in half]
            change = []
            for x, (a, b) in zip(far, pairs):
                real, imag = x[:128], x[128:]
                known = jnp.concatenate([measured[0, 0, slots[a]], measured[0, 0, slots[b]]], axis=1)
                ratio = known * lax.rsqrt(real * real + imag * imag + 0.25) - 1.0
                change.append(jnp.concatenate([real * ratio, imag * ratio], axis=0))
            half = [cross(left_mul(tables[0], tables[1], x)) for x in change]
            back = [right_mul(x, tables[2], tables[3]) for x in half]
            for x, (a, b) in zip(back, pairs):
                put(x[:128], gathered[a][1])
                put(x[128:], gathered[b][1])
            return carry

        lax.fori_loop(0, (count + GROUP - 1) // GROUP, some, 0)
        if with_light:
            bring.wait()
            for i, d in enumerate(AROUND):

                def other(slot, carry):
                    row = notes[i, 0, slot] + d[0] * 384
                    col = notes[i, 1, slot] + d[1] * 384
                    touches = (row > -128) & (row < 384) & (col > -128) & (col < 384)

                    @pl.when(touches)
                    def _():
                        low_row, low_col = jnp.bitwise_and(row, 7), jnp.bitwise_and(col, 127)
                        brighten(row, col, turned(power, low_row, low_col))

                    return carry

                lax.fori_loop(0, notes[i, 2, 0], other, 0)

    return kernel


def between_kernel(grid):
    def kernel(
        update, light, field,
        ext, cleared, inverse,
        near_in, relay_in, far, side, corner, far_in, side_in, corner_in, sems,
        halo_far, halo_side, halo_corner, halo_far_in, halo_side_in, halo_corner_in, more,
    ):
        place = Place(grid)
        greet(place)
        fold = Fold(place, update, near_in, relay_in, far, side, corner, far_in, side_in, corner_in, sems)
        halo = Halo(place, ext, halo_far, halo_side, halo_corner, halo_far_in, halo_side_in, halo_corner_in, more)
        fold.pack()
        greeted(place)
        fold.start(True)
        halo.clear()
        inverse[...] = 1.0 / (light[128:512, 128:512] + 1.0)
        for p in range(2):
            ext[p, 64:448, 0:384] = field[p, 64:448, 0:384] + update[p, 64:448, 0:384] * inverse[...]
        cleared[...] = jnp.zeros_like(cleared)
        fold.finish(0, ext, 64, inverse)
        halo.pack(0)
        halo.start(0)
        fold.finish(1, ext, 64, inverse, lambda: halo.start_rest(0))
        halo.pack(1)
        halo.start(1)
        halo.start_rest(1)
        halo.forward()
        halo.finish()
        fold.close()

    return kernel


def last_kernel(grid):
    def kernel(update, inverse, ext, out, near_in, relay_in, far, side, corner, far_in, side_in, corner_in, sems):
        place = Place(grid)
        greet(place)
        fold = Fold(place, update, near_in, relay_in, far, side, corner, far_in, side_in, corner_in, sems)
        fold.pack()
        greeted(place)
        fold.start(False)
        for p in range(2):
            out[p] = ext[p, 64:448, 0:384] + update[p, 64:448, 0:384] * inverse[...]
        for p in range(2):
            fold.finish(p, out, 0, inverse)
        fold.close()

    return kernel


def hold(x):
    return pltpu.with_memory_space_constraint(x, pltpu.MemorySpace.HBM)


def params(collective_id=None):
    if collective_id is None:
        return pltpu.CompilerParams(vmem_limit_bytes=LIMIT)
    return pltpu.CompilerParams(collective_id=collective_id, has_side_effects=True, vmem_limit_bytes=LIMIT)


def shards(grid, tables, object_field, probe, amplitudes, offsets, counts):
    f32, i32 = jnp.float32, jnp.int32
    shape = jax.ShapeDtypeStruct
    ext_shape, light_shape = shape((2, 512, 512), f32), shape((648, 640), f32)
    offsets = jnp.swapaxes(offsets, 2, 3)
    packs = [pltpu.VMEM((2, 64, 256), f32), pltpu.VMEM((2, 2, 192, 128), f32), pltpu.VMEM((2, 2, 64, 128), f32)]
    folds = [pltpu.VMEM((2, 64, 384), f32), pltpu.VMEM((2, 64, 128), f32)] + packs + packs
    sems = pltpu.SemaphoreType.DMA((2, 2, 11))
    ext, around, measured, tables, beams, power, update, light = pl.pallas_call(
        spread_kernel(grid),
        name="spread",
        out_shape=(
            ext_shape,
            shape((8, 8, 128), i32),
            shape(amplitudes.shape, f32),
            shape(tables.shape, tables.dtype),
            shape((12, 2, 128, 128), f32),
            shape((136, 128), f32),
            ext_shape,
            light_shape,
        ),
        in_specs=[HBM, HBM, SMEM, SMEM, HBM, HBM, HBM],
        out_specs=(VMEM,) * 8,
        scratch_shapes=[pltpu.VMEM((8, 128), i32), pltpu.VMEM((1, 1, 2, 12), i32), pltpu.VMEM((2, 136, 128), f32)]
        + packs
        + packs
        + [sems, pltpu.SemaphoreType.DMA((2, 8)), pltpu.SemaphoreType.DMA((6,))],
        compiler_params=params(0),
    )(hold(object_field), hold(offsets), counts, offsets, hold(amplitudes), hold(tables), hold(probe))
    update, light = pl.pallas_call(
        gradient_kernel(True),
        name="gradient_light",
        out_shape=(ext_shape, light_shape),
        in_specs=[SMEM] * 2 + [VMEM] * 8,
        out_specs=(VMEM,) * 2,
        scratch_shapes=[pltpu.SMEM((8, 8, 128), i32), pltpu.SemaphoreType.DMA((1,))],
        input_output_aliases={7: 0, 9: 1},
        compiler_params=params(),
    )(offsets, counts, around, ext, beams, measured, tables, update, power, light)
    ext, cleared, inverse = pl.pallas_call(
        between_kernel(grid),
        name="between",
        out_shape=(ext_shape, ext_shape, shape((384, 384), f32)),
        in_specs=[VMEM] * 3,
        out_specs=(VMEM,) * 3,
        scratch_shapes=folds + [sems] + packs + packs + [sems],
        compiler_params=params(1),
    )(update, light, ext)
    update = pl.pallas_call(
        gradient_kernel(False),
        name="gradient",
        out_shape=ext_shape,
        in_specs=[SMEM] * 2 + [VMEM] * 5,
        out_specs=VMEM,
        input_output_aliases={6: 0},
        compiler_params=params(),
    )(offsets, counts, ext, beams, measured, tables, cleared)
    return pl.pallas_call(
        last_kernel(grid),
        name="last",
        out_shape=shape((2, 384, 384), f32),
        in_specs=[VMEM] * 3,
        out_specs=VMEM,
        scratch_shapes=folds + [sems],
        compiler_params=params(2),
    )(update, inverse, ext)


def solution(mesh):
    grid = (mesh.shape["row"], mesh.shape["col"])
    tables = dft_tables(128)
    placed = (
        P(None, "row", "col"),
        P(),
        P("row", "col", None, None, None),
        P("row", "col", None, None),
        P("row", "col"),
    )

    def body(*args):
        return shards(grid, jnp.asarray(tables), *args)

    return jax.shard_map(body, mesh=mesh, in_specs=placed, out_specs=P(None, "row", "col"), check_vma=False)
```

```python
import math

import jax
import jax.numpy as jnp
import numpy as np
from jax import lax
from jax.experimental import pallas as pl
from jax.experimental.pallas import tpu as pltpu
from jax.sharding import PartitionSpec as P

AROUND = ((-1, 0), (1, 0), (0, -1), (0, 1), (-1, -1), (-1, 1), (1, -1), (1, 1))
MESH = pl.DeviceIdType.MESH
VMEM = pl.BlockSpec(memory_space=pltpu.VMEM)
SMEM = pl.BlockSpec(memory_space=pltpu.SMEM)
HBM = pl.BlockSpec(memory_space=pltpu.MemorySpace.HBM)
LIMIT = 24 << 20
NEAR, FAR, LEFT, RIGHT, FAR_LEFT, FAR_RIGHT, LEFT_NEXT, RIGHT_NEXT, RELAY, EDGE_LEFT, EDGE_RIGHT = range(11)
DIAGONAL = (FAR_LEFT, FAR_RIGHT, EDGE_LEFT, EDGE_RIGHT)


def dft_tables(length):
    index = np.arange(length)
    angle = (np.outer(index, index) % length) * (2.0 * math.pi / length)
    cosine, sine = np.cos(angle) / math.sqrt(length), np.sin(angle) / math.sqrt(length)
    table = np.block([[cosine, -sine], [sine, cosine]])
    high = table.astype(jnp.bfloat16)
    low = (table - high.astype(np.float64)).astype(jnp.bfloat16)
    return np.stack([high, low, high.T, low.T])


def swap(x):
    return pltpu.roll(x, 64, x.ndim - 1)


def lower(rows):
    return lax.broadcasted_iota(jnp.int32, (rows, 128), 1) < 64


def pack(x, keep_low):
    rows = x.shape[0] // 2
    keep = lower(rows) if keep_low else ~lower(rows)
    return jnp.where(keep, x[:rows], swap(x[rows:]))


def unpack(x):
    return jnp.concatenate([x, swap(x)], axis=0)


def merge(a, b):
    keep = lower(a.shape[0])
    return jnp.concatenate([jnp.where(keep, a, b), jnp.where(keep, swap(a), swap(b))], axis=0)


class Place:
    def __init__(self, grid):
        self.row, self.col = lax.axis_index("row"), lax.axis_index("col")
        self.odd = lax.rem(self.row, 2)
        self.near_row = self.row + 1 - 2 * self.odd
        self.far_row = self.row - 1 + 2 * self.odd
        self.grid = grid
        far = (self.far_row >= 0) & (self.far_row < grid[0])
        left, right = self.col > 0, self.col < grid[1] - 1
        self.far, self.left, self.right = far, left, right
        ends = (far & jnp.logical_not(left), far & jnp.logical_not(right))
        both = (None, far, left, right, far & left, far & right, left, right, None) + ends
        self.sends = both
        order = (NEAR, FAR, RIGHT, LEFT, FAR_RIGHT, FAR_LEFT, RIGHT_NEXT, LEFT_NEXT, RELAY, EDGE_LEFT, EDGE_RIGHT)
        self.gets = tuple(both[i] for i in order)
        self.near_border = self.pick(320, 0)
        self.far_border = self.pick(0, 320)
        self.near_halo = self.pick(448, 0)
        self.far_halo = self.pick(0, 448)

    def pick(self, even, odd):
        return pl.multiple_of(even + self.odd * (odd - even), 64)

    def target(self, which):
        row = {NEAR: self.near_row, RELAY: self.near_row, FAR: self.far_row}
        row.update({which: self.far_row for which in DIAGONAL})
        side = {LEFT: -1, FAR_LEFT: -1, LEFT_NEXT: -1, RIGHT: 1, FAR_RIGHT: 1, RIGHT_NEXT: 1}
        return {"row": row.get(which, self.row), "col": self.col + side.get(which, 0)}


def when(condition, body):
    if condition is None:
        body()
    else:
        pl.when(condition)(body)


def greet(place):
    barrier = pltpu.get_barrier_semaphore()
    for which in (NEAR, FAR, LEFT, RIGHT, FAR_LEFT, FAR_RIGHT):
        when(
            place.sends[which],
            lambda: pl.semaphore_signal(
                barrier, inc=1, device_id=place.target(which), device_id_type=MESH
            ),
        )


def greeted(place):
    far, left, right = (jnp.where(x, 1, 0) for x in (place.far, place.left, place.right))
    pl.semaphore_wait(pltpu.get_barrier_semaphore(), 1 + far + (left + right) * (1 + far))


def greet_all(place):
    barrier = pltpu.get_barrier_semaphore()
    count = 0
    for d in AROUND:
        count += jnp.where(beside(place, d), 1, 0)

        @pl.when(beside(place, d))
        def _():
            pl.semaphore_signal(
                barrier, inc=1, device_id={"row": place.row + d[0], "col": place.col + d[1]}, device_id_type=MESH
            )

    return count


def beside(place, d):
    row, col = place.row + d[0], place.col + d[1]
    return (row >= 0) & (row < place.grid[0]) & (col >= 0) & (col < place.grid[1])


def remote(place, which, src, dst, sems, p):
    return pltpu.make_async_remote_copy(
        src, dst, sems.at[0, p, which], sems.at[1, p, which], device_id=place.target(which), device_id_type=MESH
    )


def start(place, copies, *which):
    for i in which:
        when(place.sends[i], copies[i].start)


def wait_recv(place, copies, *which):
    for i in which:
        when(place.gets[i], copies[i].wait_recv)


def wait_send(place, copies, gone, *which):
    for i in which or range(len(copies)):
        if i not in gone:
            when(place.sends[i], copies[i].wait_send)
    gone.update(which or range(len(copies)))


def strips(far, far_in, side, side_in, corner, corner_in, p):
    return {
        FAR: (far.at[p], far_in.at[p]),
        FAR_LEFT: (corner.at[0, p], corner_in.at[0, p]),
        FAR_RIGHT: (corner.at[1, p], corner_in.at[1, p]),
        EDGE_LEFT: (corner.at[0, p], corner_in.at[1, p]),
        EDGE_RIGHT: (corner.at[1, p], corner_in.at[0, p]),
        LEFT: (side.at[0, p, 0:64], side_in.at[0, p, 0:64]),
        RIGHT: (side.at[1, p, 0:64], side_in.at[1, p, 0:64]),
        LEFT_NEXT: (side.at[0, p, 64:192], side_in.at[0, p, 64:192]),
        RIGHT_NEXT: (side.at[1, p, 64:192], side_in.at[1, p, 64:192]),
    }


def at_rows(first, rows):
    return pl.ds(pl.multiple_of(first, 64), rows)


class Halo:
    def __init__(self, place, ext, far, side, corner, far_in, side_in, corner_in, sems):
        self.place, self.ext, self.far, self.far_in = place, ext, far, far_in
        self.gone = (set(), set())
        self.side, self.corner, self.side_in, self.corner_in = side, corner, side_in, corner_in
        near, target = at_rows(place.near_border + 64, 64), at_rows(place.far_halo, 64)
        self.copies = []
        for p in range(2):
            ends = strips(far, far_in, side, side_in, corner, corner_in, p)
            ends[NEAR] = (ext.at[p, near, 0:384], ext.at[p, target, 0:384])
            ends[RELAY] = (ext.at[p, near, 384:512], ext.at[p, target, 384:512])
            self.copies.append([remote(place, i, *ends[i], sems, p) for i in range(11)])

    def clear(self):
        place = self.place

        @pl.when(jnp.logical_not(place.far))
        def _():
            self.far_in[...] = jnp.zeros((2, 64, 256), jnp.float32)
            self.corner_in[...] = jnp.zeros((2, 2, 64, 128), jnp.float32)

        for k, side in enumerate((place.right, place.left)):

            @pl.when(jnp.logical_not(side))
            def _():
                self.side_in[k] = jnp.zeros((2, 192, 128), jnp.float32)

    def pack(self, p):
        place, ext = self.place, self.ext
        for k, lane in enumerate((0, 256)):
            for i, first in enumerate((place.near_border, place.far_border)):
                self.side[k, p, 32 * i : 32 * i + 32] = pack(ext[p, at_rows(first + 64, 64), lane : lane + 128], k == 0)
        rows = at_rows(place.far_border + 64, 64)
        self.far[p, :, 0:128] = ext[p, rows, 128:256]
        self.far[p, :, 128:256] = jnp.where(lower(64), ext[p, rows, 256:384], ext[p, rows, 0:128])

    def pack_rest(self, p):
        for k, lane in enumerate((0, 256)):
            self.side[k, p, 64:192] = pack(self.ext[p, 128:384, lane : lane + 128], k == 0)

    def start(self, p):
        start(self.place, self.copies[p], LEFT, RIGHT, FAR)

    def start_rest(self, p):
        wait_send(self.place, self.copies[p], self.gone[p], LEFT, RIGHT)
        start(self.place, self.copies[p], LEFT_NEXT, RIGHT_NEXT, NEAR)

    def forward(self):
        place, ext, low = self.place, self.ext, lower(64)
        for p in range(2):
            wait_recv(place, self.copies[p], LEFT, RIGHT)
            for i, first in enumerate((place.near_border, place.far_border)):
                parts = [self.side_in[k, p, 32 * i : 32 * i + 32] for k in range(2)]
                ext[p, at_rows(first + 64, 64), 384:512] = merge(*parts)
            start(place, self.copies[p], RELAY)
            rows = at_rows(place.far_border + 64, 64)
            self.corner[0, p] = jnp.where(low, ext[p, rows, 0:128], ext[p, rows, 384:512])
            self.corner[1, p] = jnp.where(low, ext[p, rows, 384:512], ext[p, rows, 256:384])
            start(place, self.copies[p], *DIAGONAL)

    def finish(self):
        place, ext, low = self.place, self.ext, lower(64)
        for p in range(2):
            wait_recv(place, self.copies[p], LEFT_NEXT, RIGHT_NEXT)
            ext[p, 128:384, 384:512] = merge(self.side_in[0, p, 64:192], self.side_in[1, p, 64:192])
            wait_recv(place, self.copies[p], FAR, *DIAGONAL)
            rows = at_rows(place.far_halo, 64)
            right, left = self.corner_in[0, p], self.corner_in[1, p]
            mixed = self.far_in[p, :, 128:256]
            ext[p, rows, 0:128] = jnp.where(low, left, mixed)
            ext[p, rows, 128:256] = self.far_in[p, :, 0:128]
            ext[p, rows, 256:384] = jnp.where(low, mixed, right)
            ext[p, rows, 384:512] = jnp.where(low, right, left)
        for p in range(2):
            wait_recv(place, self.copies[p], NEAR, RELAY)
            wait_send(place, self.copies[p], self.gone[p])


class Fold:
    def __init__(self, place, update, near_in, relay_in, far, side, corner, far_in, side_in, corner_in, sems):
        self.place, self.update, self.near_in, self.relay_in = place, update, near_in, relay_in
        self.far, self.far_in = far, far_in
        self.gone = (set(), set())
        self.side, self.corner, self.side_in, self.corner_in = side, corner, side_in, corner_in
        near = at_rows(place.near_halo, 64)
        self.copies = []
        for p in range(2):
            ends = strips(far, far_in, side, side_in, corner, corner_in, p)
            ends[NEAR] = (update.at[p, near, 0:384], near_in.at[p])
            ends[RELAY] = (update.at[p, near, 384:512], relay_in.at[p])
            self.copies.append([remote(place, i, *ends[i], sems, p) for i in range(11)])

    def pack(self):
        place, update, low = self.place, self.update, lower(64)

        @pl.when(jnp.logical_not(place.far))
        def _():
            self.corner_in[...] = jnp.zeros((2, 2, 64, 128), jnp.float32)

        rows = at_rows(place.far_halo, 64)
        for p in range(2):
            tiles = [update[p, rows, 128 * t : 128 * t + 128] for t in range(4)]
            self.corner[0, p] = jnp.where(low, tiles[0], tiles[3])
            self.corner[1, p] = jnp.where(low, tiles[3], tiles[2])
            self.far[p, :, 0:128] = tiles[1]
            self.far[p, :, 128:256] = jnp.where(low, tiles[2], tiles[0])
            for k in range(2):
                self.side[k, p, 64:192] = pack(update[p, 128:384, 384:512], k == 1)

    def start(self, paced):
        place, update = self.place, self.update
        for p in range(2):
            start(place, self.copies[p], *DIAGONAL, RELAY)
        start(place, self.copies[0], FAR, LEFT_NEXT, RIGHT_NEXT)
        if not paced:
            start(place, self.copies[1], FAR)
        for p in range(2):
            wait_recv(place, self.copies[p], RELAY, *DIAGONAL)
            extra = (self.relay_in[p], jnp.where(lower(64), self.corner_in[0, p], self.corner_in[1, p]))
            for i, first in enumerate((place.near_border, place.far_border)):
                part = update[p, at_rows(first + 64, 64), 384:512] + extra[i]
                for k in range(2):
                    self.side[k, p, 32 * i : 32 * i + 32] = pack(part, k == 1)
            start(place, self.copies[p], LEFT, RIGHT)
            if p == 0 and paced:
                start(place, self.copies[0], NEAR)
                wait_send(place, self.copies[0], self.gone[0], FAR, LEFT_NEXT, RIGHT_NEXT)
                start(place, self.copies[1], FAR)
            if p == 0:
                start(place, self.copies[1], LEFT_NEXT, RIGHT_NEXT)
        if not paced:
            start(place, self.copies[0], NEAR)
        start(place, self.copies[1], NEAR)

    def finish(self, p, dest, base, inverse, between=None):
        place = self.place
        sides = ((place.right, 256, lambda x: jnp.where(lower(x.shape[0]), 0.0, x)), (place.left, 0, lambda x: jnp.where(lower(x.shape[0]), x, 0.0)))

        def add(first, lane, value):
            lanes, rows = pl.ds(lane, value.shape[1]), value.shape[0]
            dest[p, at_rows(first + base, rows), lanes] += value * inverse[at_rows(first, rows), lanes]

        wait_recv(place, self.copies[p], NEAR)
        add(place.near_border, 0, self.near_in[p])

        @pl.when(place.far)
        def _():
            self.copies[p][FAR].wait_recv()
            mixed = self.far_in[p, :, 128:256]
            add(place.far_border, 0, jnp.where(lower(64), self.corner_in[1, p], mixed))
            add(place.far_border, 128, self.far_in[p, :, 0:128])
            add(place.far_border, 256, jnp.where(lower(64), mixed, self.corner_in[0, p]))

        for k, (here, lane, keep) in enumerate(sides):

            @pl.when(here)
            def _():
                self.copies[p][LEFT_NEXT + k].wait_recv()
                add(64, lane, keep(unpack(self.side_in[k, p, 64:192])))

        if between is not None:
            between()
        for k, (here, lane, keep) in enumerate(sides):

            @pl.when(here)
            def _():
                self.copies[p][LEFT + k].wait_recv()
                add(place.near_border, lane, keep(unpack(self.side_in[k, p, 0:32])))
                add(place.far_border, lane, keep(unpack(self.side_in[k, p, 32:64])))

    def close(self):
        for p in range(2):
            wait_send(self.place, self.copies[p], self.gone[p])


def spread_kernel(grid):
    def kernel(
        field, offsets, counts, places, measured, tables, probe,
        ext, around, measured_here, tables_here, beams, power, update, light,
        mine, offsets_here, tall, far, side, corner, far_in, side_in, corner_in, sems, notes, local,
    ):
        place = Place(grid)
        peers = greet_all(place)
        pulls = [pltpu.make_async_copy(offsets, offsets_here, local.at[0])]
        pulls += [pltpu.make_async_copy(field.at[p], ext.at[p, 64:448, 0:384], local.at[1 + p]) for p in range(2)]
        later = [
            pltpu.make_async_copy(measured, measured_here, local.at[3]),
            pltpu.make_async_copy(tables, tables_here, local.at[4]),
        ]
        pulls.append(pltpu.make_async_copy(probe, tall.at[:, 8:136], local.at[5]))
        for pull in pulls:
            pull.start()
        halo = Halo(place, ext, far, side, corner, far_in, side_in, corner_in, sems)
        halo.clear()
        for i, d in enumerate(AROUND):

            @pl.when(jnp.logical_not(beside(place, d)))
            def _():
                around[i] = jnp.zeros((8, 128), jnp.int32)

        pulls[0].wait()
        mine[0:2, 0:12] = offsets_here[0, 0]
        mine[2:3, 0:1] = jnp.full((1, 1), counts[0, 0], jnp.int32)
        letters = []
        for i, d in enumerate(AROUND):
            letter = pltpu.make_async_remote_copy(
                mine,
                around.at[AROUND.index((-d[0], -d[1]))],
                notes.at[0, i],
                notes.at[1, i],
                device_id={"row": place.row + d[0], "col": place.col + d[1]},
                device_id_type=MESH,
            )
            letters.append(letter)
        pulls[1].wait()
        halo.pack(0)
        pl.semaphore_wait(pltpu.get_barrier_semaphore(), peers)
        for i, d in enumerate(AROUND):
            pl.when(beside(place, d))(letters[i].start)
        halo.start(0)
        pulls[2].wait()
        halo.pack(1)
        halo.start(1)
        for p in range(2):
            halo.pack_rest(p)
            halo.start_rest(p)
        for pull in later:
            pull.start()
        update[...] = jnp.zeros_like(update)
        halo.forward()
        light[...] = jnp.zeros_like(light)
        pulls[3].wait()
        for p in range(2):
            tall[p, 0:8] = tall[p, 128:136]
        power[...] = tall[0] * tall[0] + tall[1] * tall[1]

        def turn(slot, carry):
            live = (slot < counts[0, 0]).astype(jnp.float32)
            low_row, low_col = places[0, 0, 0, slot] & 7, places[0, 0, 1, slot] & 127
            for p in range(2):
                beams[slot, p] = pltpu.roll(tall[p, pl.ds(8 - low_row, 128), :], low_col, 1) * live
            return carry

        lax.fori_loop(0, 12, turn, 0)
        halo.finish()
        for i, d in enumerate(AROUND):
            pl.when(beside(place, d))(letters[i].wait_send)
            pl.when(beside(place, (-d[0], -d[1])))(letters[i].wait_recv)
        for pull in later:
            pull.wait()

    return kernel


def split(x):
    high = x.astype(jnp.bfloat16)
    return high, (x - high.astype(jnp.float32)).astype(jnp.bfloat16)


def dot(a, b):
    return jnp.dot(a, b, preferred_element_type=jnp.float32)


def right_mul(x, high, low):
    xh, xl = split(x)
    return dot(xh, high) + dot(xl, high) + dot(xh, low)


def left_mul(high, low, x):
    xh, xl = split(x)
    return dot(high, xh) + dot(high, xl) + dot(low, xh)


def cross(x):
    return jnp.concatenate(
        [
            jnp.concatenate([x[:128, :128], x[128:, :128]], axis=1),
            jnp.concatenate([x[:128, 128:], x[128:, 128:]], axis=1),
        ],
        axis=0,
    )


def gradient_kernel(with_light):
    def kernel(*refs):
        if with_light:
            offsets, counts, around, ext, beams, measured, tables, _, power, _, update, light, notes, arrived = refs
        else:
            offsets, counts, ext, beams, measured, tables, _, update = refs
        count = counts[0, 0]
        if with_light:
            bring = pltpu.make_async_copy(around, notes, arrived.at[0])
            bring.start()
        lane = lax.broadcasted_iota(jnp.int32, (128, 128), 1)
        sub = lax.broadcasted_iota(jnp.int32, (8, 128), 0)

        def turned(source, shift_rows, shift_lanes):
            return pltpu.roll(source[pl.ds(8 - shift_rows, 128), :], shift_lanes, 1)

        def scatter(dest, first, lanes, shift_rows, shift_lanes, value):
            head = jnp.where(sub >= shift_rows, value[:8], 0.0)
            main = jnp.concatenate([head, value[8:]], axis=0)
            tail = jnp.where(sub < shift_rows, value[:8], 0.0)
            for which, at in enumerate(lanes):
                keep = lane >= shift_lanes if which == 0 else lane < shift_lanes
                dest[pl.ds(first, 128), at] += jnp.where(keep, main, 0.0)
                dest[pl.ds(first + 128, 8), at] += jnp.where(keep[:8], tail, 0.0)

        def tiles_of(col, base, wrap):
            tile = lax.shift_right_arithmetic(col, 7) + base
            first = lax.rem(tile + wrap, wrap)
            second = lax.rem(tile + wrap + 1, wrap)
            return [pl.ds(pl.multiple_of(t * 128, 128), 128) for t in (first, second)]

        def brighten(row, col, value):
            low_row, low_col = jnp.bitwise_and(row, 7), jnp.bitwise_and(col, 127)
            first = pl.multiple_of(row - low_row + 128, 8)
            scatter(light, first, tiles_of(col, 1, 5), low_row, low_col, value)

        def gather(slot):
            row, col = offsets[0, 0, 0, slot], offsets[0, 0, 1, slot]
            low_row, low_col = jnp.bitwise_and(row, 7), jnp.bitwise_and(col, 127)
            first = pl.multiple_of(row - low_row + 64, 8)
            lanes = tiles_of(col, 0, 4)
            beam = [beams[slot, p] for p in range(2)]
            window = []
            for p in range(2):
                main = jnp.where(
                    lane >= low_col, ext[p, pl.ds(first, 128), lanes[0]], ext[p, pl.ds(first, 128), lanes[1]]
                )
                tail = jnp.where(
                    lane[:8] >= low_col,
                    ext[p, pl.ds(first + 128, 8), lanes[0]],
                    ext[p, pl.ds(first + 128, 8), lanes[1]],
                )
                window.append(jnp.concatenate([jnp.where(sub >= low_row, main[:8], tail), main[8:]], axis=0))
            real = beam[0] * window[0] - beam[1] * window[1]
            imag = beam[0] * window[1] + beam[1] * window[0]
            return jnp.concatenate([real, imag], axis=1), (slot, first, lanes, low_row, low_col, row, col)

        def put(back, at):
            slot, first, lanes, low_row, low_col, row, col = at
            beam = [beams[slot, p] for p in range(2)]
            real, imag = back[:, :128], back[:, 128:]
            scatter(update.at[0], first, lanes, low_row, low_col, beam[0] * real + beam[1] * imag)
            scatter(update.at[1], first, lanes, low_row, low_col, beam[0] * imag - beam[1] * real)
            if with_light:
                brighten(row, col, beam[0] * beam[0] + beam[1] * beam[1])

        def block(size):
            slots = list(range(size))
            pairs = [(k, k + 1) for k in range(0, size, 2)]
            got, given, raw = {}, {}, {}

            def fetch(k):
                a, b = pairs[k]
                got[k] = gather(slots[a]), gather(slots[b])
                given[k] = split(jnp.concatenate([got[k][0][0], got[k][1][0]], axis=0))

            def multiply(n, k):
                high, low = given[k]
                if n in (0, 3):
                    t, u = (tables[0], tables[1]) if n == 0 else (tables[2], tables[3])
                    raw[k] = dot(high, t) + dot(low, t) + dot(high, u)
                else:
                    t, u = (tables[2], tables[3]) if n == 1 else (tables[0], tables[1])
                    raw[k] = dot(t, high) + dot(t, low) + dot(u, high)

            def after(n, k):
                a, b = pairs[k]
                x = raw[k]
                if n == 3:
                    put(x[:128], got[k][0][1])
                    put(x[128:], got[k][1][1])
                    return
                if n == 1:
                    real, imag = x[:128], x[128:]
                    known = jnp.concatenate([measured[0, 0, slots[a]], measured[0, 0, slots[b]]], axis=1)
                    ratio = known * lax.rsqrt(real * real + imag * imag + 0.25) - 1.0
                    x = jnp.concatenate([real * ratio, imag * ratio], axis=0)
                else:
                    x = cross(x)
                given[k] = split(x)

            todo = [(n, k) for n in range(4) for k in range(len(pairs))]
            fetch(0)
            for i, (n, k) in enumerate(todo):
                multiply(n, k)
                if n == 0 and k + 1 < len(pairs):
                    fetch(k + 1)
                if i:
                    after(*todo[i - 1])
            after(*todo[-1])

        pl.when(count > 6)(lambda: block(12))
        pl.when(count <= 6)(lambda: block(6))
        if with_light:
            bring.wait()
            for i, d in enumerate(AROUND):

                def other(slot, carry):
                    row = notes[i, 0, slot] + d[0] * 384
                    col = notes[i, 1, slot] + d[1] * 384
                    touches = (row > -128) & (row < 384) & (col > -128) & (col < 384)

                    @pl.when(touches)
                    def _():
                        low_row, low_col = jnp.bitwise_and(row, 7), jnp.bitwise_and(col, 127)
                        brighten(row, col, turned(power, low_row, low_col))

                    return carry

                lax.fori_loop(0, notes[i, 2, 0], other, 0)

    return kernel


def between_kernel(grid):
    def kernel(
        update, light, field,
        ext, cleared, inverse,
        near_in, relay_in, far, side, corner, far_in, side_in, corner_in, sems,
        halo_far, halo_side, halo_corner, halo_far_in, halo_side_in, halo_corner_in, more,
    ):
        place = Place(grid)
        greet(place)
        fold = Fold(place, update, near_in, relay_in, far, side, corner, far_in, side_in, corner_in, sems)
        halo = Halo(place, ext, halo_far, halo_side, halo_corner, halo_far_in, halo_side_in, halo_corner_in, more)
        fold.pack()
        greeted(place)
        fold.start(True)
        halo.clear()
        inverse[...] = 1.0 / (light[128:512, 128:512] + 1.0)
        for p in range(2):
            ext[p, 64:448, 0:384] = field[p, 64:448, 0:384] + update[p, 64:448, 0:384] * inverse[...]
        cleared[...] = jnp.zeros_like(cleared)
        fold.finish(0, ext, 64, inverse, lambda: halo.pack_rest(0))
        halo.pack(0)
        halo.start(0)

        def meanwhile():
            halo.start_rest(0)
            halo.pack_rest(1)

        fold.finish(1, ext, 64, inverse, meanwhile)
        halo.pack(1)
        halo.start(1)
        halo.start_rest(1)
        halo.forward()
        halo.finish()
        fold.close()

    return kernel


def last_kernel(grid):
    def kernel(update, inverse, ext, out, near_in, relay_in, far, side, corner, far_in, side_in, corner_in, sems):
        place = Place(grid)
        greet(place)
        fold = Fold(place, update, near_in, relay_in, far, side, corner, far_in, side_in, corner_in, sems)
        fold.pack()
        greeted(place)
        fold.start(False)
        for p in range(2):
            out[p] = ext[p, 64:448, 0:384] + update[p, 64:448, 0:384] * inverse[...]
        for p in range(2):
            fold.finish(p, out, 0, inverse)
        fold.close()

    return kernel


def hold(x):
    return pltpu.with_memory_space_constraint(x, pltpu.MemorySpace.HBM)


def params(collective_id=None):
    if collective_id is None:
        return pltpu.CompilerParams(vmem_limit_bytes=LIMIT)
    return pltpu.CompilerParams(collective_id=collective_id, has_side_effects=True, vmem_limit_bytes=LIMIT)


def shards(grid, tables, object_field, probe, amplitudes, offsets, counts):
    f32, i32 = jnp.float32, jnp.int32
    shape = jax.ShapeDtypeStruct
    ext_shape, light_shape = shape((2, 512, 512), f32), shape((648, 640), f32)
    offsets = jnp.swapaxes(offsets, 2, 3)
    packs = [pltpu.VMEM((2, 64, 256), f32), pltpu.VMEM((2, 2, 192, 128), f32), pltpu.VMEM((2, 2, 64, 128), f32)]
    folds = [pltpu.VMEM((2, 64, 384), f32), pltpu.VMEM((2, 64, 128), f32)] + packs + packs
    sems = pltpu.SemaphoreType.DMA((2, 2, 11))
    ext, around, measured, tables, beams, power, update, light = pl.pallas_call(
        spread_kernel(grid),
        name="spread",
        out_shape=(
            ext_shape,
            shape((8, 8, 128), i32),
            shape(amplitudes.shape, f32),
            shape(tables.shape, tables.dtype),
            shape((12, 2, 128, 128), f32),
            shape((136, 128), f32),
            ext_shape,
            light_shape,
        ),
        in_specs=[HBM, HBM, SMEM, SMEM, HBM, HBM, HBM],
        out_specs=(VMEM,) * 8,
        scratch_shapes=[pltpu.VMEM((8, 128), i32), pltpu.VMEM((1, 1, 2, 12), i32), pltpu.VMEM((2, 136, 128), f32)]
        + packs
        + packs
        + [sems, pltpu.SemaphoreType.DMA((2, 8)), pltpu.SemaphoreType.DMA((6,))],
        compiler_params=params(0),
    )(hold(object_field), hold(offsets), counts, offsets, hold(amplitudes), hold(tables), hold(probe))
    update, light = pl.pallas_call(
        gradient_kernel(True),
        name="gradient_light",
        out_shape=(ext_shape, light_shape),
        in_specs=[SMEM] * 2 + [VMEM] * 8,
        out_specs=(VMEM,) * 2,
        scratch_shapes=[pltpu.SMEM((8, 8, 128), i32), pltpu.SemaphoreType.DMA((1,))],
        input_output_aliases={7: 0, 9: 1},
        compiler_params=params(),
    )(offsets, counts, around, ext, beams, measured, tables, update, power, light)
    ext, cleared, inverse = pl.pallas_call(
        between_kernel(grid),
        name="between",
        out_shape=(ext_shape, ext_shape, shape((384, 384), f32)),
        in_specs=[VMEM] * 3,
        out_specs=(VMEM,) * 3,
        scratch_shapes=folds + [sems] + packs + packs + [sems],
        compiler_params=params(1),
    )(update, light, ext)
    update = pl.pallas_call(
        gradient_kernel(False),
        name="gradient",
        out_shape=ext_shape,
        in_specs=[SMEM] * 2 + [VMEM] * 5,
        out_specs=VMEM,
        input_output_aliases={6: 0},
        compiler_params=params(),
    )(offsets, counts, ext, beams, measured, tables, cleared)
    return pl.pallas_call(
        last_kernel(grid),
        name="last",
        out_shape=shape((2, 384, 384), f32),
        in_specs=[VMEM] * 3,
        out_specs=VMEM,
        scratch_shapes=folds + [sems],
        compiler_params=params(2),
    )(update, inverse, ext)


def solution(mesh):
    grid = (mesh.shape["row"], mesh.shape["col"])
    tables = dft_tables(128)
    placed = (
        P(None, "row", "col"),
        P(),
        P("row", "col", None, None, None),
        P("row", "col", None, None),
        P("row", "col"),
    )

    def body(*args):
        return shards(grid, jnp.asarray(tables), *args)

    return jax.shard_map(body, mesh=mesh, in_specs=placed, out_specs=P(None, "row", "col"), check_vma=False)
```

```python
import math

import jax
import jax.numpy as jnp
import numpy as np
from jax import lax
from jax.experimental import pallas as pl
from jax.experimental.pallas import tpu as pltpu
from jax.sharding import PartitionSpec as P

AROUND = ((-1, 0), (1, 0), (0, -1), (0, 1), (-1, -1), (-1, 1), (1, -1), (1, 1))
MESH = pl.DeviceIdType.MESH
VMEM = pl.BlockSpec(memory_space=pltpu.VMEM)
SMEM = pl.BlockSpec(memory_space=pltpu.SMEM)
HBM = pl.BlockSpec(memory_space=pltpu.MemorySpace.HBM)
LIMIT = 24 << 20
NEAR, FAR, LEFT, RIGHT, FAR_LEFT, FAR_RIGHT, LEFT_NEXT, RIGHT_NEXT, RELAY, EDGE_LEFT, EDGE_RIGHT = range(11)
DIAGONAL = (FAR_LEFT, FAR_RIGHT, EDGE_LEFT, EDGE_RIGHT)


def dft_tables(length):
    index = np.arange(length)
    angle = (np.outer(index, index) % length) * (2.0 * math.pi / length)
    cosine, sine = np.cos(angle) / math.sqrt(length), np.sin(angle) / math.sqrt(length)
    table = np.block([[cosine, -sine], [sine, cosine]])
    high = table.astype(jnp.bfloat16)
    low = (table - high.astype(np.float64)).astype(jnp.bfloat16)
    return np.stack([high, low, high.T, low.T])


def swap(x):
    return pltpu.roll(x, 64, x.ndim - 1)


def lower(rows):
    return lax.broadcasted_iota(jnp.int32, (rows, 128), 1) < 64


def pack(x, keep_low):
    rows = x.shape[0] // 2
    keep = lower(rows) if keep_low else ~lower(rows)
    return jnp.where(keep, x[:rows], swap(x[rows:]))


def unpack(x):
    return jnp.concatenate([x, swap(x)], axis=0)


def merge(a, b):
    keep = lower(a.shape[0])
    return jnp.concatenate([jnp.where(keep, a, b), jnp.where(keep, swap(a), swap(b))], axis=0)


class Place:
    def __init__(self, grid):
        self.row, self.col = lax.axis_index("row"), lax.axis_index("col")
        self.odd = lax.rem(self.row, 2)
        self.near_row = self.row + 1 - 2 * self.odd
        self.far_row = self.row - 1 + 2 * self.odd
        self.grid = grid
        far = (self.far_row >= 0) & (self.far_row < grid[0])
        left, right = self.col > 0, self.col < grid[1] - 1
        self.far, self.left, self.right = far, left, right
        ends = (far & jnp.logical_not(left), far & jnp.logical_not(right))
        both = (None, far, left, right, far & left, far & right, left, right, None) + ends
        self.sends = both
        order = (NEAR, FAR, RIGHT, LEFT, FAR_RIGHT, FAR_LEFT, RIGHT_NEXT, LEFT_NEXT, RELAY, EDGE_LEFT, EDGE_RIGHT)
        self.gets = tuple(both[i] for i in order)
        self.near_border = self.pick(320, 0)
        self.far_border = self.pick(0, 320)
        self.near_halo = self.pick(448, 0)
        self.far_halo = self.pick(0, 448)

    def pick(self, even, odd):
        return pl.multiple_of(even + self.odd * (odd - even), 64)

    def target(self, which):
        row = {NEAR: self.near_row, RELAY: self.near_row, FAR: self.far_row}
        row.update({which: self.far_row for which in DIAGONAL})
        side = {LEFT: -1, FAR_LEFT: -1, LEFT_NEXT: -1, RIGHT: 1, FAR_RIGHT: 1, RIGHT_NEXT: 1}
        return {"row": row.get(which, self.row), "col": self.col + side.get(which, 0)}


def when(condition, body):
    if condition is None:
        body()
    else:
        pl.when(condition)(body)


def greet(place):
    barrier = pltpu.get_barrier_semaphore()
    for which in (NEAR, FAR, LEFT, RIGHT, FAR_LEFT, FAR_RIGHT):
        when(
            place.sends[which],
            lambda: pl.semaphore_signal(
                barrier, inc=1, device_id=place.target(which), device_id_type=MESH
            ),
        )


def greeted(place):
    far, left, right = (jnp.where(x, 1, 0) for x in (place.far, place.left, place.right))
    pl.semaphore_wait(pltpu.get_barrier_semaphore(), 1 + far + (left + right) * (1 + far))


def greet_all(place):
    barrier = pltpu.get_barrier_semaphore()
    count = 0
    for d in AROUND:
        count += jnp.where(beside(place, d), 1, 0)

        @pl.when(beside(place, d))
        def _():
            pl.semaphore_signal(
                barrier, inc=1, device_id={"row": place.row + d[0], "col": place.col + d[1]}, device_id_type=MESH
            )

    return count


def beside(place, d):
    row, col = place.row + d[0], place.col + d[1]
    return (row >= 0) & (row < place.grid[0]) & (col >= 0) & (col < place.grid[1])


def remote(place, which, src, dst, sems, p):
    return pltpu.make_async_remote_copy(
        src, dst, sems.at[0, p, which], sems.at[1, p, which], device_id=place.target(which), device_id_type=MESH
    )


def start(place, copies, *which):
    for i in which:
        when(place.sends[i], copies[i].start)


def wait_recv(place, copies, *which):
    for i in which:
        when(place.gets[i], copies[i].wait_recv)


def wait_send(place, copies, gone, *which):
    for i in which or range(len(copies)):
        if i not in gone:
            when(place.sends[i], copies[i].wait_send)
    gone.update(which or range(len(copies)))


def strips(far, far_in, side, side_in, corner, corner_in, p):
    return {
        FAR: (far.at[p], far_in.at[p]),
        FAR_LEFT: (corner.at[0, p], corner_in.at[0, p]),
        FAR_RIGHT: (corner.at[1, p], corner_in.at[1, p]),
        EDGE_LEFT: (corner.at[0, p], corner_in.at[1, p]),
        EDGE_RIGHT: (corner.at[1, p], corner_in.at[0, p]),
        LEFT: (side.at[0, p, 0:64], side_in.at[0, p, 0:64]),
        RIGHT: (side.at[1, p, 0:64], side_in.at[1, p, 0:64]),
        LEFT_NEXT: (side.at[0, p, 64:192], side_in.at[0, p, 64:192]),
        RIGHT_NEXT: (side.at[1, p, 64:192], side_in.at[1, p, 64:192]),
    }


def at_rows(first, rows):
    return pl.ds(pl.multiple_of(first, 64), rows)


class Halo:
    def __init__(self, place, ext, far, side, corner, far_in, side_in, corner_in, sems):
        self.place, self.ext, self.far, self.far_in = place, ext, far, far_in
        self.gone = (set(), set())
        self.side, self.corner, self.side_in, self.corner_in = side, corner, side_in, corner_in
        near, target = at_rows(place.near_border + 64, 64), at_rows(place.far_halo, 64)
        self.copies = []
        for p in range(2):
            ends = strips(far, far_in, side, side_in, corner, corner_in, p)
            ends[NEAR] = (ext.at[p, near, 0:384], ext.at[p, target, 0:384])
            ends[RELAY] = (ext.at[p, near, 384:512], ext.at[p, target, 384:512])
            self.copies.append([remote(place, i, *ends[i], sems, p) for i in range(11)])

    def clear(self):
        place = self.place

        @pl.when(jnp.logical_not(place.far))
        def _():
            self.far_in[...] = jnp.zeros((2, 64, 256), jnp.float32)
            self.corner_in[...] = jnp.zeros((2, 2, 64, 128), jnp.float32)

        for k, side in enumerate((place.right, place.left)):

            @pl.when(jnp.logical_not(side))
            def _():
                self.side_in[k] = jnp.zeros((2, 192, 128), jnp.float32)

    def pack(self, p):
        place, ext = self.place, self.ext
        for k, lane in enumerate((0, 256)):
            for i, first in enumerate((place.near_border, place.far_border)):
                self.side[k, p, 32 * i : 32 * i + 32] = pack(ext[p, at_rows(first + 64, 64), lane : lane + 128], k == 0)
        rows = at_rows(place.far_border + 64, 64)
        self.far[p, :, 0:128] = ext[p, rows, 128:256]
        self.far[p, :, 128:256] = jnp.where(lower(64), ext[p, rows, 256:384], ext[p, rows, 0:128])

    def pack_rest(self, p):
        for k, lane in enumerate((0, 256)):
            self.side[k, p, 64:192] = pack(self.ext[p, 128:384, lane : lane + 128], k == 0)

    def start(self, p):
        start(self.place, self.copies[p], LEFT, RIGHT, FAR)

    def start_rest(self, p):
        wait_send(self.place, self.copies[p], self.gone[p], LEFT, RIGHT)
        start(self.place, self.copies[p], LEFT_NEXT, RIGHT_NEXT, NEAR)

    def forward(self):
        place, ext, low = self.place, self.ext, lower(64)
        for p in range(2):
            wait_recv(place, self.copies[p], LEFT, RIGHT)
            for i, first in enumerate((place.near_border, place.far_border)):
                parts = [self.side_in[k, p, 32 * i : 32 * i + 32] for k in range(2)]
                ext[p, at_rows(first + 64, 64), 384:512] = merge(*parts)
            start(place, self.copies[p], RELAY)
            rows = at_rows(place.far_border + 64, 64)
            self.corner[0, p] = jnp.where(low, ext[p, rows, 0:128], ext[p, rows, 384:512])
            self.corner[1, p] = jnp.where(low, ext[p, rows, 384:512], ext[p, rows, 256:384])
            start(place, self.copies[p], *DIAGONAL)

    def finish(self):
        place, ext, low = self.place, self.ext, lower(64)
        for p in range(2):
            wait_recv(place, self.copies[p], LEFT_NEXT, RIGHT_NEXT)
            ext[p, 128:384, 384:512] = merge(self.side_in[0, p, 64:192], self.side_in[1, p, 64:192])
            wait_recv(place, self.copies[p], FAR, *DIAGONAL)
            rows = at_rows(place.far_halo, 64)
            right, left = self.corner_in[0, p], self.corner_in[1, p]
            mixed = self.far_in[p, :, 128:256]
            ext[p, rows, 0:128] = jnp.where(low, left, mixed)
            ext[p, rows, 128:256] = self.far_in[p, :, 0:128]
            ext[p, rows, 256:384] = jnp.where(low, mixed, right)
            ext[p, rows, 384:512] = jnp.where(low, right, left)
        for p in range(2):
            wait_recv(place, self.copies[p], NEAR, RELAY)
            wait_send(place, self.copies[p], self.gone[p])


class Fold:
    def __init__(self, place, update, near_in, relay_in, far, side, corner, far_in, side_in, corner_in, sems):
        self.place, self.update, self.near_in, self.relay_in = place, update, near_in, relay_in
        self.far, self.far_in = far, far_in
        self.gone = (set(), set())
        self.side, self.corner, self.side_in, self.corner_in = side, corner, side_in, corner_in
        near = at_rows(place.near_halo, 64)
        self.copies = []
        for p in range(2):
            ends = strips(far, far_in, side, side_in, corner, corner_in, p)
            ends[NEAR] = (update.at[p, near, 0:384], near_in.at[p])
            ends[RELAY] = (update.at[p, near, 384:512], relay_in.at[p])
            self.copies.append([remote(place, i, *ends[i], sems, p) for i in range(11)])

    def pack(self):
        place, update, low = self.place, self.update, lower(64)

        @pl.when(jnp.logical_not(place.far))
        def _():
            self.corner_in[...] = jnp.zeros((2, 2, 64, 128), jnp.float32)

        rows = at_rows(place.far_halo, 64)
        for p in range(2):
            tiles = [update[p, rows, 128 * t : 128 * t + 128] for t in range(4)]
            self.corner[0, p] = jnp.where(low, tiles[0], tiles[3])
            self.corner[1, p] = jnp.where(low, tiles[3], tiles[2])
            self.far[p, :, 0:128] = tiles[1]
            self.far[p, :, 128:256] = jnp.where(low, tiles[2], tiles[0])
            for k in range(2):
                self.side[k, p, 64:192] = pack(update[p, 128:384, 384:512], k == 1)

    def start(self, paced):
        place, update = self.place, self.update
        for p in range(2):
            start(place, self.copies[p], *DIAGONAL, RELAY)
        start(place, self.copies[0], FAR, LEFT_NEXT, RIGHT_NEXT)
        if not paced:
            start(place, self.copies[1], FAR)
        for p in range(2):
            wait_recv(place, self.copies[p], RELAY, *DIAGONAL)
            extra = (self.relay_in[p], jnp.where(lower(64), self.corner_in[0, p], self.corner_in[1, p]))
            for i, first in enumerate((place.near_border, place.far_border)):
                part = update[p, at_rows(first + 64, 64), 384:512] + extra[i]
                for k in range(2):
                    self.side[k, p, 32 * i : 32 * i + 32] = pack(part, k == 1)
            start(place, self.copies[p], LEFT, RIGHT)
            if p == 0 and paced:
                start(place, self.copies[0], NEAR)
                wait_send(place, self.copies[0], self.gone[0], FAR, LEFT_NEXT, RIGHT_NEXT)
                start(place, self.copies[1], FAR)
            if p == 0:
                start(place, self.copies[1], LEFT_NEXT, RIGHT_NEXT)
        if not paced:
            start(place, self.copies[0], NEAR)
        start(place, self.copies[1], NEAR)

    def finish(self, p, dest, base, inverse, between=None):
        place = self.place
        sides = ((place.right, 256, lambda x: jnp.where(lower(x.shape[0]), 0.0, x)), (place.left, 0, lambda x: jnp.where(lower(x.shape[0]), x, 0.0)))

        def add(first, lane, value):
            lanes, rows = pl.ds(lane, value.shape[1]), value.shape[0]
            dest[p, at_rows(first + base, rows), lanes] += value * inverse[at_rows(first, rows), lanes]

        wait_recv(place, self.copies[p], NEAR)
        add(place.near_border, 0, self.near_in[p])

        @pl.when(place.far)
        def _():
            self.copies[p][FAR].wait_recv()
            mixed = self.far_in[p, :, 128:256]
            add(place.far_border, 0, jnp.where(lower(64), self.corner_in[1, p], mixed))
            add(place.far_border, 128, self.far_in[p, :, 0:128])
            add(place.far_border, 256, jnp.where(lower(64), mixed, self.corner_in[0, p]))

        for k, (here, lane, keep) in enumerate(sides):

            @pl.when(here)
            def _():
                self.copies[p][LEFT_NEXT + k].wait_recv()
                add(64, lane, keep(unpack(self.side_in[k, p, 64:192])))

        if between is not None:
            between()
        for k, (here, lane, keep) in enumerate(sides):

            @pl.when(here)
            def _():
                self.copies[p][LEFT + k].wait_recv()
                add(place.near_border, lane, keep(unpack(self.side_in[k, p, 0:32])))
                add(place.far_border, lane, keep(unpack(self.side_in[k, p, 32:64])))

    def close(self):
        for p in range(2):
            wait_send(self.place, self.copies[p], self.gone[p])


def spread_kernel(grid):
    def kernel(
        field, offsets, counts, measured, tables, probe,
        ext, around, measured_here, tables_here, beams, power, update, light, places,
        mine, offsets_here, tall, far, side, corner, far_in, side_in, corner_in, sems, notes, local,
    ):
        place = Place(grid)
        peers = greet_all(place)
        pulls = [pltpu.make_async_copy(offsets, offsets_here, local.at[0])]
        pulls += [pltpu.make_async_copy(field.at[p], ext.at[p, 64:448, 0:384], local.at[1 + p]) for p in range(2)]
        later = [
            pltpu.make_async_copy(measured, measured_here, local.at[3]),
            pltpu.make_async_copy(tables, tables_here, local.at[4]),
        ]
        pulls.append(pltpu.make_async_copy(probe, tall.at[:, 8:136], local.at[5]))
        pulls.append(pltpu.make_async_copy(offsets, places, local.at[6]))
        for pull in pulls:
            pull.start()
        halo = Halo(place, ext, far, side, corner, far_in, side_in, corner_in, sems)
        halo.clear()
        for i, d in enumerate(AROUND):

            @pl.when(jnp.logical_not(beside(place, d)))
            def _():
                around[i] = jnp.zeros((8, 128), jnp.int32)

        pulls[0].wait()
        mine[0:2, 0:12] = offsets_here[0, 0]
        mine[2:3, 0:1] = jnp.full((1, 1), counts[0, 0], jnp.int32)
        letters = []
        for i, d in enumerate(AROUND):
            letter = pltpu.make_async_remote_copy(
                mine,
                around.at[AROUND.index((-d[0], -d[1]))],
                notes.at[0, i],
                notes.at[1, i],
                device_id={"row": place.row + d[0], "col": place.col + d[1]},
                device_id_type=MESH,
            )
            letters.append(letter)
        pulls[1].wait()
        halo.pack(0)
        pl.semaphore_wait(pltpu.get_barrier_semaphore(), peers)
        for i, d in enumerate(AROUND):
            pl.when(beside(place, d))(letters[i].start)
        halo.start(0)
        pulls[2].wait()
        halo.pack(1)
        halo.start(1)
        for p in range(2):
            halo.pack_rest(p)
            halo.start_rest(p)
        for pull in later:
            pull.start()
        update[...] = jnp.zeros_like(update)
        halo.forward()
        light[...] = jnp.zeros_like(light)
        pulls[3].wait()
        pulls[4].wait()
        for p in range(2):
            tall[p, 0:8] = tall[p, 128:136]
        power[...] = tall[0] * tall[0] + tall[1] * tall[1]

        def turn(slot, carry):
            live = (slot < counts[0, 0]).astype(jnp.float32)
            low_row, low_col = places[0, 0, 0, slot] & 7, places[0, 0, 1, slot] & 127
            for p in range(2):
                beams[slot, p] = pltpu.roll(tall[p, pl.ds(8 - low_row, 128), :], low_col, 1) * live
            return carry

        lax.fori_loop(0, 12, turn, 0)
        halo.finish()
        for i, d in enumerate(AROUND):
            pl.when(beside(place, d))(letters[i].wait_send)
            pl.when(beside(place, (-d[0], -d[1])))(letters[i].wait_recv)
        for pull in later:
            pull.wait()

    return kernel


def split(x):
    high = x.astype(jnp.bfloat16)
    return high, (x - high.astype(jnp.float32)).astype(jnp.bfloat16)


def dot(a, b):
    return jnp.dot(a, b, preferred_element_type=jnp.float32)


def right_mul(x, high, low):
    xh, xl = split(x)
    return dot(xh, high) + dot(xl, high) + dot(xh, low)


def left_mul(high, low, x):
    xh, xl = split(x)
    return dot(high, xh) + dot(high, xl) + dot(low, xh)


def cross(x):
    return jnp.concatenate(
        [
            jnp.concatenate([x[:128, :128], x[128:, :128]], axis=1),
            jnp.concatenate([x[:128, 128:], x[128:, 128:]], axis=1),
        ],
        axis=0,
    )


def gradient_kernel(with_light):
    def kernel(*refs):
        if with_light:
            offsets, counts, around, ext, beams, measured, tables, _, power, _, update, light, notes, arrived = refs
        else:
            offsets, counts, ext, beams, measured, tables, _, update = refs
        count = counts[0, 0]
        if with_light:
            bring = pltpu.make_async_copy(around, notes, arrived.at[0])
            bring.start()
        lane = lax.broadcasted_iota(jnp.int32, (128, 128), 1)
        sub = lax.broadcasted_iota(jnp.int32, (8, 128), 0)

        def turned(source, shift_rows, shift_lanes):
            return pltpu.roll(source[pl.ds(8 - shift_rows, 128), :], shift_lanes, 1)

        def scatter(dest, first, lanes, shift_rows, shift_lanes, value):
            head = jnp.where(sub >= shift_rows, value[:8], 0.0)
            main = jnp.concatenate([head, value[8:]], axis=0)
            tail = jnp.where(sub < shift_rows, value[:8], 0.0)
            for which, at in enumerate(lanes):
                keep = lane >= shift_lanes if which == 0 else lane < shift_lanes
                dest[pl.ds(first, 128), at] += jnp.where(keep, main, 0.0)
                dest[pl.ds(first + 128, 8), at] += jnp.where(keep[:8], tail, 0.0)

        def tiles_of(col, base, wrap):
            tile = lax.shift_right_arithmetic(col, 7) + base
            first = lax.rem(tile + wrap, wrap)
            second = lax.rem(tile + wrap + 1, wrap)
            return [pl.ds(pl.multiple_of(t * 128, 128), 128) for t in (first, second)]

        def brighten(row, col, value):
            low_row, low_col = jnp.bitwise_and(row, 7), jnp.bitwise_and(col, 127)
            first = pl.multiple_of(row - low_row + 128, 8)
            scatter(light, first, tiles_of(col, 1, 5), low_row, low_col, value)

        def gather(slot):
            row, col = offsets[0, 0, 0, slot], offsets[0, 0, 1, slot]
            low_row, low_col = jnp.bitwise_and(row, 7), jnp.bitwise_and(col, 127)
            first = pl.multiple_of(row - low_row + 64, 8)
            lanes = tiles_of(col, 0, 4)
            beam = [beams[slot, p] for p in range(2)]
            window = []
            for p in range(2):
                main = jnp.where(
                    lane >= low_col, ext[p, pl.ds(first, 128), lanes[0]], ext[p, pl.ds(first, 128), lanes[1]]
                )
                tail = jnp.where(
                    lane[:8] >= low_col,
                    ext[p, pl.ds(first + 128, 8), lanes[0]],
                    ext[p, pl.ds(first + 128, 8), lanes[1]],
                )
                window.append(jnp.concatenate([jnp.where(sub >= low_row, main[:8], tail), main[8:]], axis=0))
            real = beam[0] * window[0] - beam[1] * window[1]
            imag = beam[0] * window[1] + beam[1] * window[0]
            return jnp.concatenate([real, imag], axis=1), (slot, first, lanes, low_row, low_col, row, col)

        def put(back, at):
            slot, first, lanes, low_row, low_col, row, col = at
            beam = [beams[slot, p] for p in range(2)]
            real, imag = back[:, :128], back[:, 128:]
            scatter(update.at[0], first, lanes, low_row, low_col, beam[0] * real + beam[1] * imag)
            scatter(update.at[1], first, lanes, low_row, low_col, beam[0] * imag - beam[1] * real)
            if with_light:
                brighten(row, col, beam[0] * beam[0] + beam[1] * beam[1])

        def block(size):
            slots = list(range(size))
            pairs = [(k, k + 1) for k in range(0, size, 2)]
            got, given, raw = {}, {}, {}

            def fetch(k):
                a, b = pairs[k]
                got[k] = gather(slots[a]), gather(slots[b])
                given[k] = split(jnp.concatenate([got[k][0][0], got[k][1][0]], axis=0))

            def multiply(n, k):
                high, low = given[k]
                if n in (0, 3):
                    t, u = (tables[0], tables[1]) if n == 0 else (tables[2], tables[3])
                    raw[k] = dot(high, t) + dot(low, t) + dot(high, u)
                else:
                    t, u = (tables[2], tables[3]) if n == 1 else (tables[0], tables[1])
                    raw[k] = dot(t, high) + dot(t, low) + dot(u, high)

            def after(n, k):
                a, b = pairs[k]
                x = raw[k]
                if n == 3:
                    put(x[:128], got[k][0][1])
                    put(x[128:], got[k][1][1])
                    return
                if n == 1:
                    real, imag = x[:128], x[128:]
                    known = jnp.concatenate([measured[0, 0, slots[a]], measured[0, 0, slots[b]]], axis=1)
                    ratio = known * lax.rsqrt(real * real + imag * imag + 0.25) - 1.0
                    x = jnp.concatenate([real * ratio, imag * ratio], axis=0)
                else:
                    x = cross(x)
                given[k] = split(x)

            todo = [(n, k) for n in range(4) for k in range(len(pairs))]
            fetch(0)
            for i, (n, k) in enumerate(todo):
                multiply(n, k)
                if n == 0 and k + 1 < len(pairs):
                    fetch(k + 1)
                if i:
                    after(*todo[i - 1])
            after(*todo[-1])

        pl.when(count > 6)(lambda: block(12))
        pl.when(count <= 6)(lambda: block(6))
        if with_light:
            bring.wait()
            for i, d in enumerate(AROUND):

                def other(slot, carry):
                    row = notes[i, 0, slot] + d[0] * 384
                    col = notes[i, 1, slot] + d[1] * 384
                    touches = (row > -128) & (row < 384) & (col > -128) & (col < 384)

                    @pl.when(touches)
                    def _():
                        low_row, low_col = jnp.bitwise_and(row, 7), jnp.bitwise_and(col, 127)
                        brighten(row, col, turned(power, low_row, low_col))

                    return carry

                lax.fori_loop(0, notes[i, 2, 0], other, 0)

    return kernel


def between_kernel(grid):
    def kernel(
        update, light, field,
        ext, cleared, inverse,
        near_in, relay_in, far, side, corner, far_in, side_in, corner_in, sems,
        halo_far, halo_side, halo_corner, halo_far_in, halo_side_in, halo_corner_in, more,
    ):
        place = Place(grid)
        greet(place)
        fold = Fold(place, update, near_in, relay_in, far, side, corner, far_in, side_in, corner_in, sems)
        halo = Halo(place, ext, halo_far, halo_side, halo_corner, halo_far_in, halo_side_in, halo_corner_in, more)
        fold.pack()
        greeted(place)
        fold.start(True)
        halo.clear()
        inverse[...] = 1.0 / (light[128:512, 128:512] + 1.0)
        for p in range(2):
            ext[p, 64:448, 0:384] = field[p, 64:448, 0:384] + update[p, 64:448, 0:384] * inverse[...]
        cleared[...] = jnp.zeros_like(cleared)
        fold.finish(0, ext, 64, inverse, lambda: halo.pack_rest(0))
        halo.pack(0)
        halo.start(0)

        def meanwhile():
            halo.start_rest(0)
            halo.pack_rest(1)

        fold.finish(1, ext, 64, inverse, meanwhile)
        halo.pack(1)
        halo.start(1)
        halo.start_rest(1)
        halo.forward()
        halo.finish()
        fold.close()

    return kernel


def last_kernel(grid):
    def kernel(update, inverse, ext, out, near_in, relay_in, far, side, corner, far_in, side_in, corner_in, sems):
        place = Place(grid)
        greet(place)
        fold = Fold(place, update, near_in, relay_in, far, side, corner, far_in, side_in, corner_in, sems)
        fold.pack()
        greeted(place)
        fold.start(False)
        for p in range(2):
            out[p] = ext[p, 64:448, 0:384] + update[p, 64:448, 0:384] * inverse[...]
        for p in range(2):
            fold.finish(p, out, 0, inverse)
        fold.close()

    return kernel


def hold(x):
    return pltpu.with_memory_space_constraint(x, pltpu.MemorySpace.HBM)


def params(collective_id=None):
    if collective_id is None:
        return pltpu.CompilerParams(vmem_limit_bytes=LIMIT)
    return pltpu.CompilerParams(collective_id=collective_id, has_side_effects=True, vmem_limit_bytes=LIMIT)


def shards(grid, tables, object_field, probe, amplitudes, offsets, counts):
    f32, i32 = jnp.float32, jnp.int32
    shape = jax.ShapeDtypeStruct
    ext_shape, light_shape = shape((2, 512, 512), f32), shape((648, 640), f32)
    offsets = jnp.swapaxes(offsets, 2, 3)
    packs = [pltpu.VMEM((2, 64, 256), f32), pltpu.VMEM((2, 2, 192, 128), f32), pltpu.VMEM((2, 2, 64, 128), f32)]
    folds = [pltpu.VMEM((2, 64, 384), f32), pltpu.VMEM((2, 64, 128), f32)] + packs + packs
    sems = pltpu.SemaphoreType.DMA((2, 2, 11))
    ext, around, measured, tables, beams, power, update, light, places = pl.pallas_call(
        spread_kernel(grid),
        name="spread",
        out_shape=(
            ext_shape,
            shape((8, 8, 128), i32),
            shape(amplitudes.shape, f32),
            shape(tables.shape, tables.dtype),
            shape((12, 2, 128, 128), f32),
            shape((136, 128), f32),
            ext_shape,
            light_shape,
            shape((1, 1, 2, 12), i32),
        ),
        in_specs=[HBM, HBM, SMEM, HBM, HBM, HBM],
        out_specs=(VMEM,) * 8 + (SMEM,),
        scratch_shapes=[pltpu.VMEM((8, 128), i32), pltpu.VMEM((1, 1, 2, 12), i32), pltpu.VMEM((2, 136, 128), f32)]
        + packs
        + packs
        + [sems, pltpu.SemaphoreType.DMA((2, 8)), pltpu.SemaphoreType.DMA((7,))],
        compiler_params=params(0),
    )(hold(object_field), hold(offsets), counts, hold(amplitudes), hold(tables), hold(probe))
    update, light = pl.pallas_call(
        gradient_kernel(True),
        name="gradient_light",
        out_shape=(ext_shape, light_shape),
        in_specs=[SMEM] * 2 + [VMEM] * 8,
        out_specs=(VMEM,) * 2,
        scratch_shapes=[pltpu.SMEM((8, 8, 128), i32), pltpu.SemaphoreType.DMA((1,))],
        input_output_aliases={7: 0, 9: 1},
        compiler_params=params(),
    )(places, counts, around, ext, beams, measured, tables, update, power, light)
    ext, cleared, inverse = pl.pallas_call(
        between_kernel(grid),
        name="between",
        out_shape=(ext_shape, ext_shape, shape((384, 384), f32)),
        in_specs=[VMEM] * 3,
        out_specs=(VMEM,) * 3,
        scratch_shapes=folds + [sems] + packs + packs + [sems],
        compiler_params=params(1),
    )(update, light, ext)
    update = pl.pallas_call(
        gradient_kernel(False),
        name="gradient",
        out_shape=ext_shape,
        in_specs=[SMEM] * 2 + [VMEM] * 5,
        out_specs=VMEM,
        input_output_aliases={6: 0},
        compiler_params=params(),
    )(places, counts, ext, beams, measured, tables, cleared)
    return pl.pallas_call(
        last_kernel(grid),
        name="last",
        out_shape=shape((2, 384, 384), f32),
        in_specs=[VMEM] * 3,
        out_specs=VMEM,
        scratch_shapes=folds + [sems],
        compiler_params=params(2),
    )(update, inverse, ext)


def solution(mesh):
    grid = (mesh.shape["row"], mesh.shape["col"])
    tables = dft_tables(128)
    placed = (
        P(None, "row", "col"),
        P(),
        P("row", "col", None, None, None),
        P("row", "col", None, None),
        P("row", "col"),
    )

    def body(*args):
        return shards(grid, jnp.asarray(tables), *args)

    return jax.shard_map(body, mesh=mesh, in_specs=placed, out_specs=P(None, "row", "col"), check_vma=False)
```

```python
import math

import jax
import jax.numpy as jnp
import numpy as np
from jax import lax
from jax.experimental import pallas as pl
from jax.experimental.pallas import tpu as pltpu
from jax.sharding import PartitionSpec as P

AROUND = ((-1, 0), (1, 0), (0, -1), (0, 1), (-1, -1), (-1, 1), (1, -1), (1, 1))
MESH = pl.DeviceIdType.MESH
VMEM = pl.BlockSpec(memory_space=pltpu.VMEM)
SMEM = pl.BlockSpec(memory_space=pltpu.SMEM)
HBM = pl.BlockSpec(memory_space=pltpu.MemorySpace.HBM)
LIMIT = 24 << 20
NEAR, FAR, LEFT, RIGHT, FAR_LEFT, FAR_RIGHT, LEFT_NEXT, RIGHT_NEXT, RELAY, EDGE_LEFT, EDGE_RIGHT = range(11)
DIAGONAL = (FAR_LEFT, FAR_RIGHT, EDGE_LEFT, EDGE_RIGHT)


def dft_tables(length):
    index = np.arange(length)
    angle = (np.outer(index, index) % length) * (2.0 * math.pi / length)
    cosine, sine = np.cos(angle) / math.sqrt(length), np.sin(angle) / math.sqrt(length)
    table = np.block([[cosine, -sine], [sine, cosine]])
    high = table.astype(jnp.bfloat16)
    low = (table - high.astype(np.float64)).astype(jnp.bfloat16)
    return np.stack([high, low, high.T, low.T])


def swap(x):
    return pltpu.roll(x, 64, x.ndim - 1)


def lower(rows):
    return lax.broadcasted_iota(jnp.int32, (rows, 128), 1) < 64


def pack(x, keep_low):
    rows = x.shape[0] // 2
    keep = lower(rows) if keep_low else ~lower(rows)
    return jnp.where(keep, x[:rows], swap(x[rows:]))


def unpack(x):
    return jnp.concatenate([x, swap(x)], axis=0)


def merge(a, b):
    keep = lower(a.shape[0])
    return jnp.concatenate([jnp.where(keep, a, b), jnp.where(keep, swap(a), swap(b))], axis=0)


class Place:
    def __init__(self, grid):
        self.row, self.col = lax.axis_index("row"), lax.axis_index("col")
        self.odd = lax.rem(self.row, 2)
        self.near_row = self.row + 1 - 2 * self.odd
        self.far_row = self.row - 1 + 2 * self.odd
        self.grid = grid
        far = (self.far_row >= 0) & (self.far_row < grid[0])
        left, right = self.col > 0, self.col < grid[1] - 1
        self.far, self.left, self.right = far, left, right
        ends = (far & jnp.logical_not(left), far & jnp.logical_not(right))
        both = (None, far, left, right, far & left, far & right, left, right, None) + ends
        self.sends = both
        order = (NEAR, FAR, RIGHT, LEFT, FAR_RIGHT, FAR_LEFT, RIGHT_NEXT, LEFT_NEXT, RELAY, EDGE_LEFT, EDGE_RIGHT)
        self.gets = tuple(both[i] for i in order)
        self.near_border = self.pick(320, 0)
        self.far_border = self.pick(0, 320)
        self.near_halo = self.pick(448, 0)
        self.far_halo = self.pick(0, 448)

    def pick(self, even, odd):
        return pl.multiple_of(even + self.odd * (odd - even), 64)

    def target(self, which):
        row = {NEAR: self.near_row, RELAY: self.near_row, FAR: self.far_row}
        row.update({which: self.far_row for which in DIAGONAL})
        side = {LEFT: -1, FAR_LEFT: -1, LEFT_NEXT: -1, RIGHT: 1, FAR_RIGHT: 1, RIGHT_NEXT: 1}
        return {"row": row.get(which, self.row), "col": self.col + side.get(which, 0)}


def when(condition, body):
    if condition is None:
        body()
    else:
        pl.when(condition)(body)


def greet(place):
    barrier = pltpu.get_barrier_semaphore()
    for which in (NEAR, FAR, LEFT, RIGHT, FAR_LEFT, FAR_RIGHT):
        when(
            place.sends[which],
            lambda: pl.semaphore_signal(
                barrier, inc=1, device_id=place.target(which), device_id_type=MESH
            ),
        )


def greeted(place):
    far, left, right = (jnp.where(x, 1, 0) for x in (place.far, place.left, place.right))
    pl.semaphore_wait(pltpu.get_barrier_semaphore(), 1 + far + (left + right) * (1 + far))


def greet_all(place):
    barrier = pltpu.get_barrier_semaphore()
    count = 0
    for d in AROUND:
        count += jnp.where(beside(place, d), 1, 0)

        @pl.when(beside(place, d))
        def _():
            pl.semaphore_signal(
                barrier, inc=1, device_id={"row": place.row + d[0], "col": place.col + d[1]}, device_id_type=MESH
            )

    return count


def beside(place, d):
    row, col = place.row + d[0], place.col + d[1]
    return (row >= 0) & (row < place.grid[0]) & (col >= 0) & (col < place.grid[1])


def remote(place, which, src, dst, sems, p):
    return pltpu.make_async_remote_copy(
        src, dst, sems.at[0, p, which], sems.at[1, p, which], device_id=place.target(which), device_id_type=MESH
    )


def start(place, copies, *which):
    for i in which:
        when(place.sends[i], copies[i].start)


def wait_recv(place, copies, *which):
    for i in which:
        when(place.gets[i], copies[i].wait_recv)


def wait_send(place, copies, gone, *which):
    for i in which or range(len(copies)):
        if i not in gone:
            when(place.sends[i], copies[i].wait_send)
    gone.update(which or range(len(copies)))


def strips(far, far_in, side, side_in, corner, corner_in, p):
    return {
        FAR: (far.at[p], far_in.at[p]),
        FAR_LEFT: (corner.at[0, p], corner_in.at[0, p]),
        FAR_RIGHT: (corner.at[1, p], corner_in.at[1, p]),
        EDGE_LEFT: (corner.at[0, p], corner_in.at[1, p]),
        EDGE_RIGHT: (corner.at[1, p], corner_in.at[0, p]),
        LEFT: (side.at[0, p, 0:64], side_in.at[0, p, 0:64]),
        RIGHT: (side.at[1, p, 0:64], side_in.at[1, p, 0:64]),
        LEFT_NEXT: (side.at[0, p, 64:192], side_in.at[0, p, 64:192]),
        RIGHT_NEXT: (side.at[1, p, 64:192], side_in.at[1, p, 64:192]),
    }


def at_rows(first, rows):
    return pl.ds(pl.multiple_of(first, 64), rows)


class Halo:
    def __init__(self, place, ext, far, side, corner, far_in, side_in, corner_in, sems):
        self.place, self.ext, self.far, self.far_in = place, ext, far, far_in
        self.gone = (set(), set())
        self.side, self.corner, self.side_in, self.corner_in = side, corner, side_in, corner_in
        near, target = at_rows(place.near_border + 64, 64), at_rows(place.far_halo, 64)
        self.copies = []
        for p in range(2):
            ends = strips(far, far_in, side, side_in, corner, corner_in, p)
            ends[NEAR] = (ext.at[p, near, 0:384], ext.at[p, target, 0:384])
            ends[RELAY] = (ext.at[p, near, 384:512], ext.at[p, target, 384:512])
            self.copies.append([remote(place, i, *ends[i], sems, p) for i in range(11)])

    def clear(self):
        place = self.place

        @pl.when(jnp.logical_not(place.far))
        def _():
            self.far_in[...] = jnp.zeros((2, 64, 256), jnp.float32)
            self.corner_in[...] = jnp.zeros((2, 2, 64, 128), jnp.float32)

        for k, side in enumerate((place.right, place.left)):

            @pl.when(jnp.logical_not(side))
            def _():
                self.side_in[k] = jnp.zeros((2, 192, 128), jnp.float32)

    def pack(self, p):
        place, ext = self.place, self.ext
        for k, lane in enumerate((0, 256)):
            for i, first in enumerate((place.near_border, place.far_border)):
                self.side[k, p, 32 * i : 32 * i + 32] = pack(ext[p, at_rows(first + 64, 64), lane : lane + 128], k == 0)
        rows = at_rows(place.far_border + 64, 64)
        self.far[p, :, 0:128] = ext[p, rows, 128:256]
        self.far[p, :, 128:256] = jnp.where(lower(64), ext[p, rows, 256:384], ext[p, rows, 0:128])

    def pack_rest(self, p):
        for k, lane in enumerate((0, 256)):
            self.side[k, p, 64:192] = pack(self.ext[p, 128:384, lane : lane + 128], k == 0)

    def start(self, p):
        start(self.place, self.copies[p], LEFT, RIGHT, FAR)

    def start_rest(self, p):
        wait_send(self.place, self.copies[p], self.gone[p], LEFT, RIGHT)
        start(self.place, self.copies[p], LEFT_NEXT, RIGHT_NEXT, NEAR)

    def forward(self):
        place, ext, low = self.place, self.ext, lower(64)
        for p in range(2):
            wait_recv(place, self.copies[p], LEFT, RIGHT)
            for i, first in enumerate((place.near_border, place.far_border)):
                parts = [self.side_in[k, p, 32 * i : 32 * i + 32] for k in range(2)]
                ext[p, at_rows(first + 64, 64), 384:512] = merge(*parts)
            start(place, self.copies[p], RELAY)
            rows = at_rows(place.far_border + 64, 64)
            self.corner[0, p] = jnp.where(low, ext[p, rows, 0:128], ext[p, rows, 384:512])
            self.corner[1, p] = jnp.where(low, ext[p, rows, 384:512], ext[p, rows, 256:384])
            start(place, self.copies[p], *DIAGONAL)

    def finish(self):
        place, ext, low = self.place, self.ext, lower(64)
        for p in range(2):
            wait_recv(place, self.copies[p], LEFT_NEXT, RIGHT_NEXT)
            ext[p, 128:384, 384:512] = merge(self.side_in[0, p, 64:192], self.side_in[1, p, 64:192])
            wait_recv(place, self.copies[p], FAR, *DIAGONAL)
            rows = at_rows(place.far_halo, 64)
            right, left = self.corner_in[0, p], self.corner_in[1, p]
            mixed = self.far_in[p, :, 128:256]
            ext[p, rows, 0:128] = jnp.where(low, left, mixed)
            ext[p, rows, 128:256] = self.far_in[p, :, 0:128]
            ext[p, rows, 256:384] = jnp.where(low, mixed, right)
            ext[p, rows, 384:512] = jnp.where(low, right, left)
        for p in range(2):
            wait_recv(place, self.copies[p], NEAR, RELAY)
            wait_send(place, self.copies[p], self.gone[p])


class Fold:
    def __init__(self, place, update, near_in, relay_in, far, side, corner, far_in, side_in, corner_in, sems):
        self.place, self.update, self.near_in, self.relay_in = place, update, near_in, relay_in
        self.far, self.far_in = far, far_in
        self.gone = (set(), set())
        self.side, self.corner, self.side_in, self.corner_in = side, corner, side_in, corner_in
        near = at_rows(place.near_halo, 64)
        self.copies = []
        for p in range(2):
            ends = strips(far, far_in, side, side_in, corner, corner_in, p)
            ends[NEAR] = (update.at[p, near, 0:384], near_in.at[p])
            ends[RELAY] = (update.at[p, near, 384:512], relay_in.at[p])
            self.copies.append([remote(place, i, *ends[i], sems, p) for i in range(11)])

    def pack(self):
        place, update, low = self.place, self.update, lower(64)

        @pl.when(jnp.logical_not(place.far))
        def _():
            self.corner_in[...] = jnp.zeros((2, 2, 64, 128), jnp.float32)

        rows = at_rows(place.far_halo, 64)
        for p in range(2):
            tiles = [update[p, rows, 128 * t : 128 * t + 128] for t in range(4)]
            self.corner[0, p] = jnp.where(low, tiles[0], tiles[3])
            self.corner[1, p] = jnp.where(low, tiles[3], tiles[2])
            self.far[p, :, 0:128] = tiles[1]
            self.far[p, :, 128:256] = jnp.where(low, tiles[2], tiles[0])
            for k in range(2):
                self.side[k, p, 64:192] = pack(update[p, 128:384, 384:512], k == 1)

    def start(self, paced):
        place, update = self.place, self.update
        for p in range(2):
            start(place, self.copies[p], *DIAGONAL, RELAY)
        start(place, self.copies[0], FAR, LEFT_NEXT, RIGHT_NEXT)
        if not paced:
            start(place, self.copies[1], FAR)
        for p in range(2):
            wait_recv(place, self.copies[p], RELAY, *DIAGONAL)
            extra = (self.relay_in[p], jnp.where(lower(64), self.corner_in[0, p], self.corner_in[1, p]))
            for i, first in enumerate((place.near_border, place.far_border)):
                part = update[p, at_rows(first + 64, 64), 384:512] + extra[i]
                for k in range(2):
                    self.side[k, p, 32 * i : 32 * i + 32] = pack(part, k == 1)
            start(place, self.copies[p], LEFT, RIGHT)
            if p == 0 and paced:
                start(place, self.copies[0], NEAR)
                wait_send(place, self.copies[0], self.gone[0], FAR, LEFT_NEXT, RIGHT_NEXT)
                start(place, self.copies[1], FAR)
            if p == 0:
                start(place, self.copies[1], LEFT_NEXT, RIGHT_NEXT)
        if not paced:
            start(place, self.copies[0], NEAR)
        start(place, self.copies[1], NEAR)

    def finish(self, p, dest, base, inverse, between=None):
        place = self.place
        sides = ((place.right, 256, lambda x: jnp.where(lower(x.shape[0]), 0.0, x)), (place.left, 0, lambda x: jnp.where(lower(x.shape[0]), x, 0.0)))

        def add(first, lane, value):
            lanes, rows = pl.ds(lane, value.shape[1]), value.shape[0]
            dest[p, at_rows(first + base, rows), lanes] += value * inverse[at_rows(first, rows), lanes]

        wait_recv(place, self.copies[p], NEAR)
        add(place.near_border, 0, self.near_in[p])

        @pl.when(place.far)
        def _():
            self.copies[p][FAR].wait_recv()
            mixed = self.far_in[p, :, 128:256]
            add(place.far_border, 0, jnp.where(lower(64), self.corner_in[1, p], mixed))
            add(place.far_border, 128, self.far_in[p, :, 0:128])
            add(place.far_border, 256, jnp.where(lower(64), mixed, self.corner_in[0, p]))

        for k, (here, lane, keep) in enumerate(sides):

            @pl.when(here)
            def _():
                self.copies[p][LEFT_NEXT + k].wait_recv()
                add(64, lane, keep(unpack(self.side_in[k, p, 64:192])))

        if between is not None:
            between()
        for k, (here, lane, keep) in enumerate(sides):

            @pl.when(here)
            def _():
                self.copies[p][LEFT + k].wait_recv()
                add(place.near_border, lane, keep(unpack(self.side_in[k, p, 0:32])))
                add(place.far_border, lane, keep(unpack(self.side_in[k, p, 32:64])))

    def close(self):
        for p in range(2):
            wait_send(self.place, self.copies[p], self.gone[p])


def spread_kernel(grid):
    def kernel(
        field, offsets, counts, measured, tables, probe,
        ext, around, measured_here, tables_here, beams, power, update, light, places,
        mine, offsets_here, tall, far, side, corner, far_in, side_in, corner_in, sems, notes, local,
    ):
        place = Place(grid)
        peers = greet_all(place)
        pulls = [pltpu.make_async_copy(offsets, offsets_here, local.at[0])]
        pulls += [pltpu.make_async_copy(field.at[p], ext.at[p, 64:448, 0:384], local.at[1 + p]) for p in range(2)]
        later = [
            pltpu.make_async_copy(measured, measured_here, local.at[3]),
            pltpu.make_async_copy(tables, tables_here, local.at[4]),
        ]
        pulls.append(pltpu.make_async_copy(probe, tall.at[:, 8:136], local.at[5]))
        pulls.append(pltpu.make_async_copy(offsets, places, local.at[6]))
        for pull in pulls:
            pull.start()
        halo = Halo(place, ext, far, side, corner, far_in, side_in, corner_in, sems)
        halo.clear()
        for i, d in enumerate(AROUND):

            @pl.when(jnp.logical_not(beside(place, d)))
            def _():
                around[i] = jnp.zeros((8, 128), jnp.int32)

        pulls[0].wait()
        mine[0:2, 0:12] = offsets_here[0, 0]
        mine[2:3, 0:1] = jnp.full((1, 1), counts[0, 0], jnp.int32)
        letters = []
        for i, d in enumerate(AROUND):
            letter = pltpu.make_async_remote_copy(
                mine,
                around.at[AROUND.index((-d[0], -d[1]))],
                notes.at[0, i],
                notes.at[1, i],
                device_id={"row": place.row + d[0], "col": place.col + d[1]},
                device_id_type=MESH,
            )
            letters.append(letter)
        pulls[1].wait()
        halo.pack(0)
        pl.semaphore_wait(pltpu.get_barrier_semaphore(), peers)
        for i, d in enumerate(AROUND):
            pl.when(beside(place, d))(letters[i].start)
        halo.start(0)
        pulls[2].wait()
        halo.pack(1)
        halo.start(1)
        for p in range(2):
            halo.pack_rest(p)
            halo.start_rest(p)
        for pull in later:
            pull.start()
        update[...] = jnp.zeros_like(update)
        halo.forward()
        light[...] = jnp.zeros_like(light)
        pulls[3].wait()
        pulls[4].wait()
        for p in range(2):
            tall[p, 0:8] = tall[p, 128:136]
        power[...] = tall[0] * tall[0] + tall[1] * tall[1]

        def turn(slot, carry):
            live = (slot < counts[0, 0]).astype(jnp.float32)
            low_row, low_col = places[0, 0, 0, slot] & 7, places[0, 0, 1, slot] & 127
            for p in range(2):
                beams[slot, p] = pltpu.roll(tall[p, pl.ds(8 - low_row, 128), :], low_col, 1) * live
            return carry

        lax.fori_loop(0, 12, turn, 0)
        halo.finish()
        for i, d in enumerate(AROUND):
            pl.when(beside(place, d))(letters[i].wait_send)
            pl.when(beside(place, (-d[0], -d[1])))(letters[i].wait_recv)
        for pull in later:
            pull.wait()

    return kernel


def split(x):
    high = x.astype(jnp.bfloat16)
    return high, (x - high.astype(jnp.float32)).astype(jnp.bfloat16)


def dot(a, b):
    return jnp.dot(a, b, preferred_element_type=jnp.float32)


def right_mul(x, high, low):
    xh, xl = split(x)
    return dot(xh, high) + dot(xl, high) + dot(xh, low)


def left_mul(high, low, x):
    xh, xl = split(x)
    return dot(high, xh) + dot(high, xl) + dot(low, xh)


def cross(x):
    return jnp.concatenate(
        [
            jnp.concatenate([x[:128, :128], x[128:, :128]], axis=1),
            jnp.concatenate([x[:128, 128:], x[128:, 128:]], axis=1),
        ],
        axis=0,
    )


def gradient_kernel(with_light):
    def kernel(*refs):
        if with_light:
            offsets, counts, around, ext, beams, measured, tables, _, power, _, update, light, notes, arrived = refs
        else:
            offsets, counts, ext, beams, measured, tables, _, update = refs
        count = counts[0, 0]
        if with_light:
            bring = pltpu.make_async_copy(around, notes, arrived.at[0])
            bring.start()
        lane = lax.broadcasted_iota(jnp.int32, (128, 128), 1)
        sub = lax.broadcasted_iota(jnp.int32, (8, 128), 0)

        def turned(source, shift_rows, shift_lanes):
            return pltpu.roll(source[pl.ds(8 - shift_rows, 128), :], shift_lanes, 1)

        def scatter(dest, first, lanes, shift_rows, shift_lanes, value):
            head = jnp.where(sub >= shift_rows, value[:8], 0.0)
            main = jnp.concatenate([head, value[8:]], axis=0)
            tail = jnp.where(sub < shift_rows, value[:8], 0.0)
            for which, at in enumerate(lanes):
                keep = lane >= shift_lanes if which == 0 else lane < shift_lanes
                dest[pl.ds(first, 128), at] += jnp.where(keep, main, 0.0)
                dest[pl.ds(first + 128, 8), at] += jnp.where(keep[:8], tail, 0.0)

        def tiles_of(col, base, wrap):
            tile = lax.shift_right_arithmetic(col, 7) + base
            first = lax.rem(tile + wrap, wrap)
            second = lax.rem(tile + wrap + 1, wrap)
            return [pl.ds(pl.multiple_of(t * 128, 128), 128) for t in (first, second)]

        def brighten(row, col, value):
            low_row, low_col = jnp.bitwise_and(row, 7), jnp.bitwise_and(col, 127)
            first = pl.multiple_of(row - low_row + 128, 8)
            scatter(light, first, tiles_of(col, 1, 5), low_row, low_col, value)

        def gather(slot):
            row, col = offsets[0, 0, 0, slot], offsets[0, 0, 1, slot]
            low_row, low_col = jnp.bitwise_and(row, 7), jnp.bitwise_and(col, 127)
            first = pl.multiple_of(row - low_row + 64, 8)
            lanes = tiles_of(col, 0, 4)
            beam = [beams[slot, p] for p in range(2)]
            window = []
            for p in range(2):
                main = jnp.where(
                    lane >= low_col, ext[p, pl.ds(first, 128), lanes[0]], ext[p, pl.ds(first, 128), lanes[1]]
                )
                tail = jnp.where(
                    lane[:8] >= low_col,
                    ext[p, pl.ds(first + 128, 8), lanes[0]],
                    ext[p, pl.ds(first + 128, 8), lanes[1]],
                )
                window.append(jnp.concatenate([jnp.where(sub >= low_row, main[:8], tail), main[8:]], axis=0))
            real = beam[0] * window[0] - beam[1] * window[1]
            imag = beam[0] * window[1] + beam[1] * window[0]
            return jnp.concatenate([real, imag], axis=1), (slot, first, lanes, low_row, low_col, row, col)

        def put(back, at):
            slot, first, lanes, low_row, low_col, row, col = at
            beam = [beams[slot, p] for p in range(2)]
            real, imag = back[:, :128], back[:, 128:]
            scatter(update.at[0], first, lanes, low_row, low_col, beam[0] * real + beam[1] * imag)
            scatter(update.at[1], first, lanes, low_row, low_col, beam[0] * imag - beam[1] * real)
            if with_light:
                brighten(row, col, beam[0] * beam[0] + beam[1] * beam[1])

        def block(size):
            slots = list(range(size))
            pairs = [(k, k + 1) for k in range(0, size, 2)]
            got, given, raw = {}, {}, {}

            def fetch(k):
                a, b = pairs[k]
                got[k] = gather(slots[a]), gather(slots[b])
                given[k] = split(jnp.concatenate([got[k][0][0], got[k][1][0]], axis=0))

            def multiply(n, k):
                high, low = given[k]
                if n in (0, 3):
                    t, u = (tables[0], tables[1]) if n == 0 else (tables[2], tables[3])
                    raw[k] = dot(high, t) + dot(low, t) + dot(high, u)
                else:
                    t, u = (tables[2], tables[3]) if n == 1 else (tables[0], tables[1])
                    raw[k] = dot(t, high) + dot(t, low) + dot(u, high)

            def after(n, k):
                a, b = pairs[k]
                x = raw[k]
                if n == 3:
                    put(x[:128], got[k][0][1])
                    put(x[128:], got[k][1][1])
                    return
                if n == 1:
                    real, imag = x[:128], x[128:]
                    known = jnp.concatenate([measured[0, 0, slots[a]], measured[0, 0, slots[b]]], axis=1)
                    ratio = known * lax.rsqrt(real * real + imag * imag + 0.25) - 1.0
                    x = jnp.concatenate([real * ratio, imag * ratio], axis=0)
                else:
                    x = cross(x)
                given[k] = split(x)

            todo = [(n, k) for n in range(4) for k in range(len(pairs))]
            fetch(0)
            for i, (n, k) in enumerate(todo):
                multiply(n, k)
                if n == 0 and k + 1 < len(pairs):
                    fetch(k + 1)
                if i:
                    after(*todo[i - 1])
            after(*todo[-1])

        pl.when(count > 6)(lambda: block(12))
        pl.when((count > 4) & (count <= 6))(lambda: block(6))
        pl.when(count <= 4)(lambda: block(4))
        if with_light:
            bring.wait()
            for i, d in enumerate(AROUND):

                def other(slot, carry):
                    row = notes[i, 0, slot] + d[0] * 384
                    col = notes[i, 1, slot] + d[1] * 384
                    touches = (row > -128) & (row < 384) & (col > -128) & (col < 384)

                    @pl.when(touches)
                    def _():
                        low_row, low_col = jnp.bitwise_and(row, 7), jnp.bitwise_and(col, 127)
                        brighten(row, col, turned(power, low_row, low_col))

                    return carry

                lax.fori_loop(0, notes[i, 2, 0], other, 0)

    return kernel


def between_kernel(grid):
    def kernel(
        update, light, field,
        ext, cleared, inverse,
        near_in, relay_in, far, side, corner, far_in, side_in, corner_in, sems,
        halo_far, halo_side, halo_corner, halo_far_in, halo_side_in, halo_corner_in, more,
    ):
        place = Place(grid)
        greet(place)
        fold = Fold(place, update, near_in, relay_in, far, side, corner, far_in, side_in, corner_in, sems)
        halo = Halo(place, ext, halo_far, halo_side, halo_corner, halo_far_in, halo_side_in, halo_corner_in, more)
        fold.pack()
        greeted(place)
        fold.start(True)
        halo.clear()
        inverse[...] = 1.0 / (light[128:512, 128:512] + 1.0)
        for p in range(2):
            ext[p, 64:448, 0:384] = field[p, 64:448, 0:384] + update[p, 64:448, 0:384] * inverse[...]
        cleared[...] = jnp.zeros_like(cleared)
        fold.finish(0, ext, 64, inverse, lambda: halo.pack_rest(0))
        halo.pack(0)
        halo.start(0)

        def meanwhile():
            halo.start_rest(0)
            halo.pack_rest(1)

        fold.finish(1, ext, 64, inverse, meanwhile)
        halo.pack(1)
        halo.start(1)
        halo.start_rest(1)
        halo.forward()
        halo.finish()
        fold.close()

    return kernel


def last_kernel(grid):
    def kernel(update, inverse, ext, out, near_in, relay_in, far, side, corner, far_in, side_in, corner_in, sems):
        place = Place(grid)
        greet(place)
        fold = Fold(place, update, near_in, relay_in, far, side, corner, far_in, side_in, corner_in, sems)
        fold.pack()
        greeted(place)
        fold.start(False)
        for p in range(2):
            out[p] = ext[p, 64:448, 0:384] + update[p, 64:448, 0:384] * inverse[...]
        for p in range(2):
            fold.finish(p, out, 0, inverse)
        fold.close()

    return kernel


def hold(x):
    return pltpu.with_memory_space_constraint(x, pltpu.MemorySpace.HBM)


def params(collective_id=None):
    if collective_id is None:
        return pltpu.CompilerParams(vmem_limit_bytes=LIMIT)
    return pltpu.CompilerParams(collective_id=collective_id, has_side_effects=True, vmem_limit_bytes=LIMIT)


def shards(grid, tables, object_field, probe, amplitudes, offsets, counts):
    f32, i32 = jnp.float32, jnp.int32
    shape = jax.ShapeDtypeStruct
    ext_shape, light_shape = shape((2, 512, 512), f32), shape((648, 640), f32)
    offsets = jnp.swapaxes(offsets, 2, 3)
    packs = [pltpu.VMEM((2, 64, 256), f32), pltpu.VMEM((2, 2, 192, 128), f32), pltpu.VMEM((2, 2, 64, 128), f32)]
    folds = [pltpu.VMEM((2, 64, 384), f32), pltpu.VMEM((2, 64, 128), f32)] + packs + packs
    sems = pltpu.SemaphoreType.DMA((2, 2, 11))
    ext, around, measured, tables, beams, power, update, light, places = pl.pallas_call(
        spread_kernel(grid),
        name="spread",
        out_shape=(
            ext_shape,
            shape((8, 8, 128), i32),
            shape(amplitudes.shape, f32),
            shape(tables.shape, tables.dtype),
            shape((12, 2, 128, 128), f32),
            shape((136, 128), f32),
            ext_shape,
            light_shape,
            shape((1, 1, 2, 12), i32),
        ),
        in_specs=[HBM, HBM, SMEM, HBM, HBM, HBM],
        out_specs=(VMEM,) * 8 + (SMEM,),
        scratch_shapes=[pltpu.VMEM((8, 128), i32), pltpu.VMEM((1, 1, 2, 12), i32), pltpu.VMEM((2, 136, 128), f32)]
        + packs
        + packs
        + [sems, pltpu.SemaphoreType.DMA((2, 8)), pltpu.SemaphoreType.DMA((7,))],
        compiler_params=params(0),
    )(hold(object_field), hold(offsets), counts, hold(amplitudes), hold(tables), hold(probe))
    update, light = pl.pallas_call(
        gradient_kernel(True),
        name="gradient_light",
        out_shape=(ext_shape, light_shape),
        in_specs=[SMEM] * 2 + [VMEM] * 8,
        out_specs=(VMEM,) * 2,
        scratch_shapes=[pltpu.SMEM((8, 8, 128), i32), pltpu.SemaphoreType.DMA((1,))],
        input_output_aliases={7: 0, 9: 1},
        compiler_params=params(),
    )(places, counts, around, ext, beams, measured, tables, update, power, light)
    ext, cleared, inverse = pl.pallas_call(
        between_kernel(grid),
        name="between",
        out_shape=(ext_shape, ext_shape, shape((384, 384), f32)),
        in_specs=[VMEM] * 3,
        out_specs=(VMEM,) * 3,
        scratch_shapes=folds + [sems] + packs + packs + [sems],
        compiler_params=params(1),
    )(update, light, ext)
    update = pl.pallas_call(
        gradient_kernel(False),
        name="gradient",
        out_shape=ext_shape,
        in_specs=[SMEM] * 2 + [VMEM] * 5,
        out_specs=VMEM,
        input_output_aliases={6: 0},
        compiler_params=params(),
    )(places, counts, ext, beams, measured, tables, cleared)
    return pl.pallas_call(
        last_kernel(grid),
        name="last",
        out_shape=shape((2, 384, 384), f32),
        in_specs=[VMEM] * 3,
        out_specs=VMEM,
        scratch_shapes=folds + [sems],
        compiler_params=params(2),
    )(update, inverse, ext)


def solution(mesh):
    grid = (mesh.shape["row"], mesh.shape["col"])
    tables = dft_tables(128)
    placed = (
        P(None, "row", "col"),
        P(),
        P("row", "col", None, None, None),
        P("row", "col", None, None),
        P("row", "col"),
    )

    def body(*args):
        return shards(grid, jnp.asarray(tables), *args)

    return jax.shard_map(body, mesh=mesh, in_specs=placed, out_specs=P(None, "row", "col"), check_vma=False)
```

```python
import math

import jax
import jax.numpy as jnp
import numpy as np
from jax import lax
from jax.experimental import pallas as pl
from jax.experimental.pallas import tpu as pltpu
from jax.sharding import PartitionSpec as P

AROUND = ((-1, 0), (1, 0), (0, -1), (0, 1), (-1, -1), (-1, 1), (1, -1), (1, 1))
MESH = pl.DeviceIdType.MESH
VMEM = pl.BlockSpec(memory_space=pltpu.VMEM)
SMEM = pl.BlockSpec(memory_space=pltpu.SMEM)
HBM = pl.BlockSpec(memory_space=pltpu.MemorySpace.HBM)
LIMIT = 24 << 20
NEAR, FAR, LEFT, RIGHT, FAR_LEFT, FAR_RIGHT, LEFT_NEXT, RIGHT_NEXT, RELAY, EDGE_LEFT, EDGE_RIGHT = range(11)
DIAGONAL = (FAR_LEFT, FAR_RIGHT, EDGE_LEFT, EDGE_RIGHT)


def dft_tables(length):
    index = np.arange(length)
    angle = (np.outer(index, index) % length) * (2.0 * math.pi / length)
    cosine, sine = np.cos(angle) / math.sqrt(length), np.sin(angle) / math.sqrt(length)
    table = np.block([[cosine, -sine], [sine, cosine]])
    high = table.astype(jnp.bfloat16)
    low = (table - high.astype(np.float64)).astype(jnp.bfloat16)
    return np.stack([high, low, high.T, low.T])


def swap(x):
    return pltpu.roll(x, 64, x.ndim - 1)


def lower(rows):
    return lax.broadcasted_iota(jnp.int32, (rows, 128), 1) < 64


def pack(x, keep_low):
    rows = x.shape[0] // 2
    keep = lower(rows) if keep_low else ~lower(rows)
    return jnp.where(keep, x[:rows], swap(x[rows:]))


def unpack(x):
    return jnp.concatenate([x, swap(x)], axis=0)


def merge(a, b):
    keep = lower(a.shape[0])
    return jnp.concatenate([jnp.where(keep, a, b), jnp.where(keep, swap(a), swap(b))], axis=0)


class Place:
    def __init__(self, grid):
        self.row, self.col = lax.axis_index("row"), lax.axis_index("col")
        self.odd = lax.rem(self.row, 2)
        self.near_row = self.row + 1 - 2 * self.odd
        self.far_row = self.row - 1 + 2 * self.odd
        self.grid = grid
        far = (self.far_row >= 0) & (self.far_row < grid[0])
        left, right = self.col > 0, self.col < grid[1] - 1
        self.far, self.left, self.right = far, left, right
        ends = (far & jnp.logical_not(left), far & jnp.logical_not(right))
        both = (None, far, left, right, far & left, far & right, left, right, None) + ends
        self.sends = both
        order = (NEAR, FAR, RIGHT, LEFT, FAR_RIGHT, FAR_LEFT, RIGHT_NEXT, LEFT_NEXT, RELAY, EDGE_LEFT, EDGE_RIGHT)
        self.gets = tuple(both[i] for i in order)
        self.near_border = self.pick(320, 0)
        self.far_border = self.pick(0, 320)
        self.near_halo = self.pick(448, 0)
        self.far_halo = self.pick(0, 448)

    def pick(self, even, odd):
        return pl.multiple_of(even + self.odd * (odd - even), 64)

    def target(self, which):
        row = {NEAR: self.near_row, RELAY: self.near_row, FAR: self.far_row}
        row.update({which: self.far_row for which in DIAGONAL})
        side = {LEFT: -1, FAR_LEFT: -1, LEFT_NEXT: -1, RIGHT: 1, FAR_RIGHT: 1, RIGHT_NEXT: 1}
        return {"row": row.get(which, self.row), "col": self.col + side.get(which, 0)}


def when(condition, body):
    if condition is None:
        body()
    else:
        pl.when(condition)(body)


def greet(place):
    barrier = pltpu.get_barrier_semaphore()
    for which in (NEAR, FAR, LEFT, RIGHT, FAR_LEFT, FAR_RIGHT):
        when(
            place.sends[which],
            lambda: pl.semaphore_signal(
                barrier, inc=1, device_id=place.target(which), device_id_type=MESH
            ),
        )


def greeted(place):
    far, left, right = (jnp.where(x, 1, 0) for x in (place.far, place.left, place.right))
    pl.semaphore_wait(pltpu.get_barrier_semaphore(), 1 + far + (left + right) * (1 + far))


def greet_all(place):
    barrier = pltpu.get_barrier_semaphore()
    count = 0
    for d in AROUND:
        count += jnp.where(beside(place, d), 1, 0)

        @pl.when(beside(place, d))
        def _():
            pl.semaphore_signal(
                barrier, inc=1, device_id={"row": place.row + d[0], "col": place.col + d[1]}, device_id_type=MESH
            )

    return count


def beside(place, d):
    row, col = place.row + d[0], place.col + d[1]
    return (row >= 0) & (row < place.grid[0]) & (col >= 0) & (col < place.grid[1])


def remote(place, which, src, dst, sems, p):
    return pltpu.make_async_remote_copy(
        src, dst, sems.at[0, p, which], sems.at[1, p, which], device_id=place.target(which), device_id_type=MESH
    )


def start(place, copies, *which):
    for i in which:
        when(place.sends[i], copies[i].start)


def wait_recv(place, copies, *which):
    for i in which:
        when(place.gets[i], copies[i].wait_recv)


def wait_send(place, copies, gone, *which):
    for i in which or range(len(copies)):
        if i not in gone:
            when(place.sends[i], copies[i].wait_send)
    gone.update(which or range(len(copies)))


def strips(far, far_in, side, side_in, corner, corner_in, p):
    return {
        FAR: (far.at[p], far_in.at[p]),
        FAR_LEFT: (corner.at[0, p], corner_in.at[0, p]),
        FAR_RIGHT: (corner.at[1, p], corner_in.at[1, p]),
        EDGE_LEFT: (corner.at[0, p], corner_in.at[1, p]),
        EDGE_RIGHT: (corner.at[1, p], corner_in.at[0, p]),
        LEFT: (side.at[0, p, 0:64], side_in.at[0, p, 0:64]),
        RIGHT: (side.at[1, p, 0:64], side_in.at[1, p, 0:64]),
        LEFT_NEXT: (side.at[0, p, 64:192], side_in.at[0, p, 64:192]),
        RIGHT_NEXT: (side.at[1, p, 64:192], side_in.at[1, p, 64:192]),
    }


def at_rows(first, rows):
    return pl.ds(pl.multiple_of(first, 64), rows)


class Halo:
    def __init__(self, place, ext, far, side, corner, far_in, side_in, corner_in, sems):
        self.place, self.ext, self.far, self.far_in = place, ext, far, far_in
        self.gone = (set(), set())
        self.side, self.corner, self.side_in, self.corner_in = side, corner, side_in, corner_in
        near, target = at_rows(place.near_border + 64, 64), at_rows(place.far_halo, 64)
        self.copies = []
        for p in range(2):
            ends = strips(far, far_in, side, side_in, corner, corner_in, p)
            ends[NEAR] = (ext.at[p, near, 0:384], ext.at[p, target, 0:384])
            ends[RELAY] = (ext.at[p, near, 384:512], ext.at[p, target, 384:512])
            self.copies.append([remote(place, i, *ends[i], sems, p) for i in range(11)])

    def clear(self):
        place = self.place

        @pl.when(jnp.logical_not(place.far))
        def _():
            self.far_in[...] = jnp.zeros((2, 64, 256), jnp.float32)
            self.corner_in[...] = jnp.zeros((2, 2, 64, 128), jnp.float32)

        for k, side in enumerate((place.right, place.left)):

            @pl.when(jnp.logical_not(side))
            def _():
                self.side_in[k] = jnp.zeros((2, 192, 128), jnp.float32)

    def pack(self, p):
        place, ext = self.place, self.ext
        for k, lane in enumerate((0, 256)):
            for i, first in enumerate((place.near_border, place.far_border)):
                self.side[k, p, 32 * i : 32 * i + 32] = pack(ext[p, at_rows(first + 64, 64), lane : lane + 128], k == 0)
        rows = at_rows(place.far_border + 64, 64)
        self.far[p, :, 0:128] = ext[p, rows, 128:256]
        self.far[p, :, 128:256] = jnp.where(lower(64), ext[p, rows, 256:384], ext[p, rows, 0:128])

    def pack_rest(self, p):
        for k, lane in enumerate((0, 256)):
            self.side[k, p, 64:192] = pack(self.ext[p, 128:384, lane : lane + 128], k == 0)

    def start(self, p):
        start(self.place, self.copies[p], LEFT, RIGHT, FAR)

    def start_rest(self, p):
        wait_send(self.place, self.copies[p], self.gone[p], LEFT, RIGHT)
        start(self.place, self.copies[p], LEFT_NEXT, RIGHT_NEXT, NEAR)

    def forward(self):
        place, ext, low = self.place, self.ext, lower(64)
        for p in range(2):
            wait_recv(place, self.copies[p], LEFT, RIGHT)
            for i, first in enumerate((place.near_border, place.far_border)):
                parts = [self.side_in[k, p, 32 * i : 32 * i + 32] for k in range(2)]
                ext[p, at_rows(first + 64, 64), 384:512] = merge(*parts)
            start(place, self.copies[p], RELAY)
            rows = at_rows(place.far_border + 64, 64)
            self.corner[0, p] = jnp.where(low, ext[p, rows, 0:128], ext[p, rows, 384:512])
            self.corner[1, p] = jnp.where(low, ext[p, rows, 384:512], ext[p, rows, 256:384])
            start(place, self.copies[p], *DIAGONAL)

    def finish(self):
        place, ext, low = self.place, self.ext, lower(64)
        for p in range(2):
            wait_recv(place, self.copies[p], LEFT_NEXT, RIGHT_NEXT)
            ext[p, 128:384, 384:512] = merge(self.side_in[0, p, 64:192], self.side_in[1, p, 64:192])
            wait_recv(place, self.copies[p], FAR, *DIAGONAL)
            rows = at_rows(place.far_halo, 64)
            right, left = self.corner_in[0, p], self.corner_in[1, p]
            mixed = self.far_in[p, :, 128:256]
            ext[p, rows, 0:128] = jnp.where(low, left, mixed)
            ext[p, rows, 128:256] = self.far_in[p, :, 0:128]
            ext[p, rows, 256:384] = jnp.where(low, mixed, right)
            ext[p, rows, 384:512] = jnp.where(low, right, left)
        for p in range(2):
            wait_recv(place, self.copies[p], NEAR, RELAY)
            wait_send(place, self.copies[p], self.gone[p])


class Fold:
    def __init__(self, place, update, near_in, relay_in, far, side, corner, far_in, side_in, corner_in, sems):
        self.place, self.update, self.near_in, self.relay_in = place, update, near_in, relay_in
        self.far, self.far_in = far, far_in
        self.gone = (set(), set())
        self.side, self.corner, self.side_in, self.corner_in = side, corner, side_in, corner_in
        near = at_rows(place.near_halo, 64)
        self.copies = []
        for p in range(2):
            ends = strips(far, far_in, side, side_in, corner, corner_in, p)
            ends[NEAR] = (update.at[p, near, 0:384], near_in.at[p])
            ends[RELAY] = (update.at[p, near, 384:512], relay_in.at[p])
            self.copies.append([remote(place, i, *ends[i], sems, p) for i in range(11)])

    def pack(self):
        place, update, low = self.place, self.update, lower(64)

        @pl.when(jnp.logical_not(place.far))
        def _():
            self.corner_in[...] = jnp.zeros((2, 2, 64, 128), jnp.float32)

        rows = at_rows(place.far_halo, 64)
        for p in range(2):
            tiles = [update[p, rows, 128 * t : 128 * t + 128] for t in range(4)]
            self.corner[0, p] = jnp.where(low, tiles[0], tiles[3])
            self.corner[1, p] = jnp.where(low, tiles[3], tiles[2])
            self.far[p, :, 0:128] = tiles[1]
            self.far[p, :, 128:256] = jnp.where(low, tiles[2], tiles[0])
            for k in range(2):
                self.side[k, p, 64:192] = pack(update[p, 128:384, 384:512], k == 1)

    def start(self, paced):
        place, update = self.place, self.update
        for p in range(2):
            start(place, self.copies[p], *DIAGONAL, RELAY)
        start(place, self.copies[0], FAR, LEFT_NEXT, RIGHT_NEXT)
        if not paced:
            start(place, self.copies[1], FAR)
        for p in range(2):
            wait_recv(place, self.copies[p], RELAY, *DIAGONAL)
            extra = (self.relay_in[p], jnp.where(lower(64), self.corner_in[0, p], self.corner_in[1, p]))
            for i, first in enumerate((place.near_border, place.far_border)):
                part = update[p, at_rows(first + 64, 64), 384:512] + extra[i]
                for k in range(2):
                    self.side[k, p, 32 * i : 32 * i + 32] = pack(part, k == 1)
            start(place, self.copies[p], LEFT, RIGHT)
            if p == 0 and paced:
                start(place, self.copies[0], NEAR)
                wait_send(place, self.copies[0], self.gone[0], FAR, LEFT_NEXT, RIGHT_NEXT)
                start(place, self.copies[1], FAR)
            if p == 0:
                start(place, self.copies[1], LEFT_NEXT, RIGHT_NEXT)
        if not paced:
            start(place, self.copies[0], NEAR)
        start(place, self.copies[1], NEAR)

    def finish(self, p, dest, base, inverse, between=None):
        place = self.place
        sides = ((place.right, 256, lambda x: jnp.where(lower(x.shape[0]), 0.0, x)), (place.left, 0, lambda x: jnp.where(lower(x.shape[0]), x, 0.0)))

        def add(first, lane, value):
            lanes, rows = pl.ds(lane, value.shape[1]), value.shape[0]
            dest[p, at_rows(first + base, rows), lanes] += value * inverse[at_rows(first, rows), lanes]

        wait_recv(place, self.copies[p], NEAR)
        add(place.near_border, 0, self.near_in[p])

        @pl.when(place.far)
        def _():
            self.copies[p][FAR].wait_recv()
            mixed = self.far_in[p, :, 128:256]
            add(place.far_border, 0, jnp.where(lower(64), self.corner_in[1, p], mixed))
            add(place.far_border, 128, self.far_in[p, :, 0:128])
            add(place.far_border, 256, jnp.where(lower(64), mixed, self.corner_in[0, p]))

        for k, (here, lane, keep) in enumerate(sides):

            @pl.when(here)
            def _():
                self.copies[p][LEFT_NEXT + k].wait_recv()
                add(64, lane, keep(unpack(self.side_in[k, p, 64:192])))

        if between is not None:
            between()
        for k, (here, lane, keep) in enumerate(sides):

            @pl.when(here)
            def _():
                self.copies[p][LEFT + k].wait_recv()
                add(place.near_border, lane, keep(unpack(self.side_in[k, p, 0:32])))
                add(place.far_border, lane, keep(unpack(self.side_in[k, p, 32:64])))

    def close(self):
        for p in range(2):
            wait_send(self.place, self.copies[p], self.gone[p])


def spread_kernel(grid):
    def kernel(
        field, offsets, counts, measured, tables, probe,
        ext, around, measured_here, tables_here, beams, power, update, light, places,
        mine, offsets_here, tall, far, side, corner, far_in, side_in, corner_in, sems, notes, local,
    ):
        place = Place(grid)
        peers = greet_all(place)
        pulls = [pltpu.make_async_copy(offsets, offsets_here, local.at[0])]
        pulls += [pltpu.make_async_copy(field.at[p], ext.at[p, 64:448, 0:384], local.at[1 + p]) for p in range(2)]
        later = [
            pltpu.make_async_copy(measured, measured_here, local.at[3]),
            pltpu.make_async_copy(tables, tables_here, local.at[4]),
        ]
        pulls.append(pltpu.make_async_copy(probe, tall.at[:, 8:136], local.at[5]))
        pulls.append(pltpu.make_async_copy(offsets, places, local.at[6]))
        for pull in pulls:
            pull.start()
        halo = Halo(place, ext, far, side, corner, far_in, side_in, corner_in, sems)
        halo.clear()
        for i, d in enumerate(AROUND):

            @pl.when(jnp.logical_not(beside(place, d)))
            def _():
                around[i] = jnp.zeros((8, 128), jnp.int32)

        pulls[0].wait()
        mine[0:2, 0:12] = offsets_here[0, 0]
        mine[2:3, 0:1] = jnp.full((1, 1), counts[0, 0], jnp.int32)
        letters = []
        for i, d in enumerate(AROUND):
            letter = pltpu.make_async_remote_copy(
                mine,
                around.at[AROUND.index((-d[0], -d[1]))],
                notes.at[0, i],
                notes.at[1, i],
                device_id={"row": place.row + d[0], "col": place.col + d[1]},
                device_id_type=MESH,
            )
            letters.append(letter)
        pulls[1].wait()
        halo.pack(0)
        pl.semaphore_wait(pltpu.get_barrier_semaphore(), peers)
        for i, d in enumerate(AROUND):
            pl.when(beside(place, d))(letters[i].start)
        halo.start(0)
        pulls[2].wait()
        halo.pack(1)
        halo.start(1)
        for p in range(2):
            halo.pack_rest(p)
            halo.start_rest(p)
        for pull in later:
            pull.start()
        update[...] = jnp.zeros_like(update)
        halo.forward()
        light[...] = jnp.zeros_like(light)
        pulls[3].wait()
        pulls[4].wait()
        for p in range(2):
            tall[p, 0:8] = tall[p, 128:136]
        power[...] = tall[0] * tall[0] + tall[1] * tall[1]

        def turn(slot, carry):
            live = (slot < counts[0, 0]).astype(jnp.float32)
            low_row, low_col = places[0, 0, 0, slot] & 7, places[0, 0, 1, slot] & 127
            for p in range(2):
                beams[slot, p] = pltpu.roll(tall[p, pl.ds(8 - low_row, 128), :], low_col, 1) * live
            return carry

        lax.fori_loop(0, 12, turn, 0)
        halo.finish()
        for i, d in enumerate(AROUND):
            pl.when(beside(place, d))(letters[i].wait_send)
            pl.when(beside(place, (-d[0], -d[1])))(letters[i].wait_recv)
        for pull in later:
            pull.wait()

    return kernel


def split(x):
    high = x.astype(jnp.bfloat16)
    return high, (x - high.astype(jnp.float32)).astype(jnp.bfloat16)


def dot(a, b):
    return jnp.dot(a, b, preferred_element_type=jnp.float32)


def right_mul(x, high, low):
    xh, xl = split(x)
    return dot(xh, high) + dot(xl, high) + dot(xh, low)


def left_mul(high, low, x):
    xh, xl = split(x)
    return dot(high, xh) + dot(high, xl) + dot(low, xh)


def cross(x):
    return jnp.concatenate(
        [
            jnp.concatenate([x[:128, :128], x[128:, :128]], axis=1),
            jnp.concatenate([x[:128, 128:], x[128:, 128:]], axis=1),
        ],
        axis=0,
    )


def gradient_kernel(with_light):
    def kernel(*refs):
        if with_light:
            offsets, counts, around, ext, beams, measured, tables, _, power, _, update, light, notes, arrived = refs
        else:
            offsets, counts, ext, beams, measured, tables, _, update = refs
        count = counts[0, 0]
        if with_light:
            bring = pltpu.make_async_copy(around, notes, arrived.at[0])
            bring.start()
        lane = lax.broadcasted_iota(jnp.int32, (128, 128), 1)
        sub = lax.broadcasted_iota(jnp.int32, (8, 128), 0)

        def turned(source, shift_rows, shift_lanes):
            return pltpu.roll(source[pl.ds(8 - shift_rows, 128), :], shift_lanes, 1)

        def scatter(dest, first, lanes, shift_rows, shift_lanes, value):
            head = jnp.where(sub >= shift_rows, value[:8], 0.0)
            main = jnp.concatenate([head, value[8:]], axis=0)
            tail = jnp.where(sub < shift_rows, value[:8], 0.0)
            for which, at in enumerate(lanes):
                keep = lane >= shift_lanes if which == 0 else lane < shift_lanes
                dest[pl.ds(first, 128), at] += jnp.where(keep, main, 0.0)
                dest[pl.ds(first + 128, 8), at] += jnp.where(keep[:8], tail, 0.0)

        def tiles_of(col, base, wrap):
            tile = lax.shift_right_arithmetic(col, 7) + base
            first = lax.rem(tile + wrap, wrap)
            second = lax.rem(tile + wrap + 1, wrap)
            return [pl.ds(pl.multiple_of(t * 128, 128), 128) for t in (first, second)]

        def brighten(row, col, value):
            low_row, low_col = jnp.bitwise_and(row, 7), jnp.bitwise_and(col, 127)
            first = pl.multiple_of(row - low_row + 128, 8)
            scatter(light, first, tiles_of(col, 1, 5), low_row, low_col, value)

        def gather(slot):
            row, col = offsets[0, 0, 0, slot], offsets[0, 0, 1, slot]
            low_row, low_col = jnp.bitwise_and(row, 7), jnp.bitwise_and(col, 127)
            first = pl.multiple_of(row - low_row + 64, 8)
            lanes = tiles_of(col, 0, 4)
            beam = [beams[slot, p] for p in range(2)]
            window = []
            for p in range(2):
                main = jnp.where(
                    lane >= low_col, ext[p, pl.ds(first, 128), lanes[0]], ext[p, pl.ds(first, 128), lanes[1]]
                )
                tail = jnp.where(
                    lane[:8] >= low_col,
                    ext[p, pl.ds(first + 128, 8), lanes[0]],
                    ext[p, pl.ds(first + 128, 8), lanes[1]],
                )
                window.append(jnp.concatenate([jnp.where(sub >= low_row, main[:8], tail), main[8:]], axis=0))
            real = beam[0] * window[0] - beam[1] * window[1]
            imag = beam[0] * window[1] + beam[1] * window[0]
            return jnp.concatenate([real, imag], axis=1), (slot, first, lanes, low_row, low_col, row, col)

        def put(back, at):
            slot, first, lanes, low_row, low_col, row, col = at
            beam = [beams[slot, p] for p in range(2)]
            real, imag = back[:, :128], back[:, 128:]
            scatter(update.at[0], first, lanes, low_row, low_col, beam[0] * real + beam[1] * imag)
            scatter(update.at[1], first, lanes, low_row, low_col, beam[0] * imag - beam[1] * real)
            if with_light:
                brighten(row, col, beam[0] * beam[0] + beam[1] * beam[1])

        def block(size):
            slots = list(range(size))
            pairs = [(k, k + 1) for k in range(0, size, 2)]
            got, given, raw = {}, {}, {}

            def fetch(k):
                a, b = pairs[k]
                got[k] = gather(slots[a]), gather(slots[b])
                given[k] = split(jnp.concatenate([got[k][0][0], got[k][1][0]], axis=0))

            def multiply(n, k):
                high, low = given[k]
                if n in (0, 3):
                    t, u = (tables[0], tables[1]) if n == 0 else (tables[2], tables[3])
                    raw[k] = dot(high, t) + dot(low, t) + dot(high, u)
                else:
                    t, u = (tables[2], tables[3]) if n == 1 else (tables[0], tables[1])
                    raw[k] = dot(t, high) + dot(t, low) + dot(u, high)

            def after(n, k):
                a, b = pairs[k]
                x = raw[k]
                if n == 3:
                    put(x[:128], got[k][0][1])
                    put(x[128:], got[k][1][1])
                    return
                if n == 1:
                    real, imag = x[:128], x[128:]
                    known = jnp.concatenate([measured[0, 0, slots[a]], measured[0, 0, slots[b]]], axis=1)
                    ratio = known * lax.rsqrt(real * real + imag * imag + 0.25) - 1.0
                    x = jnp.concatenate([real * ratio, imag * ratio], axis=0)
                else:
                    x = cross(x)
                given[k] = split(x)

            todo = [(n, k) for n in range(4) for k in range(len(pairs))]
            fetch(0)
            for i, (n, k) in enumerate(todo):
                multiply(n, k)
                if n == 0 and k + 1 < len(pairs):
                    fetch(k + 1)
                if i:
                    after(*todo[i - 1])
            after(*todo[-1])

        pl.when(count > 6)(lambda: block(12))
        pl.when(count <= 6)(lambda: block(6))
        if with_light:
            bring.wait()
            for i, d in enumerate(AROUND):

                def other(slot, carry):
                    row = notes[i, 0, slot] + d[0] * 384
                    col = notes[i, 1, slot] + d[1] * 384
                    touches = (row > -128) & (row < 384) & (col > -128) & (col < 384)

                    @pl.when(touches)
                    def _():
                        low_row, low_col = jnp.bitwise_and(row, 7), jnp.bitwise_and(col, 127)
                        brighten(row, col, turned(power, low_row, low_col))

                    return carry

                lax.fori_loop(0, notes[i, 2, 0], other, 0)

    return kernel


def between_kernel(grid):
    def kernel(
        update, light, field,
        ext, cleared, inverse,
        near_in, relay_in, far, side, corner, far_in, side_in, corner_in, sems,
        halo_far, halo_side, halo_corner, halo_far_in, halo_side_in, halo_corner_in, more,
    ):
        place = Place(grid)
        greet(place)
        fold = Fold(place, update, near_in, relay_in, far, side, corner, far_in, side_in, corner_in, sems)
        halo = Halo(place, ext, halo_far, halo_side, halo_corner, halo_far_in, halo_side_in, halo_corner_in, more)
        fold.pack()
        greeted(place)
        fold.start(False)
        halo.clear()
        inverse[...] = 1.0 / (light[128:512, 128:512] + 1.0)
        for p in range(2):
            ext[p, 64:448, 0:384] = field[p, 64:448, 0:384] + update[p, 64:448, 0:384] * inverse[...]
        cleared[...] = jnp.zeros_like(cleared)
        fold.finish(0, ext, 64, inverse, lambda: halo.pack_rest(0))
        halo.pack(0)
        halo.start(0)

        def meanwhile():
            halo.start_rest(0)
            halo.pack_rest(1)

        fold.finish(1, ext, 64, inverse, meanwhile)
        halo.pack(1)
        halo.start(1)
        halo.start_rest(1)
        halo.forward()
        halo.finish()
        fold.close()

    return kernel


def last_kernel(grid):
    def kernel(update, inverse, ext, out, near_in, relay_in, far, side, corner, far_in, side_in, corner_in, sems):
        place = Place(grid)
        greet(place)
        fold = Fold(place, update, near_in, relay_in, far, side, corner, far_in, side_in, corner_in, sems)
        fold.pack()
        greeted(place)
        fold.start(False)
        for p in range(2):
            out[p] = ext[p, 64:448, 0:384] + update[p, 64:448, 0:384] * inverse[...]
        for p in range(2):
            fold.finish(p, out, 0, inverse)
        fold.close()

    return kernel


def hold(x):
    return pltpu.with_memory_space_constraint(x, pltpu.MemorySpace.HBM)


def params(collective_id=None):
    if collective_id is None:
        return pltpu.CompilerParams(vmem_limit_bytes=LIMIT)
    return pltpu.CompilerParams(collective_id=collective_id, has_side_effects=True, vmem_limit_bytes=LIMIT)


def shards(grid, tables, object_field, probe, amplitudes, offsets, counts):
    f32, i32 = jnp.float32, jnp.int32
    shape = jax.ShapeDtypeStruct
    ext_shape, light_shape = shape((2, 512, 512), f32), shape((648, 640), f32)
    offsets = jnp.swapaxes(offsets, 2, 3)
    packs = [pltpu.VMEM((2, 64, 256), f32), pltpu.VMEM((2, 2, 192, 128), f32), pltpu.VMEM((2, 2, 64, 128), f32)]
    folds = [pltpu.VMEM((2, 64, 384), f32), pltpu.VMEM((2, 64, 128), f32)] + packs + packs
    sems = pltpu.SemaphoreType.DMA((2, 2, 11))
    ext, around, measured, tables, beams, power, update, light, places = pl.pallas_call(
        spread_kernel(grid),
        name="spread",
        out_shape=(
            ext_shape,
            shape((8, 8, 128), i32),
            shape(amplitudes.shape, f32),
            shape(tables.shape, tables.dtype),
            shape((12, 2, 128, 128), f32),
            shape((136, 128), f32),
            ext_shape,
            light_shape,
            shape((1, 1, 2, 12), i32),
        ),
        in_specs=[HBM, HBM, SMEM, HBM, HBM, HBM],
        out_specs=(VMEM,) * 8 + (SMEM,),
        scratch_shapes=[pltpu.VMEM((8, 128), i32), pltpu.VMEM((1, 1, 2, 12), i32), pltpu.VMEM((2, 136, 128), f32)]
        + packs
        + packs
        + [sems, pltpu.SemaphoreType.DMA((2, 8)), pltpu.SemaphoreType.DMA((7,))],
        compiler_params=params(0),
    )(hold(object_field), hold(offsets), counts, hold(amplitudes), hold(tables), hold(probe))
    update, light = pl.pallas_call(
        gradient_kernel(True),
        name="gradient_light",
        out_shape=(ext_shape, light_shape),
        in_specs=[SMEM] * 2 + [VMEM] * 8,
        out_specs=(VMEM,) * 2,
        scratch_shapes=[pltpu.SMEM((8, 8, 128), i32), pltpu.SemaphoreType.DMA((1,))],
        input_output_aliases={7: 0, 9: 1},
        compiler_params=params(),
    )(places, counts, around, ext, beams, measured, tables, update, power, light)
    ext, cleared, inverse = pl.pallas_call(
        between_kernel(grid),
        name="between",
        out_shape=(ext_shape, ext_shape, shape((384, 384), f32)),
        in_specs=[VMEM] * 3,
        out_specs=(VMEM,) * 3,
        scratch_shapes=folds + [sems] + packs + packs + [sems],
        compiler_params=params(1),
    )(update, light, ext)
    update = pl.pallas_call(
        gradient_kernel(False),
        name="gradient",
        out_shape=ext_shape,
        in_specs=[SMEM] * 2 + [VMEM] * 5,
        out_specs=VMEM,
        input_output_aliases={6: 0},
        compiler_params=params(),
    )(places, counts, ext, beams, measured, tables, cleared)
    return pl.pallas_call(
        last_kernel(grid),
        name="last",
        out_shape=shape((2, 384, 384), f32),
        in_specs=[VMEM] * 3,
        out_specs=VMEM,
        scratch_shapes=folds + [sems],
        compiler_params=params(2),
    )(update, inverse, ext)


def solution(mesh):
    grid = (mesh.shape["row"], mesh.shape["col"])
    tables = dft_tables(128)
    placed = (
        P(None, "row", "col"),
        P(),
        P("row", "col", None, None, None),
        P("row", "col", None, None),
        P("row", "col"),
    )

    def body(*args):
        return shards(grid, jnp.asarray(tables), *args)

    return jax.shard_map(body, mesh=mesh, in_specs=placed, out_specs=P(None, "row", "col"), check_vma=False)
```
